128 devices in a mesh: leaf: 2 (over core), front: 64 (over z, y, x).
Axes of the slice: x: 4, y: 4, z: 4, core: 2. Of those that a mesh axis runs over, the one named last changes fastest.
Arguments:
- front_block: float32 [8192, 8192], P('leaf', 'front'), as said below
- child_update: float32 [2, 6144, 8192], P('leaf', None, 'front'), as said below
- child_map: int32 [2, 48], P('leaf'), may hold values from 0 to 63, as said below
Outputs:
- factored: float32 [8192, 8192], P('leaf', 'front')
The draws below stay inside these ranges and needn't reach their ends.
Inputs may be any that keep to these rules, and one draw needn't show every extreme that they name: `child_map`: each row is strictly increasing, holds 48 distinct blocks, and always names block 0 and block 63. `front_block`: Symmetric; the assembled front is positive definite. `child_update`: each child's update is symmetric and positive semidefinite in the child's order; columns of parent blocks that the child's map does not name are zero.
All inputs are finite; a program needn't handle non-finite values.
Results may differ from the reference program's by a relative error of at most 0.000088.
Values sent between devices are 32-bit elements; how exact they have to be, the bound alone decides.
A program may use at most 128 MiB of HBM per device.

```python
import jax
import jax.numpy as jnp
from jax import lax

BLK = 128
PB = 64
CB = 48
P_SIZE = 8192
C = 6144
S = 512
NCH = 2


kernel_reach = 0.25


front_gain = 2.0


log_two = 0.6931471805599453


def distance_kernel(points):
    distance = jnp.abs(points[:, None, 0] - points[None, :, 0])
    distance = distance + jnp.abs(points[:, None, 1] - points[None, :, 1])
    distance = distance + jnp.abs(points[:, None, 2] - points[None, :, 2])
    return jnp.exp(-distance / kernel_reach)


def child_blocks(key):
    child_keys = jax.random.split(jax.random.fold_in(key, 7), NCH)

    def one_child(child_key):
        chosen = jax.random.permutation(child_key, PB - 2)[:CB - 2] + 1
        ends = jnp.array([0, PB - 1], dtype=jnp.int32)
        return jnp.sort(jnp.concatenate([ends, chosen.astype(jnp.int32)]))
    return jax.vmap(one_child)(child_keys)


def draw_child_map(key, part):
    return child_blocks(key).astype(jnp.int32)


def draw_child_update(key, part):
    blocks = child_blocks(key)
    offsets = jnp.arange(BLK, dtype=jnp.int32)

    def one_child(inputs):
        child, child_blocks_row = inputs
        child_key = jax.random.fold_in(jax.random.fold_in(key, 11), child)
        point_key = jax.random.fold_in(child_key, 0)
        points = jax.random.uniform(point_key, (C, 3), jnp.float32)
        symmetric = distance_kernel(points)
        col_index = (child_blocks_row[:, None] * BLK + offsets[None, :]).reshape(-1)
        return jnp.zeros((C, P_SIZE), jnp.float32).at[:, col_index].set(symmetric)
    return lax.map(one_child, (jnp.arange(NCH, dtype=jnp.int32), blocks))


def draw_front_block(key, part):
    point_key, diag_key = jax.random.split(jax.random.fold_in(key, 3), 2)
    points = jax.random.uniform(point_key, (P_SIZE, 3), jnp.float32)
    extra = jnp.exp(jax.random.uniform(diag_key, (P_SIZE,), jnp.float32, -log_two, log_two))
    return front_gain * distance_kernel(points) + jnp.diag(extra)


def setup_inputs(seed: int = 0) -> dict:
    splits = jax.random.split(jax.random.key(seed), 4)
    return {
        "front_block": draw_front_block(jax.random.fold_in(splits[3], 71), 0),
        "child_update": draw_child_update(jax.random.fold_in(splits[3], 71), 0),
        "child_map": draw_child_map(jax.random.fold_in(splits[3], 71), 0),
    }


def solve_right(factor, rows):
    return lax.linalg.triangular_solve(factor, rows, left_side=False, lower=True, transpose_a=True)

def reference(front_block, child_update, child_map):
    assembled = front_block
    offsets = jnp.arange(BLK, dtype=jnp.int32)
    for child in range(NCH):
        row_index = (child_map[child][:, None] * BLK + offsets[None, :]).reshape(-1).astype(jnp.int32)
        assembled = assembled.at[row_index].add(child_update[child])
    factor = jnp.linalg.cholesky(assembled[:S, :S])
    solved = solve_right(factor, assembled[:, :S])
    lower_rows = solved[S:]
    schur_part = assembled[S:, S:] - jnp.dot(lower_rows, lower_rows.T, precision=lax.Precision.HIGHEST)
    top_part = jnp.concatenate([factor, lower_rows.T], axis=1)
    bottom_part = jnp.concatenate([lower_rows, schur_part], axis=1)
    return jnp.concatenate([top_part, bottom_part], axis=0)
```

```python
import jax
import jax.numpy as jnp
from jax import lax
from jax.sharding import PartitionSpec as P

BLK = 128
S = 512
HIGHEST = lax.Precision.HIGHEST


def gather_half(blocks, child_map, half, half_blocks):
    parent = half * half_blocks + jnp.arange(half_blocks, dtype=jnp.int32)
    hit = child_map[None, :] == parent[:, None]
    found = jnp.any(hit, axis=1)
    index = jnp.argmax(hit, axis=1)
    picked = jnp.take(blocks, index, axis=0)
    picked = jnp.where(found[:, None, None], picked, jnp.zeros_like(picked))
    return picked.reshape(half_blocks * BLK, blocks.shape[2])


def per_device(front_block, child_update, child_map):
    rows, cols = front_block.shape
    n_leaf = lax.axis_size("leaf")
    n_front = lax.axis_size("front")
    leaf = lax.axis_index("leaf")
    front = lax.axis_index("front")
    half_blocks = rows // BLK

    blocks = child_update[0].reshape(-1, BLK, cols)
    cmap = child_map[0]
    own = gather_half(blocks, cmap, leaf, half_blocks)
    send = gather_half(blocks, cmap, 1 - leaf, half_blocks)
    recv = lax.ppermute(send, "leaf", [(0, 1), (1, 0)])
    first = jnp.where(leaf == 0, own, recv)
    second = jnp.where(leaf == 0, recv, own)
    assembled = front_block + first + second

    top = assembled[:S]
    piv_cols = S // cols
    is_piv = front < piv_cols
    col_at = jnp.minimum(front, piv_cols - 1) * cols
    panel = lax.dynamic_update_slice_in_dim(
        jnp.zeros((S, S), jnp.float32), jnp.where(is_piv, top, jnp.zeros_like(top)), col_at, 1
    )
    pivot = lax.psum(panel, "front")
    factor = jnp.linalg.cholesky(pivot)

    own_solved = lax.linalg.triangular_solve(factor, top, left_side=True, lower=True).T
    from_leaf0 = lax.ppermute(own_solved, "leaf", [(0, 1)])
    col_solved = jnp.where(leaf == 0, own_solved, from_leaf0)

    piece = rows // n_front
    per_block = BLK // piece
    pieces = []
    for part in range(per_block):
        pairs = []
        for lf in range(n_leaf):
            for k in range(n_front // per_block):
                src = lf * n_front + lf * half_blocks + k
                dst = lf * n_front + per_block * k + part
                pairs.append((src, dst))
        pieces.append(lax.ppermute(col_solved[part * piece:(part + 1) * piece], ("leaf", "front"), pairs))
    my_piece = pieces[0]
    for part in range(1, per_block):
        my_piece = jnp.where(front % per_block == part, pieces[part], my_piece)
    row_solved = lax.all_gather(my_piece, "front", tiled=True)

    schur = assembled - jnp.dot(row_solved, col_solved.T, precision=HIGHEST)

    row_global = leaf * rows + jnp.arange(rows, dtype=jnp.int32)
    col_global = front * cols + jnp.arange(cols, dtype=jnp.int32)
    col_start = jnp.minimum(front * cols, S - cols)
    left_rows = lax.dynamic_slice_in_dim(row_solved, col_start, cols, 1)
    left_top = jnp.pad(lax.dynamic_slice_in_dim(factor, col_start, cols, 1), ((0, rows - S), (0, 0)))
    left_part = jnp.where(row_global[:, None] < S, left_top, left_rows)
    right_top = jnp.pad(col_solved.T, ((0, rows - S), (0, 0)))
    right_part = jnp.where(row_global[:, None] < S, right_top, schur)
    return jnp.where(col_global[None, :] < S, left_part, right_part)


def solution(mesh):
    return jax.shard_map(
        per_device,
        mesh=mesh,
        in_specs=(P("leaf", "front"), P("leaf", None, "front"), P("leaf", None)),
        out_specs=P("leaf", "front"),
        check_vma=False,
    )
```

```python
import functools

import jax
import jax.numpy as jnp
from jax import lax
from jax.experimental import pallas as pl
from jax.experimental.pallas import tpu as pltpu
from jax.sharding import PartitionSpec as P

BLK = 128
S = 512
HIGHEST = lax.Precision.HIGHEST
MESH = pl.DeviceIdType.MESH


def gather_half(blocks, child_map, half, half_blocks):
    parent = half * half_blocks + jnp.arange(half_blocks, dtype=jnp.int32)
    hit = child_map[None, :] == parent[:, None]
    found = jnp.any(hit, axis=1)
    index = jnp.argmax(hit, axis=1)
    picked = jnp.take(blocks, index, axis=0)
    picked = jnp.where(found[:, None, None], picked, jnp.zeros_like(picked))
    return picked.reshape(half_blocks * BLK, blocks.shape[2])


def pivot_kernel(n_front, n_src, top_ref, out_ref, chunk, sem_a, sem_b, send_a, send_b, recv_g, send_g):
    leaf = lax.axis_index("leaf")
    me = lax.axis_index("front")
    per_src = n_front // n_src
    rows = chunk.shape[0]

    @pl.when((leaf == 0) & (me < n_src))
    def _():
        for k in range(per_src):
            src = top_ref.at[pl.ds(k * rows, rows)]
            dst = me * per_src + k
            if k == 0:
                @pl.when(me == 0)
                def _():
                    pltpu.make_async_copy(src, chunk, sem_a).start()

                @pl.when(me != 0)
                def _():
                    pltpu.make_async_remote_copy(
                        src, chunk, send_a.at[k], sem_a, device_id=(0, dst), device_id_type=MESH
                    ).start()
            else:
                pltpu.make_async_remote_copy(
                    src, chunk, send_a.at[k], sem_a, device_id=(0, dst), device_id_type=MESH
                ).start()

    @pl.when((leaf == 0) & (me == 0))
    def _():
        pltpu.make_async_copy(top_ref.at[pl.ds(0, rows)], chunk, sem_a).wait()

    @pl.when((leaf == 0) & (me != 0))
    def _():
        pltpu.make_async_remote_copy(
            top_ref.at[pl.ds(0, rows)], chunk, send_a.at[0], sem_a, device_id=(0, me), device_id_type=MESH
        ).wait_recv()

    @pl.when(leaf == 0)
    def _():
        pltpu.make_async_remote_copy(
            chunk, chunk, send_b, sem_b, device_id=(1, me), device_id_type=MESH
        ).start()

    @pl.when(leaf == 1)
    def _():
        pltpu.make_async_remote_copy(
            chunk, chunk, send_b, sem_b, device_id=(0, me), device_id_type=MESH
        ).wait_recv()

    pltpu.make_async_copy(chunk, out_ref.at[me], recv_g.at[me]).start()

    def send(j, carry):
        dst = lax.rem(me + j, n_front)
        pltpu.make_async_remote_copy(
            chunk, out_ref.at[me], send_g.at[j], recv_g.at[me], device_id=(leaf, dst), device_id_type=MESH
        ).start()
        return carry

    lax.fori_loop(1, n_front, send, 0)

    pltpu.make_async_copy(chunk, out_ref.at[me], recv_g.at[me]).wait()

    def receive(j, carry):
        src = lax.rem(me + j, n_front)
        pltpu.make_async_remote_copy(
            chunk, out_ref.at[src], send_g.at[j], recv_g.at[src], device_id=(leaf, src), device_id_type=MESH
        ).wait_recv()
        return carry

    lax.fori_loop(1, n_front, receive, 0)

    def sent(j, carry):
        dst = lax.rem(me + j, n_front)
        pltpu.make_async_remote_copy(
            chunk, out_ref.at[me], send_g.at[j], recv_g.at[me], device_id=(leaf, dst), device_id_type=MESH
        ).wait_send()
        return carry

    lax.fori_loop(1, n_front, sent, 0)

    @pl.when(leaf == 0)
    def _():
        pltpu.make_async_remote_copy(
            chunk, chunk, send_b, sem_b, device_id=(1, me), device_id_type=MESH
        ).wait_send()

    @pl.when((leaf == 0) & (me < n_src))
    def _():
        for k in range(per_src):
            src = top_ref.at[pl.ds(k * rows, rows)]
            dst = me * per_src + k
            if k == 0:
                @pl.when(me != 0)
                def _():
                    pltpu.make_async_remote_copy(
                        src, chunk, send_a.at[k], sem_a, device_id=(0, dst), device_id_type=MESH
                    ).wait_send()
            else:
                pltpu.make_async_remote_copy(
                    src, chunk, send_a.at[k], sem_a, device_id=(0, dst), device_id_type=MESH
                ).wait_send()


def broadcast_pivot(top, n_front):
    cols = top.shape[1]
    n_src = S // cols
    per_src = n_front // n_src
    rows = S // per_src
    gathered = pl.pallas_call(
        functools.partial(pivot_kernel, n_front, n_src),
        out_shape=jax.ShapeDtypeStruct((n_front, rows, cols), jnp.float32),
        in_specs=[pl.BlockSpec(memory_space=pltpu.VMEM)],
        out_specs=pl.BlockSpec(memory_space=pltpu.VMEM),
        scratch_shapes=[
            pltpu.VMEM((rows, cols), jnp.float32),
            pltpu.SemaphoreType.DMA,
            pltpu.SemaphoreType.DMA,
            pltpu.SemaphoreType.DMA((per_src,)),
            pltpu.SemaphoreType.DMA,
            pltpu.SemaphoreType.DMA((n_front,)),
            pltpu.SemaphoreType.DMA((n_front,)),
        ],
        compiler_params=pltpu.CompilerParams(has_side_effects=True),
    )(top)
    return gathered.reshape(n_src, per_src, rows, cols).transpose(1, 2, 0, 3).reshape(S, S)


def per_device(front_block, child_update, child_map):
    rows, cols = front_block.shape
    n_leaf = lax.axis_size("leaf")
    n_front = lax.axis_size("front")
    leaf = lax.axis_index("leaf")
    front = lax.axis_index("front")
    half_blocks = rows // BLK

    blocks = child_update[0].reshape(-1, BLK, cols)
    cmap = child_map[0]
    own = gather_half(blocks, cmap, leaf, half_blocks)
    send = gather_half(blocks, cmap, 1 - leaf, half_blocks)
    recv = lax.ppermute(send, "leaf", [(0, 1), (1, 0)])
    first = jnp.where(leaf == 0, own, recv)
    second = jnp.where(leaf == 0, recv, own)
    assembled = front_block + first + second

    top = assembled[:S]
    panel_rows = top.T

    piece = rows // n_front
    per_block = BLK // piece
    pieces = []
    for part in range(per_block):
        pairs = []
        for lf in range(n_leaf):
            for k in range(n_front // per_block):
                src = lf * half_blocks + k
                dst = lf * n_front + per_block * k + part
                pairs.append((src, dst))
        pieces.append(lax.ppermute(panel_rows[part * piece:(part + 1) * piece], ("leaf", "front"), pairs))
    my_piece = pieces[0]
    for part in range(1, per_block):
        my_piece = jnp.where(front % per_block == part, pieces[part], my_piece)
    panel = lax.all_gather(my_piece, "front", tiled=True)

    pivot = broadcast_pivot(top, n_front)
    factor = jnp.linalg.cholesky(pivot)
    inverse = lax.linalg.triangular_solve(
        factor, jnp.eye(S, dtype=jnp.float32), left_side=True, lower=True
    )

    own_solved = jnp.dot(panel_rows, inverse.T, precision=HIGHEST)
    from_leaf0 = lax.ppermute(own_solved, "leaf", [(0, 1)])
    col_solved = jnp.where(leaf == 0, own_solved, from_leaf0)

    row_solved = jnp.dot(panel, inverse.T, precision=HIGHEST)
    schur = assembled - jnp.dot(row_solved, col_solved.T, precision=HIGHEST)

    row_global = leaf * rows + jnp.arange(rows, dtype=jnp.int32)
    col_global = front * cols + jnp.arange(cols, dtype=jnp.int32)
    col_start = jnp.minimum(front * cols, S - cols)
    left_rows = lax.dynamic_slice_in_dim(row_solved, col_start, cols, 1)
    left_top = jnp.pad(lax.dynamic_slice_in_dim(factor, col_start, cols, 1), ((0, rows - S), (0, 0)))
    left_part = jnp.where(row_global[:, None] < S, left_top, left_rows)
    right_top = jnp.pad(col_solved.T, ((0, rows - S), (0, 0)))
    right_part = jnp.where(row_global[:, None] < S, right_top, schur)
    return jnp.where(col_global[None, :] < S, left_part, right_part)


def solution(mesh):
    return jax.shard_map(
        per_device,
        mesh=mesh,
        in_specs=(P("leaf", "front"), P("leaf", None, "front"), P("leaf", None)),
        out_specs=P("leaf", "front"),
        check_vma=False,
    )
```

```python
import functools

import jax
import jax.numpy as jnp
from jax import lax
from jax.experimental import pallas as pl
from jax.experimental.pallas import tpu as pltpu
from jax.sharding import PartitionSpec as P

BLK = 128
S = 512
HIGHEST = lax.Precision.HIGHEST
MESH = pl.DeviceIdType.MESH


def gather_half(blocks, child_map, half, half_blocks):
    parent = half * half_blocks + jnp.arange(half_blocks, dtype=jnp.int32)
    hit = child_map[None, :] == parent[:, None]
    found = jnp.any(hit, axis=1)
    index = jnp.argmax(hit, axis=1)
    picked = jnp.take(blocks, index, axis=0)
    picked = jnp.where(found[:, None, None], picked, jnp.zeros_like(picked))
    return picked.reshape(half_blocks * BLK, blocks.shape[2])


def pivot_kernel(n_front, n_src, top_ref, out_ref, chunk, sem_a, sem_b, send_a, send_b, recv_g, send_g):
    leaf = lax.axis_index("leaf")
    me = lax.axis_index("front")
    per_src = n_front // n_src
    rows = chunk.shape[0]

    @pl.when((leaf == 0) & (me < n_src))
    def _():
        for k in range(per_src):
            src = top_ref.at[pl.ds(k * rows, rows)]
            dst = me * per_src + k
            if k == 0:
                @pl.when(me == 0)
                def _():
                    pltpu.make_async_copy(src, chunk, sem_a).start()

                @pl.when(me != 0)
                def _():
                    pltpu.make_async_remote_copy(
                        src, chunk, send_a.at[k], sem_a, device_id=(0, dst), device_id_type=MESH
                    ).start()
            else:
                pltpu.make_async_remote_copy(
                    src, chunk, send_a.at[k], sem_a, device_id=(0, dst), device_id_type=MESH
                ).start()

    @pl.when((leaf == 0) & (me == 0))
    def _():
        pltpu.make_async_copy(top_ref.at[pl.ds(0, rows)], chunk, sem_a).wait()

    @pl.when((leaf == 0) & (me != 0))
    def _():
        pltpu.make_async_remote_copy(
            top_ref.at[pl.ds(0, rows)], chunk, send_a.at[0], sem_a, device_id=(0, me), device_id_type=MESH
        ).wait_recv()

    @pl.when(leaf == 0)
    def _():
        pltpu.make_async_remote_copy(
            chunk, chunk, send_b, sem_b, device_id=(1, me), device_id_type=MESH
        ).start()

    @pl.when(leaf == 1)
    def _():
        pltpu.make_async_remote_copy(
            chunk, chunk, send_b, sem_b, device_id=(0, me), device_id_type=MESH
        ).wait_recv()

    pltpu.make_async_copy(chunk, out_ref.at[me], recv_g.at[me]).start()

    def send(j, carry):
        dst = lax.rem(me + j, n_front)
        pltpu.make_async_remote_copy(
            chunk, out_ref.at[me], send_g.at[j], recv_g.at[me], device_id=(leaf, dst), device_id_type=MESH
        ).start()
        return carry

    lax.fori_loop(1, n_front, send, 0)

    pltpu.make_async_copy(chunk, out_ref.at[me], recv_g.at[me]).wait()

    def receive(j, carry):
        src = lax.rem(me + j, n_front)
        pltpu.make_async_remote_copy(
            chunk, out_ref.at[src], send_g.at[j], recv_g.at[src], device_id=(leaf, src), device_id_type=MESH
        ).wait_recv()
        return carry

    lax.fori_loop(1, n_front, receive, 0)

    def sent(j, carry):
        dst = lax.rem(me + j, n_front)
        pltpu.make_async_remote_copy(
            chunk, out_ref.at[me], send_g.at[j], recv_g.at[me], device_id=(leaf, dst), device_id_type=MESH
        ).wait_send()
        return carry

    lax.fori_loop(1, n_front, sent, 0)

    @pl.when(leaf == 0)
    def _():
        pltpu.make_async_remote_copy(
            chunk, chunk, send_b, sem_b, device_id=(1, me), device_id_type=MESH
        ).wait_send()

    @pl.when((leaf == 0) & (me < n_src))
    def _():
        for k in range(per_src):
            src = top_ref.at[pl.ds(k * rows, rows)]
            dst = me * per_src + k
            if k == 0:
                @pl.when(me != 0)
                def _():
                    pltpu.make_async_remote_copy(
                        src, chunk, send_a.at[k], sem_a, device_id=(0, dst), device_id_type=MESH
                    ).wait_send()
            else:
                pltpu.make_async_remote_copy(
                    src, chunk, send_a.at[k], sem_a, device_id=(0, dst), device_id_type=MESH
                ).wait_send()


def broadcast_pivot(top, n_front):
    cols = top.shape[1]
    n_src = S // cols
    per_src = n_front // n_src
    rows = S // per_src
    gathered = pl.pallas_call(
        functools.partial(pivot_kernel, n_front, n_src),
        out_shape=jax.ShapeDtypeStruct((n_front, rows, cols), jnp.float32),
        in_specs=[pl.BlockSpec(memory_space=pltpu.VMEM)],
        out_specs=pl.BlockSpec(memory_space=pltpu.VMEM),
        scratch_shapes=[
            pltpu.VMEM((rows, cols), jnp.float32),
            pltpu.SemaphoreType.DMA,
            pltpu.SemaphoreType.DMA,
            pltpu.SemaphoreType.DMA((per_src,)),
            pltpu.SemaphoreType.DMA,
            pltpu.SemaphoreType.DMA((n_front,)),
            pltpu.SemaphoreType.DMA((n_front,)),
        ],
        compiler_params=pltpu.CompilerParams(has_side_effects=True),
    )(top)
    return gathered.reshape(n_src, per_src, rows, cols).transpose(1, 2, 0, 3).reshape(S, S)


def per_device(front_block, child_update, child_map):
    rows, cols = front_block.shape
    n_leaf = lax.axis_size("leaf")
    n_front = lax.axis_size("front")
    leaf = lax.axis_index("leaf")
    front = lax.axis_index("front")
    half_blocks = rows // BLK

    blocks = child_update[0].reshape(-1, BLK, cols)
    cmap = child_map[0]
    own = gather_half(blocks, cmap, leaf, half_blocks)
    send = gather_half(blocks, cmap, 1 - leaf, half_blocks)
    recv = lax.ppermute(send, "leaf", [(0, 1), (1, 0)])
    first = jnp.where(leaf == 0, own, recv)
    second = jnp.where(leaf == 0, recv, own)
    assembled = front_block + first + second

    top = assembled[:S]
    panel_rows = top.T

    piece = rows // n_front
    per_block = BLK // piece
    pieces = []
    for part in range(per_block):
        pairs = []
        for lf in range(n_leaf):
            for k in range(n_front // per_block):
                src = lf * half_blocks + k
                dst = lf * n_front + per_block * k + part
                pairs.append((src, dst))
        pieces.append(lax.ppermute(panel_rows[part * piece:(part + 1) * piece], ("leaf", "front"), pairs))
    my_piece = pieces[0]
    for part in range(1, per_block):
        my_piece = jnp.where(front % per_block == part, pieces[part], my_piece)
    pivot = broadcast_pivot(top, n_front)
    my_piece, pivot = lax.optimization_barrier((my_piece, pivot))
    panel = lax.all_gather(my_piece, "front", tiled=True)
    factor = jnp.linalg.cholesky(pivot)
    row_solved = lax.linalg.triangular_solve(factor, panel, left_side=False, lower=True, transpose_a=True)

    in_half = front // half_blocks == leaf
    candidate = lax.dynamic_slice_in_dim(row_solved, (front % half_blocks) * BLK, BLK, 0)
    other = lax.ppermute(candidate, "leaf", [(0, 1), (1, 0)])
    col_solved = jnp.where(in_half, candidate, other)

    schur = assembled - jnp.dot(row_solved, col_solved.T, precision=HIGHEST)

    row_global = leaf * rows + jnp.arange(rows, dtype=jnp.int32)
    col_global = front * cols + jnp.arange(cols, dtype=jnp.int32)
    col_start = jnp.minimum(front * cols, S - cols)
    left_rows = lax.dynamic_slice_in_dim(row_solved, col_start, cols, 1)
    left_top = jnp.pad(lax.dynamic_slice_in_dim(factor, col_start, cols, 1), ((0, rows - S), (0, 0)))
    left_part = jnp.where(row_global[:, None] < S, left_top, left_rows)
    right_top = jnp.pad(col_solved.T, ((0, rows - S), (0, 0)))
    right_part = jnp.where(row_global[:, None] < S, right_top, schur)
    return jnp.where(col_global[None, :] < S, left_part, right_part)


def solution(mesh):
    return jax.shard_map(
        per_device,
        mesh=mesh,
        in_specs=(P("leaf", "front"), P("leaf", None, "front"), P("leaf", None)),
        out_specs=P("leaf", "front"),
        check_vma=False,
    )
```

```python
import functools

import jax
import jax.numpy as jnp
from jax import lax
from jax.experimental import pallas as pl
from jax.experimental.pallas import tpu as pltpu
from jax.sharding import PartitionSpec as P

BLK = 128
S = 512
HIGHEST = lax.Precision.HIGHEST
MESH = pl.DeviceIdType.MESH


def gather_half(blocks, child_map, half, half_blocks):
    parent = half * half_blocks + jnp.arange(half_blocks, dtype=jnp.int32)
    hit = child_map[None, :] == parent[:, None]
    found = jnp.any(hit, axis=1)
    index = jnp.argmax(hit, axis=1)
    picked = jnp.take(blocks, index, axis=0)
    picked = jnp.where(found[:, None, None], picked, jnp.zeros_like(picked))
    return picked.reshape(half_blocks * BLK, blocks.shape[2])


def pivot_kernel(n_front, n_src, top_ref, out_ref, chunk, sem_a, sem_b, send_a, send_b, recv_g, send_g):
    leaf = lax.axis_index("leaf")
    me = lax.axis_index("front")
    per_src = n_front // n_src
    rows = chunk.shape[0]

    @pl.when((leaf == 0) & (me < n_src))
    def _():
        for k in range(per_src):
            src = top_ref.at[pl.ds(k * rows, rows)]
            dst = me * per_src + k
            if k == 0:
                @pl.when(me == 0)
                def _():
                    pltpu.make_async_copy(src, chunk, sem_a).start()

                @pl.when(me != 0)
                def _():
                    pltpu.make_async_remote_copy(
                        src, chunk, send_a.at[k], sem_a, device_id=(0, dst), device_id_type=MESH
                    ).start()
            else:
                pltpu.make_async_remote_copy(
                    src, chunk, send_a.at[k], sem_a, device_id=(0, dst), device_id_type=MESH
                ).start()

    @pl.when((leaf == 0) & (me == 0))
    def _():
        pltpu.make_async_copy(top_ref.at[pl.ds(0, rows)], chunk, sem_a).wait()

    @pl.when((leaf == 0) & (me != 0))
    def _():
        pltpu.make_async_remote_copy(
            top_ref.at[pl.ds(0, rows)], chunk, send_a.at[0], sem_a, device_id=(0, me), device_id_type=MESH
        ).wait_recv()

    @pl.when(leaf == 0)
    def _():
        pltpu.make_async_remote_copy(
            chunk, chunk, send_b, sem_b, device_id=(1, me), device_id_type=MESH
        ).start()

    @pl.when(leaf == 1)
    def _():
        pltpu.make_async_remote_copy(
            chunk, chunk, send_b, sem_b, device_id=(0, me), device_id_type=MESH
        ).wait_recv()

    pltpu.make_async_copy(chunk, out_ref.at[me], recv_g.at[me]).start()

    def send(j, carry):
        dst = lax.rem(me + j, n_front)
        pltpu.make_async_remote_copy(
            chunk, out_ref.at[me], send_g.at[j], recv_g.at[me], device_id=(leaf, dst), device_id_type=MESH
        ).start()
        return carry

    lax.fori_loop(1, n_front, send, 0)

    pltpu.make_async_copy(chunk, out_ref.at[me], recv_g.at[me]).wait()

    def receive(j, carry):
        src = lax.rem(me + j, n_front)
        pltpu.make_async_remote_copy(
            chunk, out_ref.at[src], send_g.at[j], recv_g.at[src], device_id=(leaf, src), device_id_type=MESH
        ).wait_recv()
        return carry

    lax.fori_loop(1, n_front, receive, 0)

    def sent(j, carry):
        dst = lax.rem(me + j, n_front)
        pltpu.make_async_remote_copy(
            chunk, out_ref.at[me], send_g.at[j], recv_g.at[me], device_id=(leaf, dst), device_id_type=MESH
        ).wait_send()
        return carry

    lax.fori_loop(1, n_front, sent, 0)

    @pl.when(leaf == 0)
    def _():
        pltpu.make_async_remote_copy(
            chunk, chunk, send_b, sem_b, device_id=(1, me), device_id_type=MESH
        ).wait_send()

    @pl.when((leaf == 0) & (me < n_src))
    def _():
        for k in range(per_src):
            src = top_ref.at[pl.ds(k * rows, rows)]
            dst = me * per_src + k
            if k == 0:
                @pl.when(me != 0)
                def _():
                    pltpu.make_async_remote_copy(
                        src, chunk, send_a.at[k], sem_a, device_id=(0, dst), device_id_type=MESH
                    ).wait_send()
            else:
                pltpu.make_async_remote_copy(
                    src, chunk, send_a.at[k], sem_a, device_id=(0, dst), device_id_type=MESH
                ).wait_send()


def broadcast_pivot(top, n_front):
    cols = top.shape[1]
    n_src = S // cols
    per_src = n_front // n_src
    rows = S // per_src
    gathered = pl.pallas_call(
        functools.partial(pivot_kernel, n_front, n_src),
        out_shape=jax.ShapeDtypeStruct((n_front, rows, cols), jnp.float32),
        in_specs=[pl.BlockSpec(memory_space=pltpu.VMEM)],
        out_specs=pl.BlockSpec(memory_space=pltpu.VMEM),
        scratch_shapes=[
            pltpu.VMEM((rows, cols), jnp.float32),
            pltpu.SemaphoreType.DMA,
            pltpu.SemaphoreType.DMA,
            pltpu.SemaphoreType.DMA((per_src,)),
            pltpu.SemaphoreType.DMA,
            pltpu.SemaphoreType.DMA((n_front,)),
            pltpu.SemaphoreType.DMA((n_front,)),
        ],
        compiler_params=pltpu.CompilerParams(has_side_effects=True),
    )(top)
    return gathered.reshape(n_src, per_src, rows, cols).transpose(1, 2, 0, 3).reshape(S, S)


def _mm(a, b):
    return jnp.dot(a, b, precision=HIGHEST, preferred_element_type=jnp.float32)


def _mm_t(a, b):
    return lax.dot_general(a, b, (((1,), (1,)), ((), ())), precision=HIGHEST,
                           preferred_element_type=jnp.float32)


def chol_inv_kernel(a_ref, l_ref, linv_ref, w_ref, d_ref, lt_ref, x_ref):
    n = a_ref.shape[0]
    b = d_ref.shape[0]
    nb = n // b
    lane = lax.broadcasted_iota(jnp.int32, (1, b), 1)
    sub = lax.broadcasted_iota(jnp.int32, (b, 1), 0)
    eye = (lax.broadcasted_iota(jnp.int32, (b, b), 0) == lax.broadcasted_iota(jnp.int32, (b, b), 1)).astype(jnp.float32)
    w_ref[...] = a_ref[...]
    l_ref[...] = jnp.zeros_like(l_ref)
    linv_ref[...] = jnp.zeros_like(linv_ref)

    def step(k, carry):
        row = d_ref[pl.ds(k, 1), :]
        piv = jnp.sum(jnp.where(lane == k, row, 0.0), axis=1, keepdims=True)
        root = jnp.sqrt(piv)
        col = jnp.where(lane >= k, row / root, 0.0)
        lt_ref[pl.ds(k, 1), :] = col
        col_t = jnp.transpose(jnp.broadcast_to(col, (8, b)))[:, 0:1]
        d_ref[...] = d_ref[...] - col_t * col
        xk = x_ref[pl.ds(k, 1), :] / root
        x_ref[pl.ds(k, 1), :] = xk
        below = jnp.where(sub > k, col_t, 0.0)
        x_ref[...] = x_ref[...] - below * xk
        return carry

    for j in range(nb):
        jb = j * b
        d_ref[...] = w_ref[jb:jb + b, jb:jb + b]
        x_ref[...] = eye
        lax.fori_loop(0, b, step, 0)
        l_ref[jb:jb + b, jb:jb + b] = jnp.transpose(lt_ref[...])
        linv_ref[jb:jb + b, jb:jb + b] = x_ref[...]
        if j < nb - 1:
            lp = _mm_t(w_ref[jb + b:, jb:jb + b], x_ref[...])
            l_ref[jb + b:, jb:jb + b] = lp
            w_ref[jb + b:, jb + b:] = w_ref[jb + b:, jb + b:] - _mm_t(lp, lp)
    for j in range(nb):
        for i in range(j + 1, nb):
            acc = jnp.zeros((b, b), jnp.float32)
            for k in range(j, i):
                acc = acc + _mm(l_ref[i * b:(i + 1) * b, k * b:(k + 1) * b], linv_ref[k * b:(k + 1) * b, j * b:(j + 1) * b])
            linv_ref[i * b:(i + 1) * b, j * b:(j + 1) * b] = -_mm(linv_ref[i * b:(i + 1) * b, i * b:(i + 1) * b], acc)


def chol_inv(a, b=128):
    n = a.shape[0]
    return pl.pallas_call(
        chol_inv_kernel,
        out_shape=(jax.ShapeDtypeStruct((n, n), jnp.float32), jax.ShapeDtypeStruct((n, n), jnp.float32)),
        in_specs=[pl.BlockSpec(memory_space=pltpu.VMEM)],
        out_specs=(pl.BlockSpec(memory_space=pltpu.VMEM), pl.BlockSpec(memory_space=pltpu.VMEM)),
        scratch_shapes=[
            pltpu.VMEM((n, n), jnp.float32),
            pltpu.VMEM((b, b), jnp.float32),
            pltpu.VMEM((b, b), jnp.float32),
            pltpu.VMEM((b, b), jnp.float32),
        ],
    )(a)


def per_device(front_block, child_update, child_map):
    rows, cols = front_block.shape
    n_leaf = lax.axis_size("leaf")
    n_front = lax.axis_size("front")
    leaf = lax.axis_index("leaf")
    front = lax.axis_index("front")
    half_blocks = rows // BLK

    blocks = child_update[0].reshape(-1, BLK, cols)
    cmap = child_map[0]
    own = gather_half(blocks, cmap, leaf, half_blocks)
    send = gather_half(blocks, cmap, 1 - leaf, half_blocks)
    recv = lax.ppermute(send, "leaf", [(0, 1), (1, 0)])
    first = jnp.where(leaf == 0, own, recv)
    second = jnp.where(leaf == 0, recv, own)
    assembled = front_block + first + second

    top = assembled[:S]
    panel_rows = top.T

    piece = rows // n_front
    per_block = BLK // piece
    pieces = []
    for part in range(per_block):
        pairs = []
        for lf in range(n_leaf):
            for k in range(n_front // per_block):
                src = lf * half_blocks + k
                dst = lf * n_front + per_block * k + part
                pairs.append((src, dst))
        pieces.append(lax.ppermute(panel_rows[part * piece:(part + 1) * piece], ("leaf", "front"), pairs))
    my_piece = pieces[0]
    for part in range(1, per_block):
        my_piece = jnp.where(front % per_block == part, pieces[part], my_piece)
    pivot = broadcast_pivot(top, n_front)
    my_piece, pivot = lax.optimization_barrier((my_piece, pivot))
    panel = lax.all_gather(my_piece, "front", tiled=True)
    factor, inverse = chol_inv(pivot)
    row_solved = lax.dot_general(panel, inverse, (((1,), (1,)), ((), ())), precision=HIGHEST)

    in_half = front // half_blocks == leaf
    candidate = lax.dynamic_slice_in_dim(row_solved, (front % half_blocks) * BLK, BLK, 0)
    other = lax.ppermute(candidate, "leaf", [(0, 1), (1, 0)])
    col_solved = jnp.where(in_half, candidate, other)

    schur = assembled - jnp.dot(row_solved, col_solved.T, precision=HIGHEST)

    row_global = leaf * rows + jnp.arange(rows, dtype=jnp.int32)
    col_global = front * cols + jnp.arange(cols, dtype=jnp.int32)
    col_start = jnp.minimum(front * cols, S - cols)
    left_rows = lax.dynamic_slice_in_dim(row_solved, col_start, cols, 1)
    left_top = jnp.pad(lax.dynamic_slice_in_dim(factor, col_start, cols, 1), ((0, rows - S), (0, 0)))
    left_part = jnp.where(row_global[:, None] < S, left_top, left_rows)
    right_top = jnp.pad(col_solved.T, ((0, rows - S), (0, 0)))
    right_part = jnp.where(row_global[:, None] < S, right_top, schur)
    return jnp.where(col_global[None, :] < S, left_part, right_part)


def solution(mesh):
    return jax.shard_map(
        per_device,
        mesh=mesh,
        in_specs=(P("leaf", "front"), P("leaf", None, "front"), P("leaf", None)),
        out_specs=P("leaf", "front"),
        check_vma=False,
    )
```

```python
import functools

import jax
import jax.numpy as jnp
from jax import lax
from jax.experimental import pallas as pl
from jax.experimental.pallas import tpu as pltpu
from jax.sharding import PartitionSpec as P

BLK = 128
S = 512
HIGHEST = lax.Precision.HIGHEST
MESH = pl.DeviceIdType.MESH


def gather_half(blocks, child_map, half, half_blocks):
    parent = half * half_blocks + jnp.arange(half_blocks, dtype=jnp.int32)
    hit = child_map[None, :] == parent[:, None]
    found = jnp.any(hit, axis=1)
    index = jnp.argmax(hit, axis=1)
    picked = jnp.take(blocks, index, axis=0)
    picked = jnp.where(found[:, None, None], picked, jnp.zeros_like(picked))
    return picked.reshape(half_blocks * BLK, blocks.shape[2])


def pivot_kernel(n_front, n_src, top_ref, out_ref, chunk, sem_a, sem_b, send_a, send_b, recv_g, send_g):
    leaf = lax.axis_index("leaf")
    me = lax.axis_index("front")
    per_src = n_front // n_src
    rows = chunk.shape[0]

    @pl.when((leaf == 0) & (me < n_src))
    def _():
        for k in range(per_src):
            src = top_ref.at[pl.ds(k * rows, rows)]
            dst = me * per_src + k
            if k == 0:
                @pl.when(me == 0)
                def _():
                    pltpu.make_async_copy(src, chunk, sem_a).start()

                @pl.when(me != 0)
                def _():
                    pltpu.make_async_remote_copy(
                        src, chunk, send_a.at[k], sem_a, device_id=(0, dst), device_id_type=MESH
                    ).start()
            else:
                pltpu.make_async_remote_copy(
                    src, chunk, send_a.at[k], sem_a, device_id=(0, dst), device_id_type=MESH
                ).start()

    @pl.when((leaf == 0) & (me == 0))
    def _():
        pltpu.make_async_copy(top_ref.at[pl.ds(0, rows)], chunk, sem_a).wait()

    @pl.when((leaf == 0) & (me != 0))
    def _():
        pltpu.make_async_remote_copy(
            top_ref.at[pl.ds(0, rows)], chunk, send_a.at[0], sem_a, device_id=(0, me), device_id_type=MESH
        ).wait_recv()

    @pl.when(leaf == 0)
    def _():
        pltpu.make_async_remote_copy(
            chunk, chunk, send_b, sem_b, device_id=(1, me), device_id_type=MESH
        ).start()

    @pl.when(leaf == 1)
    def _():
        pltpu.make_async_remote_copy(
            chunk, chunk, send_b, sem_b, device_id=(0, me), device_id_type=MESH
        ).wait_recv()

    pltpu.make_async_copy(chunk, out_ref.at[me], recv_g.at[me]).start()

    def send(j, carry):
        dst = lax.rem(me + j, n_front)
        pltpu.make_async_remote_copy(
            chunk, out_ref.at[me], send_g.at[j], recv_g.at[me], device_id=(leaf, dst), device_id_type=MESH
        ).start()
        return carry

    lax.fori_loop(1, n_front, send, 0)

    pltpu.make_async_copy(chunk, out_ref.at[me], recv_g.at[me]).wait()

    def receive(j, carry):
        src = lax.rem(me + j, n_front)
        pltpu.make_async_remote_copy(
            chunk, out_ref.at[src], send_g.at[j], recv_g.at[src], device_id=(leaf, src), device_id_type=MESH
        ).wait_recv()
        return carry

    lax.fori_loop(1, n_front, receive, 0)

    def sent(j, carry):
        dst = lax.rem(me + j, n_front)
        pltpu.make_async_remote_copy(
            chunk, out_ref.at[me], send_g.at[j], recv_g.at[me], device_id=(leaf, dst), device_id_type=MESH
        ).wait_send()
        return carry

    lax.fori_loop(1, n_front, sent, 0)

    @pl.when(leaf == 0)
    def _():
        pltpu.make_async_remote_copy(
            chunk, chunk, send_b, sem_b, device_id=(1, me), device_id_type=MESH
        ).wait_send()

    @pl.when((leaf == 0) & (me < n_src))
    def _():
        for k in range(per_src):
            src = top_ref.at[pl.ds(k * rows, rows)]
            dst = me * per_src + k
            if k == 0:
                @pl.when(me != 0)
                def _():
                    pltpu.make_async_remote_copy(
                        src, chunk, send_a.at[k], sem_a, device_id=(0, dst), device_id_type=MESH
                    ).wait_send()
            else:
                pltpu.make_async_remote_copy(
                    src, chunk, send_a.at[k], sem_a, device_id=(0, dst), device_id_type=MESH
                ).wait_send()


def broadcast_pivot(top, n_front):
    cols = top.shape[1]
    n_src = S // cols
    per_src = n_front // n_src
    rows = S // per_src
    gathered = pl.pallas_call(
        functools.partial(pivot_kernel, n_front, n_src),
        out_shape=jax.ShapeDtypeStruct((n_front, rows, cols), jnp.float32),
        in_specs=[pl.BlockSpec(memory_space=pltpu.VMEM)],
        out_specs=pl.BlockSpec(memory_space=pltpu.VMEM),
        scratch_shapes=[
            pltpu.VMEM((rows, cols), jnp.float32),
            pltpu.SemaphoreType.DMA,
            pltpu.SemaphoreType.DMA,
            pltpu.SemaphoreType.DMA((per_src,)),
            pltpu.SemaphoreType.DMA,
            pltpu.SemaphoreType.DMA((n_front,)),
            pltpu.SemaphoreType.DMA((n_front,)),
        ],
        compiler_params=pltpu.CompilerParams(has_side_effects=True),
    )(top)
    return gathered.reshape(n_src, per_src, rows, cols).transpose(1, 2, 0, 3).reshape(S, S)


PANEL = 8


def _mm(a, b):
    return jnp.dot(a, b, precision=HIGHEST, preferred_element_type=jnp.float32)


def _mm_t(a, b):
    return lax.dot_general(a, b, (((1,), (1,)), ((), ())), precision=HIGHEST,
                           preferred_element_type=jnp.float32)


def _mm_tn(a, b):
    return lax.dot_general(a, b, (((0,), (0,)), ((), ())), precision=HIGHEST,
                           preferred_element_type=jnp.float32)


def chol_inv_kernel(a_ref, l_ref, linv_ref, w_ref, d_ref, ut_ref, lo_ref, x_ref):
    n = a_ref.shape[0]
    b = d_ref.shape[0]
    nb = n // b
    lane = lax.broadcasted_iota(jnp.int32, (PANEL, b), 1)
    sub = lax.broadcasted_iota(jnp.int32, (PANEL, 1), 0)
    w_ref[...] = a_ref[...]
    l_ref[...] = jnp.zeros_like(l_ref)
    linv_ref[...] = jnp.zeros_like(linv_ref)

    def factor_panel(p, carry):
        k = pl.multiple_of(p * PANEL, PANEL)
        r = d_ref[pl.ds(k, PANEL), :]
        for t in range(PANEL):
            c = k + t
            colv = jnp.sum(jnp.where(lane == c, r, 0.0), axis=1, keepdims=True)
            piv = jnp.sum(jnp.where(sub == t, colv, 0.0), axis=0, keepdims=True)
            root = jnp.sqrt(piv)
            urow = jnp.where(lane[t:t + 1] >= c, r[t:t + 1] / root, 0.0)
            f = jnp.where(sub > t, colv / root, 0.0)
            r = jnp.where(sub == t, urow, r - f * urow)
        ut_ref[pl.ds(k, PANEL), :] = r
        d_ref[...] = d_ref[...] - _mm_tn(r, r)
        return carry

    def invert_panel(p, carry):
        k = pl.multiple_of(p * PANEL, PANEL)
        lrows = lo_ref[pl.ds(k, PANEL), :]
        e = (lane == sub + k).astype(jnp.float32) - _mm(lrows, x_ref[...])
        for t in range(PANEL):
            c = k + t
            colv = jnp.sum(jnp.where(lane == c, lrows, 0.0), axis=1, keepdims=True)
            diag = jnp.sum(jnp.where(sub == t, colv, 0.0), axis=0, keepdims=True)
            xrow = e[t:t + 1] / diag
            f = jnp.where(sub > t, colv, 0.0)
            e = jnp.where(sub == t, xrow, e - f * xrow)
        x_ref[pl.ds(k, PANEL), :] = e
        return carry

    for j in range(nb):
        jb = j * b
        d_ref[...] = w_ref[jb:jb + b, jb:jb + b]
        ut_ref[...] = jnp.zeros_like(ut_ref)
        x_ref[...] = jnp.zeros_like(x_ref)
        lax.fori_loop(0, b // PANEL, factor_panel, 0)
        lo_ref[...] = jnp.transpose(ut_ref[...])
        lax.fori_loop(0, b // PANEL, invert_panel, 0)
        l_ref[jb:jb + b, jb:jb + b] = lo_ref[...]
        linv_ref[jb:jb + b, jb:jb + b] = x_ref[...]
        if j < nb - 1:
            lp = _mm_t(w_ref[jb + b:, jb:jb + b], x_ref[...])
            l_ref[jb + b:, jb:jb + b] = lp
            w_ref[jb + b:, jb + b:] = w_ref[jb + b:, jb + b:] - _mm_t(lp, lp)
    for j in range(nb):
        for i in range(j + 1, nb):
            acc = jnp.zeros((b, b), jnp.float32)
            for k in range(j, i):
                acc = acc + _mm(l_ref[i * b:(i + 1) * b, k * b:(k + 1) * b], linv_ref[k * b:(k + 1) * b, j * b:(j + 1) * b])
            linv_ref[i * b:(i + 1) * b, j * b:(j + 1) * b] = -_mm(linv_ref[i * b:(i + 1) * b, i * b:(i + 1) * b], acc)


def chol_inv(a, b=128):
    n = a.shape[0]
    return pl.pallas_call(
        chol_inv_kernel,
        out_shape=(jax.ShapeDtypeStruct((n, n), jnp.float32), jax.ShapeDtypeStruct((n, n), jnp.float32)),
        in_specs=[pl.BlockSpec(memory_space=pltpu.VMEM)],
        out_specs=(pl.BlockSpec(memory_space=pltpu.VMEM), pl.BlockSpec(memory_space=pltpu.VMEM)),
        scratch_shapes=[
            pltpu.VMEM((n, n), jnp.float32),
            pltpu.VMEM((b, b), jnp.float32),
            pltpu.VMEM((b, b), jnp.float32),
            pltpu.VMEM((b, b), jnp.float32),
            pltpu.VMEM((b, b), jnp.float32),
        ],
    )(a)


def per_device(front_block, child_update, child_map):
    rows, cols = front_block.shape
    n_leaf = lax.axis_size("leaf")
    n_front = lax.axis_size("front")
    leaf = lax.axis_index("leaf")
    front = lax.axis_index("front")
    half_blocks = rows // BLK

    blocks = child_update[0].reshape(-1, BLK, cols)
    cmap = child_map[0]
    own = gather_half(blocks, cmap, leaf, half_blocks)
    send = gather_half(blocks, cmap, 1 - leaf, half_blocks)
    recv = lax.ppermute(send, "leaf", [(0, 1), (1, 0)])
    first = jnp.where(leaf == 0, own, recv)
    second = jnp.where(leaf == 0, recv, own)
    assembled = front_block + first + second

    top = assembled[:S]
    panel_rows = top.T

    piece = rows // n_front
    per_block = BLK // piece
    pieces = []
    for part in range(per_block):
        pairs = []
        for lf in range(n_leaf):
            for k in range(n_front // per_block):
                src = lf * half_blocks + k
                dst = lf * n_front + per_block * k + part
                pairs.append((src, dst))
        pieces.append(lax.ppermute(panel_rows[part * piece:(part + 1) * piece], ("leaf", "front"), pairs))
    my_piece = pieces[0]
    for part in range(1, per_block):
        my_piece = jnp.where(front % per_block == part, pieces[part], my_piece)
    pivot = broadcast_pivot(top, n_front)
    my_piece, pivot = lax.optimization_barrier((my_piece, pivot))
    panel = lax.all_gather(my_piece, "front", tiled=True)
    factor, inverse = chol_inv(pivot)
    row_solved = lax.dot_general(panel, inverse, (((1,), (1,)), ((), ())), precision=HIGHEST)

    in_half = front // half_blocks == leaf
    candidate = lax.dynamic_slice_in_dim(row_solved, (front % half_blocks) * BLK, BLK, 0)
    other = lax.ppermute(candidate, "leaf", [(0, 1), (1, 0)])
    col_solved = jnp.where(in_half, candidate, other)

    schur = assembled - jnp.dot(row_solved, col_solved.T, precision=HIGHEST)

    row_global = leaf * rows + jnp.arange(rows, dtype=jnp.int32)
    col_global = front * cols + jnp.arange(cols, dtype=jnp.int32)
    col_start = jnp.minimum(front * cols, S - cols)
    left_rows = lax.dynamic_slice_in_dim(row_solved, col_start, cols, 1)
    left_top = jnp.pad(lax.dynamic_slice_in_dim(factor, col_start, cols, 1), ((0, rows - S), (0, 0)))
    left_part = jnp.where(row_global[:, None] < S, left_top, left_rows)
    right_top = jnp.pad(col_solved.T, ((0, rows - S), (0, 0)))
    right_part = jnp.where(row_global[:, None] < S, right_top, schur)
    return jnp.where(col_global[None, :] < S, left_part, right_part)


def solution(mesh):
    return jax.shard_map(
        per_device,
        mesh=mesh,
        in_specs=(P("leaf", "front"), P("leaf", None, "front"), P("leaf", None)),
        out_specs=P("leaf", "front"),
        check_vma=False,
    )
```

```python
import functools

import jax
import jax.numpy as jnp
from jax import lax
from jax.experimental import pallas as pl
from jax.experimental.pallas import tpu as pltpu
from jax.sharding import PartitionSpec as P

BLK = 128
S = 512
HIGHEST = lax.Precision.HIGHEST
MESH = pl.DeviceIdType.MESH


def gather_half(blocks, child_map, half, half_blocks):
    parent = half * half_blocks + jnp.arange(half_blocks, dtype=jnp.int32)
    hit = child_map[None, :] == parent[:, None]
    found = jnp.any(hit, axis=1)
    index = jnp.argmax(hit, axis=1)
    picked = jnp.take(blocks, index, axis=0)
    picked = jnp.where(found[:, None, None], picked, jnp.zeros_like(picked))
    return picked.reshape(half_blocks * BLK, blocks.shape[2])


def pivot_kernel(n_front, n_src, top_ref, out_ref, chunk, sem_a, sem_b, send_a, send_b, recv_g, send_g):
    leaf = lax.axis_index("leaf")
    me = lax.axis_index("front")
    per_src = n_front // n_src
    rows = chunk.shape[0]

    @pl.when((leaf == 0) & (me < n_src))
    def _():
        for k in range(per_src):
            src = top_ref.at[pl.ds(k * rows, rows)]
            dst = me * per_src + k
            if k == 0:
                @pl.when(me == 0)
                def _():
                    pltpu.make_async_copy(src, chunk, sem_a).start()

                @pl.when(me != 0)
                def _():
                    pltpu.make_async_remote_copy(
                        src, chunk, send_a.at[k], sem_a, device_id=(0, dst), device_id_type=MESH
                    ).start()
            else:
                pltpu.make_async_remote_copy(
                    src, chunk, send_a.at[k], sem_a, device_id=(0, dst), device_id_type=MESH
                ).start()

    @pl.when((leaf == 0) & (me == 0))
    def _():
        pltpu.make_async_copy(top_ref.at[pl.ds(0, rows)], chunk, sem_a).wait()

    @pl.when((leaf == 0) & (me != 0))
    def _():
        pltpu.make_async_remote_copy(
            top_ref.at[pl.ds(0, rows)], chunk, send_a.at[0], sem_a, device_id=(0, me), device_id_type=MESH
        ).wait_recv()

    @pl.when(leaf == 0)
    def _():
        pltpu.make_async_remote_copy(
            chunk, chunk, send_b, sem_b, device_id=(1, me), device_id_type=MESH
        ).start()

    @pl.when(leaf == 1)
    def _():
        pltpu.make_async_remote_copy(
            chunk, chunk, send_b, sem_b, device_id=(0, me), device_id_type=MESH
        ).wait_recv()

    pltpu.make_async_copy(chunk, out_ref.at[me], recv_g.at[me]).start()

    def send(j, carry):
        dst = lax.rem(me + j, n_front)
        pltpu.make_async_remote_copy(
            chunk, out_ref.at[me], send_g.at[j], recv_g.at[me], device_id=(leaf, dst), device_id_type=MESH
        ).start()
        return carry

    lax.fori_loop(1, n_front, send, 0)

    pltpu.make_async_copy(chunk, out_ref.at[me], recv_g.at[me]).wait()

    def receive(j, carry):
        src = lax.rem(me + j, n_front)
        pltpu.make_async_remote_copy(
            chunk, out_ref.at[src], send_g.at[j], recv_g.at[src], device_id=(leaf, src), device_id_type=MESH
        ).wait_recv()
        return carry

    lax.fori_loop(1, n_front, receive, 0)

    def sent(j, carry):
        dst = lax.rem(me + j, n_front)
        pltpu.make_async_remote_copy(
            chunk, out_ref.at[me], send_g.at[j], recv_g.at[me], device_id=(leaf, dst), device_id_type=MESH
        ).wait_send()
        return carry

    lax.fori_loop(1, n_front, sent, 0)

    @pl.when(leaf == 0)
    def _():
        pltpu.make_async_remote_copy(
            chunk, chunk, send_b, sem_b, device_id=(1, me), device_id_type=MESH
        ).wait_send()

    @pl.when((leaf == 0) & (me < n_src))
    def _():
        for k in range(per_src):
            src = top_ref.at[pl.ds(k * rows, rows)]
            dst = me * per_src + k
            if k == 0:
                @pl.when(me != 0)
                def _():
                    pltpu.make_async_remote_copy(
                        src, chunk, send_a.at[k], sem_a, device_id=(0, dst), device_id_type=MESH
                    ).wait_send()
            else:
                pltpu.make_async_remote_copy(
                    src, chunk, send_a.at[k], sem_a, device_id=(0, dst), device_id_type=MESH
                ).wait_send()


def broadcast_pivot(top, n_front):
    cols = top.shape[1]
    n_src = S // cols
    per_src = n_front // n_src
    rows = S // per_src
    gathered = pl.pallas_call(
        functools.partial(pivot_kernel, n_front, n_src),
        out_shape=jax.ShapeDtypeStruct((n_front, rows, cols), jnp.float32),
        in_specs=[pl.BlockSpec(memory_space=pltpu.VMEM)],
        out_specs=pl.BlockSpec(memory_space=pltpu.VMEM),
        scratch_shapes=[
            pltpu.VMEM((rows, cols), jnp.float32),
            pltpu.SemaphoreType.DMA,
            pltpu.SemaphoreType.DMA,
            pltpu.SemaphoreType.DMA((per_src,)),
            pltpu.SemaphoreType.DMA,
            pltpu.SemaphoreType.DMA((n_front,)),
            pltpu.SemaphoreType.DMA((n_front,)),
        ],
        compiler_params=pltpu.CompilerParams(has_side_effects=True),
    )(top)
    return gathered.reshape(n_src, per_src, rows, cols).transpose(1, 2, 0, 3).reshape(S, S)


PANEL = 8


def _mm(a, b):
    return jnp.dot(a, b, precision=HIGHEST, preferred_element_type=jnp.float32)


def _mm_t(a, b):
    return lax.dot_general(a, b, (((1,), (1,)), ((), ())), precision=HIGHEST,
                           preferred_element_type=jnp.float32)


def _mm_tn(a, b):
    return lax.dot_general(a, b, (((0,), (0,)), ((), ())), precision=HIGHEST,
                           preferred_element_type=jnp.float32)


def chol_inv_kernel(a_ref, l_ref, linv_ref, w_ref, d_ref, ut_ref, lo_ref, x_ref):
    n = a_ref.shape[0]
    b = d_ref.shape[0]
    nb = n // b
    lane = lax.broadcasted_iota(jnp.int32, (PANEL, b), 1)
    sub = lax.broadcasted_iota(jnp.int32, (PANEL, 1), 0)
    w_ref[...] = a_ref[...]
    l_ref[...] = jnp.zeros_like(l_ref)
    linv_ref[...] = jnp.zeros_like(linv_ref)

    def factor_panel(p, carry):
        k = pl.multiple_of(p * PANEL, PANEL)
        r = d_ref[pl.ds(k, PANEL), :]
        for t in range(PANEL):
            c = k + t
            colv = jnp.sum(jnp.where(lane == c, r, 0.0), axis=1, keepdims=True)
            piv = jnp.sum(jnp.where(sub == t, colv, 0.0), axis=0, keepdims=True)
            root = jnp.sqrt(piv)
            urow = jnp.where(lane[t:t + 1] >= c, r[t:t + 1] / root, 0.0)
            f = jnp.where(sub > t, colv / root, 0.0)
            r = jnp.where(sub == t, urow, r - f * urow)
        ut_ref[pl.ds(k, PANEL), :] = r
        d_ref[...] = d_ref[...] - _mm_tn(r, r)
        return carry

    def invert_panel(p, carry):
        k = pl.multiple_of(p * PANEL, PANEL)
        lrows = lo_ref[pl.ds(k, PANEL), :]
        e = (lane == sub + k).astype(jnp.float32) - _mm(lrows, x_ref[...])
        for t in range(PANEL):
            c = k + t
            colv = jnp.sum(jnp.where(lane == c, lrows, 0.0), axis=1, keepdims=True)
            diag = jnp.sum(jnp.where(sub == t, colv, 0.0), axis=0, keepdims=True)
            xrow = e[t:t + 1] / diag
            f = jnp.where(sub > t, colv, 0.0)
            e = jnp.where(sub == t, xrow, e - f * xrow)
        x_ref[pl.ds(k, PANEL), :] = e
        return carry

    for j in range(nb):
        jb = j * b
        d_ref[...] = w_ref[jb:jb + b, jb:jb + b]
        ut_ref[...] = jnp.zeros_like(ut_ref)
        x_ref[...] = jnp.zeros_like(x_ref)
        lax.fori_loop(0, b // PANEL, factor_panel, 0)
        lo_ref[...] = jnp.transpose(ut_ref[...])
        lax.fori_loop(0, b // PANEL, invert_panel, 0)
        l_ref[jb:jb + b, jb:jb + b] = lo_ref[...]
        linv_ref[jb:jb + b, jb:jb + b] = x_ref[...]
        if j < nb - 1:
            lp = _mm_t(w_ref[jb + b:, jb:jb + b], x_ref[...])
            l_ref[jb + b:, jb:jb + b] = lp
            w_ref[jb + b:, jb + b:] = w_ref[jb + b:, jb + b:] - _mm_t(lp, lp)
    for j in range(nb):
        for i in range(j + 1, nb):
            acc = jnp.zeros((b, b), jnp.float32)
            for k in range(j, i):
                acc = acc + _mm(l_ref[i * b:(i + 1) * b, k * b:(k + 1) * b], linv_ref[k * b:(k + 1) * b, j * b:(j + 1) * b])
            linv_ref[i * b:(i + 1) * b, j * b:(j + 1) * b] = -_mm(linv_ref[i * b:(i + 1) * b, i * b:(i + 1) * b], acc)


def chol_inv(a, b=128):
    n = a.shape[0]
    return pl.pallas_call(
        chol_inv_kernel,
        out_shape=(jax.ShapeDtypeStruct((n, n), jnp.float32), jax.ShapeDtypeStruct((n, n), jnp.float32)),
        in_specs=[pl.BlockSpec(memory_space=pltpu.VMEM)],
        out_specs=(pl.BlockSpec(memory_space=pltpu.VMEM), pl.BlockSpec(memory_space=pltpu.VMEM)),
        scratch_shapes=[
            pltpu.VMEM((n, n), jnp.float32),
            pltpu.VMEM((b, b), jnp.float32),
            pltpu.VMEM((b, b), jnp.float32),
            pltpu.VMEM((b, b), jnp.float32),
            pltpu.VMEM((b, b), jnp.float32),
        ],
    )(a)


def per_device(front_block, child_update, child_map):
    rows, cols = front_block.shape
    n_leaf = lax.axis_size("leaf")
    n_front = lax.axis_size("front")
    leaf = lax.axis_index("leaf")
    front = lax.axis_index("front")
    half_blocks = rows // BLK

    blocks = child_update[0].reshape(-1, BLK, cols)
    cmap = child_map[0]
    own = gather_half(blocks, cmap, leaf, half_blocks)
    send = gather_half(blocks, cmap, 1 - leaf, half_blocks)
    recv = lax.ppermute(send, "leaf", [(0, 1), (1, 0)])
    first = jnp.where(leaf == 0, own, recv)
    second = jnp.where(leaf == 0, recv, own)
    assembled = front_block + first + second

    top = assembled[:S]
    panel_rows = top.T

    piece = rows // n_front
    per_block = BLK // piece
    pieces = []
    for part in range(per_block):
        pairs = []
        for lf in range(n_leaf):
            for k in range(n_front // per_block):
                src = lf * half_blocks + k
                dst = lf * n_front + per_block * k + part
                pairs.append((src, dst))
        pieces.append(lax.ppermute(panel_rows[part * piece:(part + 1) * piece], ("leaf", "front"), pairs))
    my_piece = pieces[0]
    for part in range(1, per_block):
        my_piece = jnp.where(front % per_block == part, pieces[part], my_piece)
    pivot = broadcast_pivot(top, n_front)
    my_piece, pivot = lax.optimization_barrier((my_piece, pivot))
    panel = lax.all_gather(my_piece, "front", tiled=True)
    factor, inverse = chol_inv(pivot)

    own_solved = lax.dot_general(panel_rows, inverse, (((1,), (1,)), ((), ())), precision=HIGHEST)
    from_leaf0 = lax.ppermute(own_solved, "leaf", [(0, 1)])
    col_solved = jnp.where(leaf == 0, own_solved, from_leaf0)

    piv_cols = S // cols
    col_at = jnp.minimum(front, piv_cols - 1) * cols

    def pivot_columns():
        inv_rows = lax.dynamic_slice_in_dim(inverse, col_at, cols, 0)
        out = lax.dot_general(panel, inv_rows, (((1,), (1,)), ((), ())), precision=HIGHEST)
        top_rows = jnp.where(leaf == 0, lax.dynamic_slice_in_dim(factor, col_at, cols, 1), out[:S])
        return lax.dynamic_update_slice_in_dim(out, top_rows, 0, 0)

    def other_columns():
        weights = jnp.dot(col_solved, inverse, precision=HIGHEST).T
        out = assembled - jnp.dot(panel, weights, precision=HIGHEST)
        top_rows = jnp.where(leaf == 0, col_solved.T, out[:S])
        return lax.dynamic_update_slice_in_dim(out, top_rows, 0, 0)

    return lax.cond(front < piv_cols, pivot_columns, other_columns)


def solution(mesh):
    return jax.shard_map(
        per_device,
        mesh=mesh,
        in_specs=(P("leaf", "front"), P("leaf", None, "front"), P("leaf", None)),
        out_specs=P("leaf", "front"),
        check_vma=False,
    )
```

```python
import functools

import jax
import jax.numpy as jnp
from jax import lax
from jax.experimental import pallas as pl
from jax.experimental.pallas import tpu as pltpu
from jax.sharding import PartitionSpec as P

BLK = 128
S = 512
HIGHEST = lax.Precision.HIGHEST
MESH = pl.DeviceIdType.MESH


def gather_half(blocks, child_map, half, half_blocks):
    parent = half * half_blocks + jnp.arange(half_blocks, dtype=jnp.int32)
    hit = child_map[None, :] == parent[:, None]
    found = jnp.any(hit, axis=1)
    index = jnp.argmax(hit, axis=1)
    picked = jnp.take(blocks, index, axis=0)
    picked = jnp.where(found[:, None, None], picked, jnp.zeros_like(picked))
    return picked.reshape(half_blocks * BLK, blocks.shape[2])


def pivot_kernel(n_front, n_src, top_ref, out_ref, chunk, sem_a, sem_b, send_a, send_b, recv_g, send_g):
    leaf = lax.axis_index("leaf")
    me = lax.axis_index("front")
    per_src = n_front // n_src
    rows = chunk.shape[0]

    @pl.when((leaf == 0) & (me < n_src))
    def _():
        for k in range(per_src):
            src = top_ref.at[pl.ds(k * rows, rows)]
            dst = me * per_src + k
            if k == 0:
                @pl.when(me == 0)
                def _():
                    pltpu.make_async_copy(src, chunk, sem_a).start()

                @pl.when(me != 0)
                def _():
                    pltpu.make_async_remote_copy(
                        src, chunk, send_a.at[k], sem_a, device_id=(0, dst), device_id_type=MESH
                    ).start()
            else:
                pltpu.make_async_remote_copy(
                    src, chunk, send_a.at[k], sem_a, device_id=(0, dst), device_id_type=MESH
                ).start()

    @pl.when((leaf == 0) & (me == 0))
    def _():
        pltpu.make_async_copy(top_ref.at[pl.ds(0, rows)], chunk, sem_a).wait()

    @pl.when((leaf == 0) & (me != 0))
    def _():
        pltpu.make_async_remote_copy(
            top_ref.at[pl.ds(0, rows)], chunk, send_a.at[0], sem_a, device_id=(0, me), device_id_type=MESH
        ).wait_recv()

    @pl.when(leaf == 0)
    def _():
        pltpu.make_async_remote_copy(
            chunk, chunk, send_b, sem_b, device_id=(1, me), device_id_type=MESH
        ).start()

    @pl.when(leaf == 1)
    def _():
        pltpu.make_async_remote_copy(
            chunk, chunk, send_b, sem_b, device_id=(0, me), device_id_type=MESH
        ).wait_recv()

    pltpu.make_async_copy(chunk, out_ref.at[me], recv_g.at[me]).start()

    def send(j, carry):
        dst = lax.rem(me + j, n_front)
        pltpu.make_async_remote_copy(
            chunk, out_ref.at[me], send_g.at[j], recv_g.at[me], device_id=(leaf, dst), device_id_type=MESH
        ).start()
        return carry

    lax.fori_loop(1, n_front, send, 0)

    pltpu.make_async_copy(chunk, out_ref.at[me], recv_g.at[me]).wait()

    def receive(j, carry):
        src = lax.rem(me + j, n_front)
        pltpu.make_async_remote_copy(
            chunk, out_ref.at[src], send_g.at[j], recv_g.at[src], device_id=(leaf, src), device_id_type=MESH
        ).wait_recv()
        return carry

    lax.fori_loop(1, n_front, receive, 0)

    def sent(j, carry):
        dst = lax.rem(me + j, n_front)
        pltpu.make_async_remote_copy(
            chunk, out_ref.at[me], send_g.at[j], recv_g.at[me], device_id=(leaf, dst), device_id_type=MESH
        ).wait_send()
        return carry

    lax.fori_loop(1, n_front, sent, 0)

    @pl.when(leaf == 0)
    def _():
        pltpu.make_async_remote_copy(
            chunk, chunk, send_b, sem_b, device_id=(1, me), device_id_type=MESH
        ).wait_send()

    @pl.when((leaf == 0) & (me < n_src))
    def _():
        for k in range(per_src):
            src = top_ref.at[pl.ds(k * rows, rows)]
            dst = me * per_src + k
            if k == 0:
                @pl.when(me != 0)
                def _():
                    pltpu.make_async_remote_copy(
                        src, chunk, send_a.at[k], sem_a, device_id=(0, dst), device_id_type=MESH
                    ).wait_send()
            else:
                pltpu.make_async_remote_copy(
                    src, chunk, send_a.at[k], sem_a, device_id=(0, dst), device_id_type=MESH
                ).wait_send()


def broadcast_pivot(top, n_front):
    cols = top.shape[1]
    n_src = S // cols
    per_src = n_front // n_src
    rows = S // per_src
    gathered = pl.pallas_call(
        functools.partial(pivot_kernel, n_front, n_src),
        out_shape=jax.ShapeDtypeStruct((n_front, rows, cols), jnp.float32),
        in_specs=[pl.BlockSpec(memory_space=pltpu.VMEM)],
        out_specs=pl.BlockSpec(memory_space=pltpu.VMEM),
        scratch_shapes=[
            pltpu.VMEM((rows, cols), jnp.float32),
            pltpu.SemaphoreType.DMA,
            pltpu.SemaphoreType.DMA,
            pltpu.SemaphoreType.DMA((per_src,)),
            pltpu.SemaphoreType.DMA,
            pltpu.SemaphoreType.DMA((n_front,)),
            pltpu.SemaphoreType.DMA((n_front,)),
        ],
        compiler_params=pltpu.CompilerParams(has_side_effects=True),
    )(top)
    return gathered.reshape(n_src, per_src, rows, cols).transpose(1, 2, 0, 3).reshape(S, S)


PANEL = 8


def _mm(a, b):
    return jnp.dot(a, b, precision=HIGHEST, preferred_element_type=jnp.float32)


def _mm_t(a, b):
    return lax.dot_general(a, b, (((1,), (1,)), ((), ())), precision=HIGHEST,
                           preferred_element_type=jnp.float32)


def chol_inv_kernel(a_ref, l_ref, linv_ref, w_ref, d_ref, e_ref, ut_ref, x_ref):
    n = a_ref.shape[0]
    b = d_ref.shape[0]
    nb = n // b
    lane = lax.broadcasted_iota(jnp.int32, (PANEL, b), 1)
    sub = lax.broadcasted_iota(jnp.int32, (PANEL, 1), 0)
    eye = (lax.broadcasted_iota(jnp.int32, (b, b), 0) == lax.broadcasted_iota(jnp.int32, (b, b), 1)).astype(jnp.float32)
    w_ref[...] = a_ref[...]
    l_ref[...] = jnp.zeros_like(l_ref)
    linv_ref[...] = jnp.zeros_like(linv_ref)

    def panel(p, carry):
        k = pl.multiple_of(p * PANEL, PANEL)
        r = d_ref[pl.ds(k, PANEL), :]
        e = e_ref[pl.ds(k, PANEL), :]
        for t in range(PANEL):
            c = k + t
            colv = jnp.sum(jnp.where(lane == c, r, 0.0), axis=1, keepdims=True)
            piv = jnp.sum(jnp.where(sub == t, colv, 0.0), axis=0, keepdims=True)
            root = jnp.sqrt(piv)
            urow = jnp.where(lane[t:t + 1] >= c, r[t:t + 1] / root, 0.0)
            f = jnp.where(sub > t, colv / root, 0.0)
            r = jnp.where(sub == t, urow, r - f * urow)
            xrow = e[t:t + 1] / root
            e = jnp.where(sub == t, xrow, e - f * xrow)
        ut_ref[pl.ds(k, PANEL), :] = r
        x_ref[pl.ds(k, PANEL), :] = e
        rt = jnp.transpose(r)
        dd = d_ref[...]
        ee = e_ref[...]
        for t in range(PANEL):
            lcol = rt[:, t:t + 1]
            dd = dd - lcol * r[t:t + 1]
            ee = ee - lcol * e[t:t + 1]
        d_ref[...] = dd
        e_ref[...] = ee
        return carry

    for j in range(nb):
        jb = j * b
        d_ref[...] = w_ref[jb:jb + b, jb:jb + b]
        e_ref[...] = eye
        lax.fori_loop(0, b // PANEL, panel, 0)
        l_ref[jb:jb + b, jb:jb + b] = jnp.transpose(ut_ref[...])
        linv_ref[jb:jb + b, jb:jb + b] = x_ref[...]
        if j < nb - 1:
            lp = _mm_t(w_ref[jb + b:, jb:jb + b], x_ref[...])
            l_ref[jb + b:, jb:jb + b] = lp
            w_ref[jb + b:, jb + b:] = w_ref[jb + b:, jb + b:] - _mm_t(lp, lp)
    for j in range(nb):
        for i in range(j + 1, nb):
            acc = jnp.zeros((b, b), jnp.float32)
            for k in range(j, i):
                acc = acc + _mm(l_ref[i * b:(i + 1) * b, k * b:(k + 1) * b], linv_ref[k * b:(k + 1) * b, j * b:(j + 1) * b])
            linv_ref[i * b:(i + 1) * b, j * b:(j + 1) * b] = -_mm(linv_ref[i * b:(i + 1) * b, i * b:(i + 1) * b], acc)


def chol_inv(a, b=128):
    n = a.shape[0]
    return pl.pallas_call(
        chol_inv_kernel,
        out_shape=(jax.ShapeDtypeStruct((n, n), jnp.float32), jax.ShapeDtypeStruct((n, n), jnp.float32)),
        in_specs=[pl.BlockSpec(memory_space=pltpu.VMEM)],
        out_specs=(pl.BlockSpec(memory_space=pltpu.VMEM), pl.BlockSpec(memory_space=pltpu.VMEM)),
        scratch_shapes=[
            pltpu.VMEM((n, n), jnp.float32),
            pltpu.VMEM((b, b), jnp.float32),
            pltpu.VMEM((b, b), jnp.float32),
            pltpu.VMEM((b, b), jnp.float32),
            pltpu.VMEM((b, b), jnp.float32),
        ],
    )(a)


def per_device(front_block, child_update, child_map):
    rows, cols = front_block.shape
    n_leaf = lax.axis_size("leaf")
    n_front = lax.axis_size("front")
    leaf = lax.axis_index("leaf")
    front = lax.axis_index("front")
    half_blocks = rows // BLK

    blocks = child_update[0].reshape(-1, BLK, cols)
    cmap = child_map[0]
    own = gather_half(blocks, cmap, leaf, half_blocks)
    send = gather_half(blocks, cmap, 1 - leaf, half_blocks)
    recv = lax.ppermute(send, "leaf", [(0, 1), (1, 0)])
    first = jnp.where(leaf == 0, own, recv)
    second = jnp.where(leaf == 0, recv, own)
    assembled = front_block + first + second

    top = assembled[:S]
    panel_rows = top.T

    piece = rows // n_front
    per_block = BLK // piece
    pieces = []
    for part in range(per_block):
        pairs = []
        for lf in range(n_leaf):
            for k in range(n_front // per_block):
                src = lf * half_blocks + k
                dst = lf * n_front + per_block * k + part
                pairs.append((src, dst))
        pieces.append(lax.ppermute(panel_rows[part * piece:(part + 1) * piece], ("leaf", "front"), pairs))
    my_piece = pieces[0]
    for part in range(1, per_block):
        my_piece = jnp.where(front % per_block == part, pieces[part], my_piece)
    pivot = broadcast_pivot(top, n_front)
    my_piece, pivot = lax.optimization_barrier((my_piece, pivot))
    panel = lax.all_gather(my_piece, "front", tiled=True)
    factor, inverse = chol_inv(pivot)

    own_solved = lax.dot_general(panel_rows, inverse, (((1,), (1,)), ((), ())), precision=HIGHEST)
    from_leaf0 = lax.ppermute(own_solved, "leaf", [(0, 1)])
    col_solved = jnp.where(leaf == 0, own_solved, from_leaf0)

    piv_cols = S // cols
    col_at = jnp.minimum(front, piv_cols - 1) * cols

    def pivot_columns():
        inv_rows = lax.dynamic_slice_in_dim(inverse, col_at, cols, 0)
        out = lax.dot_general(panel, inv_rows, (((1,), (1,)), ((), ())), precision=HIGHEST)
        top_rows = jnp.where(leaf == 0, lax.dynamic_slice_in_dim(factor, col_at, cols, 1), out[:S])
        return lax.dynamic_update_slice_in_dim(out, top_rows, 0, 0)

    def other_columns():
        weights = jnp.dot(col_solved, inverse, precision=HIGHEST).T
        out = assembled - jnp.dot(panel, weights, precision=HIGHEST)
        top_rows = jnp.where(leaf == 0, col_solved.T, out[:S])
        return lax.dynamic_update_slice_in_dim(out, top_rows, 0, 0)

    return lax.cond(front < piv_cols, pivot_columns, other_columns)


def solution(mesh):
    return jax.shard_map(
        per_device,
        mesh=mesh,
        in_specs=(P("leaf", "front"), P("leaf", None, "front"), P("leaf", None)),
        out_specs=P("leaf", "front"),
        check_vma=False,
    )
```

```python
import functools

import jax
import jax.numpy as jnp
from jax import lax
from jax.experimental import pallas as pl
from jax.experimental.pallas import tpu as pltpu
from jax.sharding import PartitionSpec as P

BLK = 128
S = 512
HIGHEST = lax.Precision.HIGHEST
HIGH = lax.Precision.HIGH
MESH = pl.DeviceIdType.MESH


def gather_half(blocks, child_map, half, half_blocks):
    parent = half * half_blocks + jnp.arange(half_blocks, dtype=jnp.int32)
    hit = child_map[None, :] == parent[:, None]
    found = jnp.any(hit, axis=1)
    index = jnp.argmax(hit, axis=1)
    picked = jnp.take(blocks, index, axis=0)
    picked = jnp.where(found[:, None, None], picked, jnp.zeros_like(picked))
    return picked.reshape(half_blocks * BLK, blocks.shape[2])


def pivot_kernel(n_front, n_src, top_ref, out_ref, chunk, sem_a, sem_b, send_a, send_b, recv_g, send_g):
    leaf = lax.axis_index("leaf")
    me = lax.axis_index("front")
    per_src = n_front // n_src
    rows = chunk.shape[0]

    @pl.when((leaf == 0) & (me < n_src))
    def _():
        for k in range(per_src):
            src = top_ref.at[pl.ds(k * rows, rows)]
            dst = me * per_src + k
            if k == 0:
                @pl.when(me == 0)
                def _():
                    pltpu.make_async_copy(src, chunk, sem_a).start()

                @pl.when(me != 0)
                def _():
                    pltpu.make_async_remote_copy(
                        src, chunk, send_a.at[k], sem_a, device_id=(0, dst), device_id_type=MESH
                    ).start()
            else:
                pltpu.make_async_remote_copy(
                    src, chunk, send_a.at[k], sem_a, device_id=(0, dst), device_id_type=MESH
                ).start()

    @pl.when((leaf == 0) & (me == 0))
    def _():
        pltpu.make_async_copy(top_ref.at[pl.ds(0, rows)], chunk, sem_a).wait()

    @pl.when((leaf == 0) & (me != 0))
    def _():
        pltpu.make_async_remote_copy(
            top_ref.at[pl.ds(0, rows)], chunk, send_a.at[0], sem_a, device_id=(0, me), device_id_type=MESH
        ).wait_recv()

    @pl.when(leaf == 0)
    def _():
        pltpu.make_async_remote_copy(
            chunk, chunk, send_b, sem_b, device_id=(1, me), device_id_type=MESH
        ).start()

    @pl.when(leaf == 1)
    def _():
        pltpu.make_async_remote_copy(
            chunk, chunk, send_b, sem_b, device_id=(0, me), device_id_type=MESH
        ).wait_recv()

    pltpu.make_async_copy(chunk, out_ref.at[me], recv_g.at[me]).start()

    def send(j, carry):
        dst = lax.rem(me + j, n_front)
        pltpu.make_async_remote_copy(
            chunk, out_ref.at[me], send_g.at[j], recv_g.at[me], device_id=(leaf, dst), device_id_type=MESH
        ).start()
        return carry

    lax.fori_loop(1, n_front, send, 0)

    pltpu.make_async_copy(chunk, out_ref.at[me], recv_g.at[me]).wait()

    def receive(j, carry):
        src = lax.rem(me + j, n_front)
        pltpu.make_async_remote_copy(
            chunk, out_ref.at[src], send_g.at[j], recv_g.at[src], device_id=(leaf, src), device_id_type=MESH
        ).wait_recv()
        return carry

    lax.fori_loop(1, n_front, receive, 0)

    def sent(j, carry):
        dst = lax.rem(me + j, n_front)
        pltpu.make_async_remote_copy(
            chunk, out_ref.at[me], send_g.at[j], recv_g.at[me], device_id=(leaf, dst), device_id_type=MESH
        ).wait_send()
        return carry

    lax.fori_loop(1, n_front, sent, 0)

    @pl.when(leaf == 0)
    def _():
        pltpu.make_async_remote_copy(
            chunk, chunk, send_b, sem_b, device_id=(1, me), device_id_type=MESH
        ).wait_send()

    @pl.when((leaf == 0) & (me < n_src))
    def _():
        for k in range(per_src):
            src = top_ref.at[pl.ds(k * rows, rows)]
            dst = me * per_src + k
            if k == 0:
                @pl.when(me != 0)
                def _():
                    pltpu.make_async_remote_copy(
                        src, chunk, send_a.at[k], sem_a, device_id=(0, dst), device_id_type=MESH
                    ).wait_send()
            else:
                pltpu.make_async_remote_copy(
                    src, chunk, send_a.at[k], sem_a, device_id=(0, dst), device_id_type=MESH
                ).wait_send()


def broadcast_pivot(top, n_front):
    cols = top.shape[1]
    n_src = S // cols
    per_src = n_front // n_src
    rows = S // per_src
    gathered = pl.pallas_call(
        functools.partial(pivot_kernel, n_front, n_src),
        out_shape=jax.ShapeDtypeStruct((n_front, rows, cols), jnp.float32),
        in_specs=[pl.BlockSpec(memory_space=pltpu.VMEM)],
        out_specs=pl.BlockSpec(memory_space=pltpu.VMEM),
        scratch_shapes=[
            pltpu.VMEM((rows, cols), jnp.float32),
            pltpu.SemaphoreType.DMA,
            pltpu.SemaphoreType.DMA,
            pltpu.SemaphoreType.DMA((per_src,)),
            pltpu.SemaphoreType.DMA,
            pltpu.SemaphoreType.DMA((n_front,)),
            pltpu.SemaphoreType.DMA((n_front,)),
        ],
        compiler_params=pltpu.CompilerParams(has_side_effects=True),
    )(top)
    return gathered.reshape(n_src, per_src, rows, cols).transpose(1, 2, 0, 3).reshape(S, S)


PANEL = 8


def _mm(a, b):
    return jnp.dot(a, b, precision=HIGHEST, preferred_element_type=jnp.float32)


def _mm_t(a, b):
    return lax.dot_general(a, b, (((1,), (1,)), ((), ())), precision=HIGHEST,
                           preferred_element_type=jnp.float32)


def chol_inv_kernel(a_ref, l_ref, linv_ref, w_ref, d_ref, e_ref, ut_ref, x_ref):
    n = a_ref.shape[0]
    b = d_ref.shape[0]
    nb = n // b
    lane = lax.broadcasted_iota(jnp.int32, (PANEL, b), 1)
    sub = lax.broadcasted_iota(jnp.int32, (PANEL, 1), 0)
    eye = (lax.broadcasted_iota(jnp.int32, (b, b), 0) == lax.broadcasted_iota(jnp.int32, (b, b), 1)).astype(jnp.float32)
    w_ref[...] = a_ref[...]
    l_ref[...] = jnp.zeros_like(l_ref)
    linv_ref[...] = jnp.zeros_like(linv_ref)

    def panel(p, carry):
        k = pl.multiple_of(p * PANEL, PANEL)
        r = d_ref[pl.ds(k, PANEL), :]
        e = e_ref[pl.ds(k, PANEL), :]
        for t in range(PANEL):
            c = k + t
            colv = jnp.sum(jnp.where(lane == c, r, 0.0), axis=1, keepdims=True)
            piv = jnp.sum(jnp.where(sub == t, colv, 0.0), axis=0, keepdims=True)
            root = jnp.sqrt(piv)
            urow = jnp.where(lane[t:t + 1] >= c, r[t:t + 1] / root, 0.0)
            f = jnp.where(sub > t, colv / root, 0.0)
            r = jnp.where(sub == t, urow, r - f * urow)
            xrow = e[t:t + 1] / root
            e = jnp.where(sub == t, xrow, e - f * xrow)
        ut_ref[pl.ds(k, PANEL), :] = r
        x_ref[pl.ds(k, PANEL), :] = e
        rt = jnp.transpose(r)
        dd = d_ref[...]
        ee = e_ref[...]
        for t in range(PANEL):
            lcol = rt[:, t:t + 1]
            dd = dd - lcol * r[t:t + 1]
            ee = ee - lcol * e[t:t + 1]
        d_ref[...] = dd
        e_ref[...] = ee
        return carry

    for j in range(nb):
        jb = j * b
        d_ref[...] = w_ref[jb:jb + b, jb:jb + b]
        e_ref[...] = eye
        lax.fori_loop(0, b // PANEL, panel, 0)
        l_ref[jb:jb + b, jb:jb + b] = jnp.transpose(ut_ref[...])
        linv_ref[jb:jb + b, jb:jb + b] = x_ref[...]
        if j < nb - 1:
            lp = _mm_t(w_ref[jb + b:, jb:jb + b], x_ref[...])
            l_ref[jb + b:, jb:jb + b] = lp
            w_ref[jb + b:, jb + b:] = w_ref[jb + b:, jb + b:] - _mm_t(lp, lp)
    for j in range(nb):
        for i in range(j + 1, nb):
            acc = jnp.zeros((b, b), jnp.float32)
            for k in range(j, i):
                acc = acc + _mm(l_ref[i * b:(i + 1) * b, k * b:(k + 1) * b], linv_ref[k * b:(k + 1) * b, j * b:(j + 1) * b])
            linv_ref[i * b:(i + 1) * b, j * b:(j + 1) * b] = -_mm(linv_ref[i * b:(i + 1) * b, i * b:(i + 1) * b], acc)


def chol_inv(a, b=128):
    n = a.shape[0]
    return pl.pallas_call(
        chol_inv_kernel,
        out_shape=(jax.ShapeDtypeStruct((n, n), jnp.float32), jax.ShapeDtypeStruct((n, n), jnp.float32)),
        in_specs=[pl.BlockSpec(memory_space=pltpu.VMEM)],
        out_specs=(pl.BlockSpec(memory_space=pltpu.VMEM), pl.BlockSpec(memory_space=pltpu.VMEM)),
        scratch_shapes=[
            pltpu.VMEM((n, n), jnp.float32),
            pltpu.VMEM((b, b), jnp.float32),
            pltpu.VMEM((b, b), jnp.float32),
            pltpu.VMEM((b, b), jnp.float32),
            pltpu.VMEM((b, b), jnp.float32),
        ],
    )(a)


def per_device(front_block, child_update, child_map):
    rows, cols = front_block.shape
    n_leaf = lax.axis_size("leaf")
    n_front = lax.axis_size("front")
    leaf = lax.axis_index("leaf")
    front = lax.axis_index("front")
    half_blocks = rows // BLK

    blocks = child_update[0].reshape(-1, BLK, cols)
    cmap = child_map[0]
    own = gather_half(blocks, cmap, leaf, half_blocks)
    send = gather_half(blocks, cmap, 1 - leaf, half_blocks)
    recv = lax.ppermute(send, "leaf", [(0, 1), (1, 0)])
    first = jnp.where(leaf == 0, own, recv)
    second = jnp.where(leaf == 0, recv, own)
    assembled = front_block + first + second

    top = assembled[:S]
    panel_rows = top.T

    piece = rows // n_front
    per_block = BLK // piece
    pieces = []
    for part in range(per_block):
        pairs = []
        for lf in range(n_leaf):
            for k in range(n_front // per_block):
                src = lf * half_blocks + k
                dst = lf * n_front + per_block * k + part
                pairs.append((src, dst))
        pieces.append(lax.ppermute(panel_rows[part * piece:(part + 1) * piece], ("leaf", "front"), pairs))
    my_piece = pieces[0]
    for part in range(1, per_block):
        my_piece = jnp.where(front % per_block == part, pieces[part], my_piece)
    pivot = broadcast_pivot(top, n_front)
    partner_rows = lax.ppermute(panel_rows, "leaf", [(0, 1)])
    col_rows = jnp.where(leaf == 0, panel_rows, partner_rows)
    my_piece, pivot = lax.optimization_barrier((my_piece, pivot))
    panel = lax.all_gather(my_piece, "front", tiled=True)
    factor, inverse = chol_inv(pivot)

    col_solved = lax.dot_general(col_rows, inverse, (((1,), (1,)), ((), ())), precision=HIGHEST)

    piv_cols = S // cols
    col_at = jnp.minimum(front, piv_cols - 1) * cols

    def pivot_columns():
        inv_rows = lax.dynamic_slice_in_dim(inverse, col_at, cols, 0)
        out = lax.dot_general(panel, inv_rows, (((1,), (1,)), ((), ())), precision=HIGH)
        top_rows = jnp.where(leaf == 0, lax.dynamic_slice_in_dim(factor, col_at, cols, 1), out[:S])
        return lax.dynamic_update_slice_in_dim(out, top_rows, 0, 0)

    def other_columns():
        weights = jnp.dot(col_solved, inverse, precision=HIGHEST).T
        out = assembled - jnp.dot(panel, weights, precision=HIGH)
        top_rows = jnp.where(leaf == 0, col_solved.T, out[:S])
        return lax.dynamic_update_slice_in_dim(out, top_rows, 0, 0)

    return lax.cond(front < piv_cols, pivot_columns, other_columns)


def solution(mesh):
    return jax.shard_map(
        per_device,
        mesh=mesh,
        in_specs=(P("leaf", "front"), P("leaf", None, "front"), P("leaf", None)),
        out_specs=P("leaf", "front"),
        check_vma=False,
    )
```

```python
import functools

import jax
import jax.numpy as jnp
from jax import lax
from jax.experimental import pallas as pl
from jax.experimental.pallas import tpu as pltpu
from jax.sharding import PartitionSpec as P

BLK = 128
S = 512
HIGHEST = lax.Precision.HIGHEST
MESH = pl.DeviceIdType.MESH


def gather_half(blocks, child_map, half, half_blocks):
    parent = half * half_blocks + jnp.arange(half_blocks, dtype=jnp.int32)
    hit = child_map[None, :] == parent[:, None]
    found = jnp.any(hit, axis=1)
    index = jnp.argmax(hit, axis=1)
    picked = jnp.take(blocks, index, axis=0)
    picked = jnp.where(found[:, None, None], picked, jnp.zeros_like(picked))
    return picked.reshape(half_blocks * BLK, blocks.shape[2])


def pivot_kernel(n_front, n_src, top_ref, out_ref, chunk, sem_a, sem_b, send_a, send_b, recv_g, send_g):
    leaf = lax.axis_index("leaf")
    me = lax.axis_index("front")
    per_src = n_front // n_src
    rows = chunk.shape[0]

    @pl.when((leaf == 0) & (me < n_src))
    def _():
        for k in range(per_src):
            src = top_ref.at[pl.ds(k * rows, rows)]
            dst = me * per_src + k
            if k == 0:
                @pl.when(me == 0)
                def _():
                    pltpu.make_async_copy(src, chunk, sem_a).start()

                @pl.when(me != 0)
                def _():
                    pltpu.make_async_remote_copy(
                        src, chunk, send_a.at[k], sem_a, device_id=(0, dst), device_id_type=MESH
                    ).start()
            else:
                pltpu.make_async_remote_copy(
                    src, chunk, send_a.at[k], sem_a, device_id=(0, dst), device_id_type=MESH
                ).start()

    @pl.when((leaf == 0) & (me == 0))
    def _():
        pltpu.make_async_copy(top_ref.at[pl.ds(0, rows)], chunk, sem_a).wait()

    @pl.when((leaf == 0) & (me != 0))
    def _():
        pltpu.make_async_remote_copy(
            top_ref.at[pl.ds(0, rows)], chunk, send_a.at[0], sem_a, device_id=(0, me), device_id_type=MESH
        ).wait_recv()

    @pl.when(leaf == 0)
    def _():
        pltpu.make_async_remote_copy(
            chunk, chunk, send_b, sem_b, device_id=(1, me), device_id_type=MESH
        ).start()

    @pl.when(leaf == 1)
    def _():
        pltpu.make_async_remote_copy(
            chunk, chunk, send_b, sem_b, device_id=(0, me), device_id_type=MESH
        ).wait_recv()

    pltpu.make_async_copy(chunk, out_ref.at[me], recv_g.at[me]).start()

    def send(j, carry):
        dst = lax.rem(me + j, n_front)
        pltpu.make_async_remote_copy(
            chunk, out_ref.at[me], send_g.at[j], recv_g.at[me], device_id=(leaf, dst), device_id_type=MESH
        ).start()
        return carry

    lax.fori_loop(1, n_front, send, 0)

    pltpu.make_async_copy(chunk, out_ref.at[me], recv_g.at[me]).wait()

    def receive(j, carry):
        src = lax.rem(me + j, n_front)
        pltpu.make_async_remote_copy(
            chunk, out_ref.at[src], send_g.at[j], recv_g.at[src], device_id=(leaf, src), device_id_type=MESH
        ).wait_recv()
        return carry

    lax.fori_loop(1, n_front, receive, 0)

    def sent(j, carry):
        dst = lax.rem(me + j, n_front)
        pltpu.make_async_remote_copy(
            chunk, out_ref.at[me], send_g.at[j], recv_g.at[me], device_id=(leaf, dst), device_id_type=MESH
        ).wait_send()
        return carry

    lax.fori_loop(1, n_front, sent, 0)

    @pl.when(leaf == 0)
    def _():
        pltpu.make_async_remote_copy(
            chunk, chunk, send_b, sem_b, device_id=(1, me), device_id_type=MESH
        ).wait_send()

    @pl.when((leaf == 0) & (me < n_src))
    def _():
        for k in range(per_src):
            src = top_ref.at[pl.ds(k * rows, rows)]
            dst = me * per_src + k
            if k == 0:
                @pl.when(me != 0)
                def _():
                    pltpu.make_async_remote_copy(
                        src, chunk, send_a.at[k], sem_a, device_id=(0, dst), device_id_type=MESH
                    ).wait_send()
            else:
                pltpu.make_async_remote_copy(
                    src, chunk, send_a.at[k], sem_a, device_id=(0, dst), device_id_type=MESH
                ).wait_send()


def broadcast_pivot(top, n_front):
    cols = top.shape[1]
    n_src = S // cols
    per_src = n_front // n_src
    rows = S // per_src
    gathered = pl.pallas_call(
        functools.partial(pivot_kernel, n_front, n_src),
        out_shape=jax.ShapeDtypeStruct((n_front, rows, cols), jnp.float32),
        in_specs=[pl.BlockSpec(memory_space=pltpu.VMEM)],
        out_specs=pl.BlockSpec(memory_space=pltpu.VMEM),
        scratch_shapes=[
            pltpu.VMEM((rows, cols), jnp.float32),
            pltpu.SemaphoreType.DMA,
            pltpu.SemaphoreType.DMA,
            pltpu.SemaphoreType.DMA((per_src,)),
            pltpu.SemaphoreType.DMA,
            pltpu.SemaphoreType.DMA((n_front,)),
            pltpu.SemaphoreType.DMA((n_front,)),
        ],
        compiler_params=pltpu.CompilerParams(has_side_effects=True),
    )(top)
    return gathered.reshape(n_src, per_src, rows, cols).transpose(1, 2, 0, 3).reshape(S, S)


PANEL = 8


def _mm(a, b):
    return jnp.dot(a, b, precision=HIGHEST, preferred_element_type=jnp.float32)


def _mm_t(a, b):
    return lax.dot_general(a, b, (((1,), (1,)), ((), ())), precision=HIGHEST,
                           preferred_element_type=jnp.float32)


def chol_inv_kernel(a_ref, l_ref, linv_ref, w_ref, d_ref, e_ref, ut_ref, x_ref):
    n = a_ref.shape[0]
    b = d_ref.shape[0]
    nb = n // b
    lane = lax.broadcasted_iota(jnp.int32, (PANEL, b), 1)
    sub = lax.broadcasted_iota(jnp.int32, (PANEL, 1), 0)
    eye = (lax.broadcasted_iota(jnp.int32, (b, b), 0) == lax.broadcasted_iota(jnp.int32, (b, b), 1)).astype(jnp.float32)
    w_ref[...] = a_ref[...]
    l_ref[...] = jnp.zeros_like(l_ref)
    linv_ref[...] = jnp.zeros_like(linv_ref)

    def panel(p, carry):
        k = pl.multiple_of(p * PANEL, PANEL)
        r = d_ref[pl.ds(k, PANEL), :]
        e = e_ref[pl.ds(k, PANEL), :]
        for t in range(PANEL):
            c = k + t
            at_c = lane == c
            colv = jnp.sum(jnp.where(at_c, r, 0.0), axis=1, keepdims=True)
            piv = jnp.sum(jnp.where(at_c[t:t + 1], r[t:t + 1], 0.0), axis=1, keepdims=True)
            scale = 1.0 / jnp.sqrt(piv)
            urow = jnp.where(lane[t:t + 1] >= c, r[t:t + 1] * scale, 0.0)
            f = jnp.where(sub > t, colv * scale, 0.0)
            r = jnp.where(sub == t, urow, r - f * urow)
            xrow = e[t:t + 1] * scale
            e = jnp.where(sub == t, xrow, e - f * xrow)
        ut_ref[pl.ds(k, PANEL), :] = r
        x_ref[pl.ds(k, PANEL), :] = e
        rt = jnp.transpose(r)
        dd = d_ref[...]
        ee = e_ref[...]
        for t in range(PANEL):
            lcol = rt[:, t:t + 1]
            dd = dd - lcol * r[t:t + 1]
            ee = ee - lcol * e[t:t + 1]
        d_ref[...] = dd
        e_ref[...] = ee
        return carry

    for j in range(nb):
        jb = j * b
        d_ref[...] = w_ref[jb:jb + b, jb:jb + b]
        e_ref[...] = eye
        lax.fori_loop(0, b // PANEL, panel, 0)
        l_ref[jb:jb + b, jb:jb + b] = jnp.transpose(ut_ref[...])
        linv_ref[jb:jb + b, jb:jb + b] = x_ref[...]
        if j < nb - 1:
            lp = _mm_t(w_ref[jb + b:, jb:jb + b], x_ref[...])
            l_ref[jb + b:, jb:jb + b] = lp
            w_ref[jb + b:, jb + b:] = w_ref[jb + b:, jb + b:] - _mm_t(lp, lp)
    for j in range(nb):
        for i in range(j + 1, nb):
            acc = jnp.zeros((b, b), jnp.float32)
            for k in range(j, i):
                acc = acc + _mm(l_ref[i * b:(i + 1) * b, k * b:(k + 1) * b], linv_ref[k * b:(k + 1) * b, j * b:(j + 1) * b])
            linv_ref[i * b:(i + 1) * b, j * b:(j + 1) * b] = -_mm(linv_ref[i * b:(i + 1) * b, i * b:(i + 1) * b], acc)


def chol_inv(a, b=128):
    n = a.shape[0]
    return pl.pallas_call(
        chol_inv_kernel,
        out_shape=(jax.ShapeDtypeStruct((n, n), jnp.float32), jax.ShapeDtypeStruct((n, n), jnp.float32)),
        in_specs=[pl.BlockSpec(memory_space=pltpu.VMEM)],
        out_specs=(pl.BlockSpec(memory_space=pltpu.VMEM), pl.BlockSpec(memory_space=pltpu.VMEM)),
        scratch_shapes=[
            pltpu.VMEM((n, n), jnp.float32),
            pltpu.VMEM((b, b), jnp.float32),
            pltpu.VMEM((b, b), jnp.float32),
            pltpu.VMEM((b, b), jnp.float32),
            pltpu.VMEM((b, b), jnp.float32),
        ],
    )(a)


def per_device(front_block, child_update, child_map):
    rows, cols = front_block.shape
    n_leaf = lax.axis_size("leaf")
    n_front = lax.axis_size("front")
    leaf = lax.axis_index("leaf")
    front = lax.axis_index("front")
    half_blocks = rows // BLK

    blocks = child_update[0].reshape(-1, BLK, cols)
    cmap = child_map[0]
    own = gather_half(blocks, cmap, leaf, half_blocks)
    send = gather_half(blocks, cmap, 1 - leaf, half_blocks)
    recv = lax.ppermute(send, "leaf", [(0, 1), (1, 0)])
    first = jnp.where(leaf == 0, own, recv)
    second = jnp.where(leaf == 0, recv, own)
    assembled = front_block + first + second

    top = assembled[:S]
    panel_rows = top.T

    piece = rows // n_front
    per_block = BLK // piece
    pieces = []
    for part in range(per_block):
        pairs = []
        for lf in range(n_leaf):
            for k in range(n_front // per_block):
                src = lf * half_blocks + k
                dst = lf * n_front + per_block * k + part
                pairs.append((src, dst))
        pieces.append(lax.ppermute(panel_rows[part * piece:(part + 1) * piece], ("leaf", "front"), pairs))
    my_piece = pieces[0]
    for part in range(1, per_block):
        my_piece = jnp.where(front % per_block == part, pieces[part], my_piece)
    pivot = broadcast_pivot(top, n_front)
    partner_rows = lax.ppermute(panel_rows, "leaf", [(0, 1)])
    col_rows = jnp.where(leaf == 0, panel_rows, partner_rows)
    my_piece, pivot = lax.optimization_barrier((my_piece, pivot))
    panel = lax.all_gather(my_piece, "front", tiled=True)
    factor, inverse = chol_inv(pivot)

    col_solved = lax.dot_general(col_rows, inverse, (((1,), (1,)), ((), ())), precision=HIGHEST)

    piv_cols = S // cols
    col_at = jnp.minimum(front, piv_cols - 1) * cols

    def pivot_columns():
        inv_rows = lax.dynamic_slice_in_dim(inverse, col_at, cols, 0)
        out = lax.dot_general(panel, inv_rows, (((1,), (1,)), ((), ())), precision=HIGHEST)
        top_rows = jnp.where(leaf == 0, lax.dynamic_slice_in_dim(factor, col_at, cols, 1), out[:S])
        return lax.dynamic_update_slice_in_dim(out, top_rows, 0, 0)

    def other_columns():
        weights = jnp.dot(col_solved, inverse, precision=HIGHEST).T
        out = assembled - jnp.dot(panel, weights, precision=HIGHEST)
        top_rows = jnp.where(leaf == 0, col_solved.T, out[:S])
        return lax.dynamic_update_slice_in_dim(out, top_rows, 0, 0)

    return lax.cond(front < piv_cols, pivot_columns, other_columns)


def solution(mesh):
    return jax.shard_map(
        per_device,
        mesh=mesh,
        in_specs=(P("leaf", "front"), P("leaf", None, "front"), P("leaf", None)),
        out_specs=P("leaf", "front"),
        check_vma=False,
    )
```

```python
import functools

import jax
import jax.numpy as jnp
from jax import lax
from jax.experimental import pallas as pl
from jax.experimental.pallas import tpu as pltpu
from jax.sharding import PartitionSpec as P

BLK = 128
S = 512
HIGHEST = lax.Precision.HIGHEST
MESH = pl.DeviceIdType.MESH


def gather_half(blocks, child_map, half, half_blocks):
    parent = half * half_blocks + jnp.arange(half_blocks, dtype=jnp.int32)
    hit = child_map[None, :] == parent[:, None]
    found = jnp.any(hit, axis=1)
    index = jnp.argmax(hit, axis=1)
    picked = jnp.take(blocks, index, axis=0)
    picked = jnp.where(found[:, None, None], picked, jnp.zeros_like(picked))
    return picked.reshape(half_blocks * BLK, blocks.shape[2])


def pivot_kernel(n_front, n_src, top_ref, out_ref, chunk, sem_a, sem_b, send_a, send_b, recv_g, send_g):
    leaf = lax.axis_index("leaf")
    me = lax.axis_index("front")
    per_src = n_front // n_src
    rows = chunk.shape[0]

    @pl.when((leaf == 0) & (me < n_src))
    def _():
        for k in range(per_src):
            src = top_ref.at[pl.ds(k * rows, rows)]
            dst = me * per_src + k
            if k == 0:
                @pl.when(me == 0)
                def _():
                    pltpu.make_async_copy(src, chunk, sem_a).start()

                @pl.when(me != 0)
                def _():
                    pltpu.make_async_remote_copy(
                        src, chunk, send_a.at[k], sem_a, device_id=(0, dst), device_id_type=MESH
                    ).start()
            else:
                pltpu.make_async_remote_copy(
                    src, chunk, send_a.at[k], sem_a, device_id=(0, dst), device_id_type=MESH
                ).start()

    @pl.when((leaf == 0) & (me == 0))
    def _():
        pltpu.make_async_copy(top_ref.at[pl.ds(0, rows)], chunk, sem_a).wait()

    @pl.when((leaf == 0) & (me != 0))
    def _():
        pltpu.make_async_remote_copy(
            top_ref.at[pl.ds(0, rows)], chunk, send_a.at[0], sem_a, device_id=(0, me), device_id_type=MESH
        ).wait_recv()

    @pl.when(leaf == 0)
    def _():
        pltpu.make_async_remote_copy(
            chunk, chunk, send_b, sem_b, device_id=(1, me), device_id_type=MESH
        ).start()

    @pl.when(leaf == 1)
    def _():
        pltpu.make_async_remote_copy(
            chunk, chunk, send_b, sem_b, device_id=(0, me), device_id_type=MESH
        ).wait_recv()

    pltpu.make_async_copy(chunk, out_ref.at[me], recv_g.at[me]).start()

    def send(j, carry):
        dst = lax.rem(me + j, n_front)
        pltpu.make_async_remote_copy(
            chunk, out_ref.at[me], send_g.at[j], recv_g.at[me], device_id=(leaf, dst), device_id_type=MESH
        ).start()
        return carry

    lax.fori_loop(1, n_front, send, 0)

    pltpu.make_async_copy(chunk, out_ref.at[me], recv_g.at[me]).wait()

    def receive(j, carry):
        src = lax.rem(me + j, n_front)
        pltpu.make_async_remote_copy(
            chunk, out_ref.at[src], send_g.at[j], recv_g.at[src], device_id=(leaf, src), device_id_type=MESH
        ).wait_recv()
        return carry

    lax.fori_loop(1, n_front, receive, 0)

    def sent(j, carry):
        dst = lax.rem(me + j, n_front)
        pltpu.make_async_remote_copy(
            chunk, out_ref.at[me], send_g.at[j], recv_g.at[me], device_id=(leaf, dst), device_id_type=MESH
        ).wait_send()
        return carry

    lax.fori_loop(1, n_front, sent, 0)

    @pl.when(leaf == 0)
    def _():
        pltpu.make_async_remote_copy(
            chunk, chunk, send_b, sem_b, device_id=(1, me), device_id_type=MESH
        ).wait_send()

    @pl.when((leaf == 0) & (me < n_src))
    def _():
        for k in range(per_src):
            src = top_ref.at[pl.ds(k * rows, rows)]
            dst = me * per_src + k
            if k == 0:
                @pl.when(me != 0)
                def _():
                    pltpu.make_async_remote_copy(
                        src, chunk, send_a.at[k], sem_a, device_id=(0, dst), device_id_type=MESH
                    ).wait_send()
            else:
                pltpu.make_async_remote_copy(
                    src, chunk, send_a.at[k], sem_a, device_id=(0, dst), device_id_type=MESH
                ).wait_send()


def broadcast_pivot(top, n_front):
    cols = top.shape[1]
    n_src = S // cols
    per_src = n_front // n_src
    rows = S // per_src
    gathered = pl.pallas_call(
        functools.partial(pivot_kernel, n_front, n_src),
        out_shape=jax.ShapeDtypeStruct((n_front, rows, cols), jnp.float32),
        in_specs=[pl.BlockSpec(memory_space=pltpu.VMEM)],
        out_specs=pl.BlockSpec(memory_space=pltpu.VMEM),
        scratch_shapes=[
            pltpu.VMEM((rows, cols), jnp.float32),
            pltpu.SemaphoreType.DMA,
            pltpu.SemaphoreType.DMA,
            pltpu.SemaphoreType.DMA((per_src,)),
            pltpu.SemaphoreType.DMA,
            pltpu.SemaphoreType.DMA((n_front,)),
            pltpu.SemaphoreType.DMA((n_front,)),
        ],
        compiler_params=pltpu.CompilerParams(has_side_effects=True),
    )(top)
    return gathered.reshape(n_src, per_src, rows, cols).transpose(1, 2, 0, 3).reshape(S, S)


PANEL = 8


def _mm(a, b):
    return jnp.dot(a, b, precision=HIGHEST, preferred_element_type=jnp.float32)


def _mm_t(a, b):
    return lax.dot_general(a, b, (((1,), (1,)), ((), ())), precision=HIGHEST,
                           preferred_element_type=jnp.float32)


def chol_inv_kernel(a_ref, l_ref, linv_ref, w_ref, d_ref, e_ref, ut_ref, x_ref, rt_ref):
    n = a_ref.shape[0]
    b = d_ref.shape[0]
    nb = n // b
    lane = lax.broadcasted_iota(jnp.int32, (PANEL, b), 1)
    sub = lax.broadcasted_iota(jnp.int32, (PANEL, 1), 0)
    eye = (lax.broadcasted_iota(jnp.int32, (b, b), 0) == lax.broadcasted_iota(jnp.int32, (b, b), 1)).astype(jnp.float32)
    w_ref[...] = a_ref[...]
    l_ref[...] = jnp.zeros_like(l_ref)
    linv_ref[...] = jnp.zeros_like(linv_ref)

    def panel(p, carry):
        k = pl.multiple_of(p * PANEL, PANEL)
        r = d_ref[pl.ds(k, PANEL), :]
        e = e_ref[pl.ds(k, PANEL), :]
        for t in range(PANEL):
            c = k + t
            at_c = lane == c
            colv = jnp.sum(jnp.where(at_c, r, 0.0), axis=1, keepdims=True)
            piv = jnp.sum(jnp.where(at_c[t:t + 1], r[t:t + 1], 0.0), axis=1, keepdims=True)
            scale = 1.0 / jnp.sqrt(piv)
            urow = jnp.where(lane[t:t + 1] >= c, r[t:t + 1] * scale, 0.0)
            f = jnp.where(sub > t, colv * scale, 0.0)
            r = jnp.where(sub == t, urow, r - f * urow)
            xrow = e[t:t + 1] * scale
            e = jnp.where(sub == t, xrow, e - f * xrow)
        ut_ref[pl.ds(k, PANEL), :] = r
        x_ref[pl.ds(k, PANEL), :] = e
        rt_ref[...] = jnp.transpose(r)

        def update(g, carry):
            row0 = pl.multiple_of(g * PANEL, PANEL)
            lg = rt_ref[pl.ds(row0, PANEL), :]
            dd = d_ref[pl.ds(row0, PANEL), :]
            ee = e_ref[pl.ds(row0, PANEL), :]
            for t in range(PANEL):
                lcol = lg[:, t:t + 1]
                dd = dd - lcol * r[t:t + 1]
                ee = ee - lcol * e[t:t + 1]
            d_ref[pl.ds(row0, PANEL), :] = dd
            e_ref[pl.ds(row0, PANEL), :] = ee
            return carry

        lax.fori_loop(p + 1, b // PANEL, update, 0)
        return carry

    for j in range(nb):
        jb = j * b
        d_ref[...] = w_ref[jb:jb + b, jb:jb + b]
        e_ref[...] = eye
        lax.fori_loop(0, b // PANEL, panel, 0)
        l_ref[jb:jb + b, jb:jb + b] = jnp.transpose(ut_ref[...])
        linv_ref[jb:jb + b, jb:jb + b] = x_ref[...]
        if j < nb - 1:
            lp = _mm_t(w_ref[jb + b:, jb:jb + b], x_ref[...])
            l_ref[jb + b:, jb:jb + b] = lp
            w_ref[jb + b:, jb + b:] = w_ref[jb + b:, jb + b:] - _mm_t(lp, lp)
    for j in range(nb):
        for i in range(j + 1, nb):
            acc = jnp.zeros((b, b), jnp.float32)
            for k in range(j, i):
                acc = acc + _mm(l_ref[i * b:(i + 1) * b, k * b:(k + 1) * b], linv_ref[k * b:(k + 1) * b, j * b:(j + 1) * b])
            linv_ref[i * b:(i + 1) * b, j * b:(j + 1) * b] = -_mm(linv_ref[i * b:(i + 1) * b, i * b:(i + 1) * b], acc)


def chol_inv(a, b=128):
    n = a.shape[0]
    return pl.pallas_call(
        chol_inv_kernel,
        out_shape=(jax.ShapeDtypeStruct((n, n), jnp.float32), jax.ShapeDtypeStruct((n, n), jnp.float32)),
        in_specs=[pl.BlockSpec(memory_space=pltpu.VMEM)],
        out_specs=(pl.BlockSpec(memory_space=pltpu.VMEM), pl.BlockSpec(memory_space=pltpu.VMEM)),
        scratch_shapes=[
            pltpu.VMEM((n, n), jnp.float32),
            pltpu.VMEM((b, b), jnp.float32),
            pltpu.VMEM((b, b), jnp.float32),
            pltpu.VMEM((b, b), jnp.float32),
            pltpu.VMEM((b, b), jnp.float32),
            pltpu.VMEM((b, PANEL), jnp.float32),
        ],
    )(a)


def per_device(front_block, child_update, child_map):
    rows, cols = front_block.shape
    n_leaf = lax.axis_size("leaf")
    n_front = lax.axis_size("front")
    leaf = lax.axis_index("leaf")
    front = lax.axis_index("front")
    half_blocks = rows // BLK

    blocks = child_update[0].reshape(-1, BLK, cols)
    cmap = child_map[0]
    own = gather_half(blocks, cmap, leaf, half_blocks)
    send = gather_half(blocks, cmap, 1 - leaf, half_blocks)
    recv = lax.ppermute(send, "leaf", [(0, 1), (1, 0)])
    first = jnp.where(leaf == 0, own, recv)
    second = jnp.where(leaf == 0, recv, own)
    assembled = front_block + first + second

    top = assembled[:S]
    panel_rows = top.T

    piece = rows // n_front
    per_block = BLK // piece
    pieces = []
    for part in range(per_block):
        pairs = []
        for lf in range(n_leaf):
            for k in range(n_front // per_block):
                src = lf * half_blocks + k
                dst = lf * n_front + per_block * k + part
                pairs.append((src, dst))
        pieces.append(lax.ppermute(panel_rows[part * piece:(part + 1) * piece], ("leaf", "front"), pairs))
    my_piece = pieces[0]
    for part in range(1, per_block):
        my_piece = jnp.where(front % per_block == part, pieces[part], my_piece)
    pivot = broadcast_pivot(top, n_front)
    partner_rows = lax.ppermute(panel_rows, "leaf", [(0, 1)])
    col_rows = jnp.where(leaf == 0, panel_rows, partner_rows)
    my_piece, pivot = lax.optimization_barrier((my_piece, pivot))
    panel = lax.all_gather(my_piece, "front", tiled=True)
    factor, inverse = chol_inv(pivot)

    col_solved = lax.dot_general(col_rows, inverse, (((1,), (1,)), ((), ())), precision=HIGHEST)

    piv_cols = S // cols
    col_at = jnp.minimum(front, piv_cols - 1) * cols

    def pivot_columns():
        inv_rows = lax.dynamic_slice_in_dim(inverse, col_at, cols, 0)
        out = lax.dot_general(panel, inv_rows, (((1,), (1,)), ((), ())), precision=HIGHEST)
        top_rows = jnp.where(leaf == 0, lax.dynamic_slice_in_dim(factor, col_at, cols, 1), out[:S])
        return lax.dynamic_update_slice_in_dim(out, top_rows, 0, 0)

    def other_columns():
        weights = jnp.dot(col_solved, inverse, precision=HIGHEST).T
        out = assembled - jnp.dot(panel, weights, precision=HIGHEST)
        top_rows = jnp.where(leaf == 0, col_solved.T, out[:S])
        return lax.dynamic_update_slice_in_dim(out, top_rows, 0, 0)

    return lax.cond(front < piv_cols, pivot_columns, other_columns)


def solution(mesh):
    return jax.shard_map(
        per_device,
        mesh=mesh,
        in_specs=(P("leaf", "front"), P("leaf", None, "front"), P("leaf", None)),
        out_specs=P("leaf", "front"),
        check_vma=False,
    )
```

```python
import functools

import jax
import jax.numpy as jnp
from jax import lax
from jax.experimental import pallas as pl
from jax.experimental.pallas import tpu as pltpu
from jax.sharding import PartitionSpec as P

BLK = 128
S = 512
HIGHEST = lax.Precision.HIGHEST
MESH = pl.DeviceIdType.MESH


def gather_half(blocks, child_map, half, half_blocks):
    parent = half * half_blocks + jnp.arange(half_blocks, dtype=jnp.int32)
    hit = child_map[None, :] == parent[:, None]
    found = jnp.any(hit, axis=1)
    index = jnp.argmax(hit, axis=1)
    picked = jnp.take(blocks, index, axis=0)
    picked = jnp.where(found[:, None, None], picked, jnp.zeros_like(picked))
    return picked.reshape(half_blocks * BLK, blocks.shape[2])


def pivot_kernel(n_front, n_src, top_ref, out_ref, chunk, sem_a, sem_b, send_a, send_b, recv_g, send_g):
    leaf = lax.axis_index("leaf")
    me = lax.axis_index("front")
    per_src = n_front // n_src
    rows = chunk.shape[0]

    @pl.when((leaf == 0) & (me < n_src))
    def _():
        for k in range(per_src):
            src = top_ref.at[pl.ds(k * rows, rows)]
            dst = me * per_src + k
            if k == 0:
                @pl.when(me == 0)
                def _():
                    pltpu.make_async_copy(src, chunk, sem_a).start()

                @pl.when(me != 0)
                def _():
                    pltpu.make_async_remote_copy(
                        src, chunk, send_a.at[k], sem_a, device_id=(0, dst), device_id_type=MESH
                    ).start()
            else:
                pltpu.make_async_remote_copy(
                    src, chunk, send_a.at[k], sem_a, device_id=(0, dst), device_id_type=MESH
                ).start()

    @pl.when((leaf == 0) & (me == 0))
    def _():
        pltpu.make_async_copy(top_ref.at[pl.ds(0, rows)], chunk, sem_a).wait()

    @pl.when((leaf == 0) & (me != 0))
    def _():
        pltpu.make_async_remote_copy(
            top_ref.at[pl.ds(0, rows)], chunk, send_a.at[0], sem_a, device_id=(0, me), device_id_type=MESH
        ).wait_recv()

    @pl.when(leaf == 0)
    def _():
        pltpu.make_async_remote_copy(
            chunk, chunk, send_b, sem_b, device_id=(1, me), device_id_type=MESH
        ).start()

    @pl.when(leaf == 1)
    def _():
        pltpu.make_async_remote_copy(
            chunk, chunk, send_b, sem_b, device_id=(0, me), device_id_type=MESH
        ).wait_recv()

    pltpu.make_async_copy(chunk, out_ref.at[me], recv_g.at[me]).start()

    def send(j, carry):
        dst = lax.rem(me + j, n_front)
        pltpu.make_async_remote_copy(
            chunk, out_ref.at[me], send_g.at[j], recv_g.at[me], device_id=(leaf, dst), device_id_type=MESH
        ).start()
        return carry

    lax.fori_loop(1, n_front, send, 0)

    pltpu.make_async_copy(chunk, out_ref.at[me], recv_g.at[me]).wait()

    def receive(j, carry):
        src = lax.rem(me + j, n_front)
        pltpu.make_async_remote_copy(
            chunk, out_ref.at[src], send_g.at[j], recv_g.at[src], device_id=(leaf, src), device_id_type=MESH
        ).wait_recv()
        return carry

    lax.fori_loop(1, n_front, receive, 0)

    def sent(j, carry):
        dst = lax.rem(me + j, n_front)
        pltpu.make_async_remote_copy(
            chunk, out_ref.at[me], send_g.at[j], recv_g.at[me], device_id=(leaf, dst), device_id_type=MESH
        ).wait_send()
        return carry

    lax.fori_loop(1, n_front, sent, 0)

    @pl.when(leaf == 0)
    def _():
        pltpu.make_async_remote_copy(
            chunk, chunk, send_b, sem_b, device_id=(1, me), device_id_type=MESH
        ).wait_send()

    @pl.when((leaf == 0) & (me < n_src))
    def _():
        for k in range(per_src):
            src = top_ref.at[pl.ds(k * rows, rows)]
            dst = me * per_src + k
            if k == 0:
                @pl.when(me != 0)
                def _():
                    pltpu.make_async_remote_copy(
                        src, chunk, send_a.at[k], sem_a, device_id=(0, dst), device_id_type=MESH
                    ).wait_send()
            else:
                pltpu.make_async_remote_copy(
                    src, chunk, send_a.at[k], sem_a, device_id=(0, dst), device_id_type=MESH
                ).wait_send()


def broadcast_pivot(top, n_front):
    cols = top.shape[1]
    n_src = S // cols
    per_src = n_front // n_src
    rows = S // per_src
    gathered = pl.pallas_call(
        functools.partial(pivot_kernel, n_front, n_src),
        out_shape=jax.ShapeDtypeStruct((n_front, rows, cols), jnp.float32),
        in_specs=[pl.BlockSpec(memory_space=pltpu.VMEM)],
        out_specs=pl.BlockSpec(memory_space=pltpu.VMEM),
        scratch_shapes=[
            pltpu.VMEM((rows, cols), jnp.float32),
            pltpu.SemaphoreType.DMA,
            pltpu.SemaphoreType.DMA,
            pltpu.SemaphoreType.DMA((per_src,)),
            pltpu.SemaphoreType.DMA,
            pltpu.SemaphoreType.DMA((n_front,)),
            pltpu.SemaphoreType.DMA((n_front,)),
        ],
        compiler_params=pltpu.CompilerParams(has_side_effects=True),
    )(top)
    return gathered


PANEL = 8


def _mm(a, b):
    return jnp.dot(a, b, precision=HIGHEST, preferred_element_type=jnp.float32)


def _mm_t(a, b):
    return lax.dot_general(a, b, (((1,), (1,)), ((), ())), precision=HIGHEST,
                           preferred_element_type=jnp.float32)


def chol_inv_kernel(a_ref, l_ref, linv_ref, w_ref, d_ref, e_ref, ut_ref, x_ref):
    n = w_ref.shape[0]
    b = d_ref.shape[0]
    nb = n // b
    lane = lax.broadcasted_iota(jnp.int32, (PANEL, b), 1)
    sub = lax.broadcasted_iota(jnp.int32, (PANEL, 1), 0)
    eye = (lax.broadcasted_iota(jnp.int32, (b, b), 0) == lax.broadcasted_iota(jnp.int32, (b, b), 1)).astype(jnp.float32)
    n_slots, rows, cols = a_ref.shape
    per_src = n_slots // (n // cols)
    for slot in range(n_slots):
        c, k = divmod(slot, per_src)
        w_ref[k * rows:(k + 1) * rows, c * cols:(c + 1) * cols] = a_ref[slot]
    l_ref[...] = jnp.zeros_like(l_ref)
    linv_ref[...] = jnp.zeros_like(linv_ref)

    def panel(p, carry):
        k = pl.multiple_of(p * PANEL, PANEL)
        r = d_ref[pl.ds(k, PANEL), :]
        e = e_ref[pl.ds(k, PANEL), :]
        for t in range(PANEL):
            c = k + t
            at_c = lane == c
            colv = jnp.sum(jnp.where(at_c, r, 0.0), axis=1, keepdims=True)
            piv = jnp.sum(jnp.where(at_c[t:t + 1], r[t:t + 1], 0.0), axis=1, keepdims=True)
            scale = 1.0 / jnp.sqrt(piv)
            urow = jnp.where(lane[t:t + 1] >= c, r[t:t + 1] * scale, 0.0)
            f = jnp.where(sub > t, colv * scale, 0.0)
            r = jnp.where(sub == t, urow, r - f * urow)
            xrow = e[t:t + 1] * scale
            e = jnp.where(sub == t, xrow, e - f * xrow)
        ut_ref[pl.ds(k, PANEL), :] = r
        x_ref[pl.ds(k, PANEL), :] = e
        rt = jnp.transpose(r)
        dd = d_ref[...]
        ee = e_ref[...]
        for t in range(PANEL):
            lcol = rt[:, t:t + 1]
            dd = dd - lcol * r[t:t + 1]
            ee = ee - lcol * e[t:t + 1]
        d_ref[...] = dd
        e_ref[...] = ee
        return carry

    for j in range(nb):
        jb = j * b
        d_ref[...] = w_ref[jb:jb + b, jb:jb + b]
        e_ref[...] = eye
        lax.fori_loop(0, b // PANEL, panel, 0)
        l_ref[jb:jb + b, jb:jb + b] = jnp.transpose(ut_ref[...])
        linv_ref[jb:jb + b, jb:jb + b] = x_ref[...]
        if j < nb - 1:
            lp = _mm_t(w_ref[jb + b:, jb:jb + b], x_ref[...])
            l_ref[jb + b:, jb:jb + b] = lp
            w_ref[jb + b:, jb + b:] = w_ref[jb + b:, jb + b:] - _mm_t(lp, lp)
    for j in range(nb):
        for i in range(j + 1, nb):
            acc = jnp.zeros((b, b), jnp.float32)
            for k in range(j, i):
                acc = acc + _mm(l_ref[i * b:(i + 1) * b, k * b:(k + 1) * b], linv_ref[k * b:(k + 1) * b, j * b:(j + 1) * b])
            linv_ref[i * b:(i + 1) * b, j * b:(j + 1) * b] = -_mm(linv_ref[i * b:(i + 1) * b, i * b:(i + 1) * b], acc)


def chol_inv(a, n, b=128):
    return pl.pallas_call(
        chol_inv_kernel,
        out_shape=(jax.ShapeDtypeStruct((n, n), jnp.float32), jax.ShapeDtypeStruct((n, n), jnp.float32)),
        in_specs=[pl.BlockSpec(memory_space=pltpu.VMEM)],
        out_specs=(pl.BlockSpec(memory_space=pltpu.VMEM), pl.BlockSpec(memory_space=pltpu.VMEM)),
        scratch_shapes=[
            pltpu.VMEM((n, n), jnp.float32),
            pltpu.VMEM((b, b), jnp.float32),
            pltpu.VMEM((b, b), jnp.float32),
            pltpu.VMEM((b, b), jnp.float32),
            pltpu.VMEM((b, b), jnp.float32),
        ],
    )(a)


def per_device(front_block, child_update, child_map):
    rows, cols = front_block.shape
    n_leaf = lax.axis_size("leaf")
    n_front = lax.axis_size("front")
    leaf = lax.axis_index("leaf")
    front = lax.axis_index("front")
    half_blocks = rows // BLK

    blocks = child_update[0].reshape(-1, BLK, cols)
    cmap = child_map[0]
    own = gather_half(blocks, cmap, leaf, half_blocks)
    send = gather_half(blocks, cmap, 1 - leaf, half_blocks)
    recv = lax.ppermute(send, "leaf", [(0, 1), (1, 0)])
    first = jnp.where(leaf == 0, own, recv)
    second = jnp.where(leaf == 0, recv, own)
    assembled = front_block + first + second

    top = assembled[:S]
    panel_rows = top.T

    piece = rows // n_front
    per_block = BLK // piece
    pieces = []
    for part in range(per_block):
        pairs = []
        for lf in range(n_leaf):
            for k in range(n_front // per_block):
                src = lf * half_blocks + k
                dst = lf * n_front + per_block * k + part
                pairs.append((src, dst))
        pieces.append(lax.ppermute(panel_rows[part * piece:(part + 1) * piece], ("leaf", "front"), pairs))
    my_piece = pieces[0]
    for part in range(1, per_block):
        my_piece = jnp.where(front % per_block == part, pieces[part], my_piece)
    partner_rows = lax.ppermute(panel_rows, "leaf", [(0, 1)])
    col_rows = jnp.where(leaf == 0, panel_rows, partner_rows)
    col_rows, top = lax.optimization_barrier((col_rows, top))
    pivot = broadcast_pivot(top, n_front)
    my_piece, pivot = lax.optimization_barrier((my_piece, pivot))
    panel = lax.all_gather(my_piece, "front", tiled=True)
    factor, inverse = chol_inv(pivot, S)

    col_solved = lax.dot_general(col_rows, inverse, (((1,), (1,)), ((), ())), precision=HIGHEST)

    piv_cols = S // cols
    col_at = jnp.minimum(front, piv_cols - 1) * cols

    def pivot_columns():
        inv_rows = lax.dynamic_slice_in_dim(inverse, col_at, cols, 0)
        out = lax.dot_general(panel, inv_rows, (((1,), (1,)), ((), ())), precision=HIGHEST)
        top_rows = jnp.where(leaf == 0, lax.dynamic_slice_in_dim(factor, col_at, cols, 1), out[:S])
        return lax.dynamic_update_slice_in_dim(out, top_rows, 0, 0)

    def other_columns():
        weights = jnp.dot(col_solved, inverse, precision=HIGHEST).T
        out = assembled - jnp.dot(panel, weights, precision=HIGHEST)
        top_rows = jnp.where(leaf == 0, col_solved.T, out[:S])
        return lax.dynamic_update_slice_in_dim(out, top_rows, 0, 0)

    return lax.cond(front < piv_cols, pivot_columns, other_columns)


def solution(mesh):
    return jax.shard_map(
        per_device,
        mesh=mesh,
        in_specs=(P("leaf", "front"), P("leaf", None, "front"), P("leaf", None)),
        out_specs=P("leaf", "front"),
        check_vma=False,
    )
```

```python
import functools

import jax
import jax.numpy as jnp
from jax import lax
from jax.experimental import pallas as pl
from jax.experimental.pallas import tpu as pltpu
from jax.sharding import PartitionSpec as P

BLK = 128
S = 512
HIGHEST = lax.Precision.HIGHEST
MESH = pl.DeviceIdType.MESH


def gather_half(blocks, child_map, half, half_blocks):
    parent = half * half_blocks + jnp.arange(half_blocks, dtype=jnp.int32)
    hit = child_map[None, :] == parent[:, None]
    found = jnp.any(hit, axis=1)
    index = jnp.argmax(hit, axis=1)
    picked = jnp.take(blocks, index, axis=0)
    picked = jnp.where(found[:, None, None], picked, jnp.zeros_like(picked))
    return picked.reshape(half_blocks * BLK, blocks.shape[2])


def pivot_kernel(dims, top_ref, out_ref, own_sem, peer_sem, send_y, send_z, send_leaf, send_x):
    n_z, n_y, n_x = dims
    leaf = lax.axis_index("leaf")
    me = lax.axis_index("front")
    x = me % n_x
    y = (me // n_x) % n_y
    z = me // (n_x * n_y)
    mine = out_ref.at[x]

    def remote(dst_leaf, dst_front, sem):
        return pltpu.make_async_remote_copy(
            mine, mine, sem, own_sem, device_id=(dst_leaf, dst_front), device_id_type=MESH
        )

    source = (leaf == 0) & (y == 0) & (z == 0)

    @pl.when(source)
    def _():
        pltpu.make_async_copy(top_ref, mine, own_sem).start()
        pltpu.make_async_copy(top_ref, mine, own_sem).wait()
        for dy in range(1, n_y):
            remote(0, dy * n_x + x, send_y.at[dy]).start()

    @pl.when(jnp.logical_not(source))
    def _():
        remote(0, me, send_y.at[0]).wait_recv()

    @pl.when((leaf == 0) & (z == 0))
    def _():
        for dz in range(1, n_z):
            remote(0, dz * n_x * n_y + y * n_x + x, send_z.at[dz]).start()

    @pl.when(leaf == 0)
    def _():
        remote(1, me, send_leaf).start()

    for dx in range(1, n_x):
        dst = me - x + (x + dx) % n_x
        pltpu.make_async_remote_copy(
            mine, mine, send_x.at[dx], peer_sem.at[x], device_id=(leaf, dst), device_id_type=MESH
        ).start()

    for dx in range(1, n_x):
        src = (x + dx) % n_x
        pltpu.make_async_remote_copy(
            out_ref.at[src], out_ref.at[src], send_x.at[dx], peer_sem.at[src],
            device_id=(leaf, me - x + src), device_id_type=MESH
        ).wait_recv()

    for dx in range(1, n_x):
        dst = me - x + (x + dx) % n_x
        pltpu.make_async_remote_copy(
            mine, mine, send_x.at[dx], peer_sem.at[x], device_id=(leaf, dst), device_id_type=MESH
        ).wait_send()

    @pl.when(leaf == 0)
    def _():
        remote(1, me, send_leaf).wait_send()

    @pl.when((leaf == 0) & (z == 0))
    def _():
        for dz in range(1, n_z):
            remote(0, dz * n_x * n_y + y * n_x + x, send_z.at[dz]).wait_send()

    @pl.when(source)
    def _():
        for dy in range(1, n_y):
            remote(0, dy * n_x + x, send_y.at[dy]).wait_send()


def broadcast_pivot(top, dims):
    rows, cols = top.shape
    n_src = S // cols
    return pl.pallas_call(
        functools.partial(pivot_kernel, dims),
        out_shape=jax.ShapeDtypeStruct((n_src, rows, cols), jnp.float32),
        in_specs=[pl.BlockSpec(memory_space=pltpu.VMEM)],
        out_specs=pl.BlockSpec(memory_space=pltpu.VMEM),
        scratch_shapes=[
            pltpu.SemaphoreType.DMA,
            pltpu.SemaphoreType.DMA((n_src,)),
            pltpu.SemaphoreType.DMA((dims[1],)),
            pltpu.SemaphoreType.DMA((dims[0],)),
            pltpu.SemaphoreType.DMA,
            pltpu.SemaphoreType.DMA((n_src,)),
        ],
        compiler_params=pltpu.CompilerParams(has_side_effects=True),
    )(top)


PANEL = 8


def _mm(a, b):
    return jnp.dot(a, b, precision=HIGHEST, preferred_element_type=jnp.float32)


def _mm_t(a, b):
    return lax.dot_general(a, b, (((1,), (1,)), ((), ())), precision=HIGHEST,
                           preferred_element_type=jnp.float32)


def chol_inv_kernel(a_ref, l_ref, linv_ref, w_ref, d_ref, e_ref, ut_ref, x_ref):
    n = w_ref.shape[0]
    b = d_ref.shape[0]
    nb = n // b
    lane = lax.broadcasted_iota(jnp.int32, (PANEL, b), 1)
    sub = lax.broadcasted_iota(jnp.int32, (PANEL, 1), 0)
    eye = (lax.broadcasted_iota(jnp.int32, (b, b), 0) == lax.broadcasted_iota(jnp.int32, (b, b), 1)).astype(jnp.float32)
    n_cb, _, cols = a_ref.shape
    for c in range(n_cb):
        w_ref[:, c * cols:(c + 1) * cols] = a_ref[c]
    l_ref[...] = jnp.zeros_like(l_ref)
    linv_ref[...] = jnp.zeros_like(linv_ref)

    def panel(p, carry):
        k = pl.multiple_of(p * PANEL, PANEL)
        r = d_ref[pl.ds(k, PANEL), :]
        e = e_ref[pl.ds(k, PANEL), :]
        for t in range(PANEL):
            c = k + t
            at_c = lane == c
            colv = jnp.sum(jnp.where(at_c, r, 0.0), axis=1, keepdims=True)
            piv = jnp.sum(jnp.where(at_c[t:t + 1], r[t:t + 1], 0.0), axis=1, keepdims=True)
            scale = 1.0 / jnp.sqrt(piv)
            urow = jnp.where(lane[t:t + 1] >= c, r[t:t + 1] * scale, 0.0)
            f = jnp.where(sub > t, colv * scale, 0.0)
            r = jnp.where(sub == t, urow, r - f * urow)
            xrow = e[t:t + 1] * scale
            e = jnp.where(sub == t, xrow, e - f * xrow)
        ut_ref[pl.ds(k, PANEL), :] = r
        x_ref[pl.ds(k, PANEL), :] = e
        rt = jnp.transpose(r)
        dd = d_ref[...]
        ee = e_ref[...]
        for t in range(PANEL):
            lcol = rt[:, t:t + 1]
            dd = dd - lcol * r[t:t + 1]
            ee = ee - lcol * e[t:t + 1]
        d_ref[...] = dd
        e_ref[...] = ee
        return carry

    for j in range(nb):
        jb = j * b
        d_ref[...] = w_ref[jb:jb + b, jb:jb + b]
        e_ref[...] = eye
        lax.fori_loop(0, b // PANEL, panel, 0)
        l_ref[jb:jb + b, jb:jb + b] = jnp.transpose(ut_ref[...])
        linv_ref[jb:jb + b, jb:jb + b] = x_ref[...]
        if j < nb - 1:
            lp = _mm_t(w_ref[jb + b:, jb:jb + b], x_ref[...])
            l_ref[jb + b:, jb:jb + b] = lp
            w_ref[jb + b:, jb + b:] = w_ref[jb + b:, jb + b:] - _mm_t(lp, lp)
    for j in range(nb):
        for i in range(j + 1, nb):
            acc = jnp.zeros((b, b), jnp.float32)
            for k in range(j, i):
                acc = acc + _mm(l_ref[i * b:(i + 1) * b, k * b:(k + 1) * b], linv_ref[k * b:(k + 1) * b, j * b:(j + 1) * b])
            linv_ref[i * b:(i + 1) * b, j * b:(j + 1) * b] = -_mm(linv_ref[i * b:(i + 1) * b, i * b:(i + 1) * b], acc)


def chol_inv(a, n, b=128):
    return pl.pallas_call(
        chol_inv_kernel,
        out_shape=(jax.ShapeDtypeStruct((n, n), jnp.float32), jax.ShapeDtypeStruct((n, n), jnp.float32)),
        in_specs=[pl.BlockSpec(memory_space=pltpu.VMEM)],
        out_specs=(pl.BlockSpec(memory_space=pltpu.VMEM), pl.BlockSpec(memory_space=pltpu.VMEM)),
        scratch_shapes=[
            pltpu.VMEM((n, n), jnp.float32),
            pltpu.VMEM((b, b), jnp.float32),
            pltpu.VMEM((b, b), jnp.float32),
            pltpu.VMEM((b, b), jnp.float32),
            pltpu.VMEM((b, b), jnp.float32),
        ],
    )(a)


def per_device(front_block, child_update, child_map):
    rows, cols = front_block.shape
    n_leaf = lax.axis_size("leaf")
    n_front = lax.axis_size("front")
    leaf = lax.axis_index("leaf")
    front = lax.axis_index("front")
    half_blocks = rows // BLK

    blocks = child_update[0].reshape(-1, BLK, cols)
    cmap = child_map[0]
    own = gather_half(blocks, cmap, leaf, half_blocks)
    send = gather_half(blocks, cmap, 1 - leaf, half_blocks)
    recv = lax.ppermute(send, "leaf", [(0, 1), (1, 0)])
    first = jnp.where(leaf == 0, own, recv)
    second = jnp.where(leaf == 0, recv, own)
    assembled = front_block + first + second

    top = assembled[:S]
    panel_rows = top.T

    piece = rows // n_front
    per_block = BLK // piece
    pieces = []
    for part in range(per_block):
        pairs = []
        for lf in range(n_leaf):
            for k in range(n_front // per_block):
                src = lf * half_blocks + k
                dst = lf * n_front + per_block * k + part
                pairs.append((src, dst))
        pieces.append(lax.ppermute(panel_rows[part * piece:(part + 1) * piece], ("leaf", "front"), pairs))
    my_piece = pieces[0]
    for part in range(1, per_block):
        my_piece = jnp.where(front % per_block == part, pieces[part], my_piece)
    partner_rows = lax.ppermute(panel_rows, "leaf", [(0, 1)])
    col_rows = jnp.where(leaf == 0, panel_rows, partner_rows)
    pivot = broadcast_pivot(top, (4, 4, 4))
    my_piece, pivot = lax.optimization_barrier((my_piece, pivot))
    panel = lax.all_gather(my_piece, "front", tiled=True)
    factor, inverse = chol_inv(pivot, S)

    col_solved = lax.dot_general(col_rows, inverse, (((1,), (1,)), ((), ())), precision=HIGHEST)

    piv_cols = S // cols
    col_at = jnp.minimum(front, piv_cols - 1) * cols

    def pivot_columns():
        inv_rows = lax.dynamic_slice_in_dim(inverse, col_at, cols, 0)
        out = lax.dot_general(panel, inv_rows, (((1,), (1,)), ((), ())), precision=HIGHEST)
        top_rows = jnp.where(leaf == 0, lax.dynamic_slice_in_dim(factor, col_at, cols, 1), out[:S])
        return lax.dynamic_update_slice_in_dim(out, top_rows, 0, 0)

    def other_columns():
        weights = jnp.dot(col_solved, inverse, precision=HIGHEST).T
        out = assembled - jnp.dot(panel, weights, precision=HIGHEST)
        top_rows = jnp.where(leaf == 0, col_solved.T, out[:S])
        return lax.dynamic_update_slice_in_dim(out, top_rows, 0, 0)

    return lax.cond(front < piv_cols, pivot_columns, other_columns)


def solution(mesh):
    return jax.shard_map(
        per_device,
        mesh=mesh,
        in_specs=(P("leaf", "front"), P("leaf", None, "front"), P("leaf", None)),
        out_specs=P("leaf", "front"),
        check_vma=False,
    )
```

```python
import functools

import jax
import jax.numpy as jnp
from jax import lax
from jax.experimental import pallas as pl
from jax.experimental.pallas import tpu as pltpu
from jax.sharding import PartitionSpec as P

BLK = 128
S = 512
HIGHEST = lax.Precision.HIGHEST
MESH = pl.DeviceIdType.MESH


def gather_half(blocks, child_map, half, half_blocks):
    parent = half * half_blocks + jnp.arange(half_blocks, dtype=jnp.int32)
    hit = child_map[None, :] == parent[:, None]
    found = jnp.any(hit, axis=1)
    index = jnp.argmax(hit, axis=1)
    picked = jnp.take(blocks, index, axis=0)
    picked = jnp.where(found[:, None, None], picked, jnp.zeros_like(picked))
    return picked.reshape(half_blocks * BLK, blocks.shape[2])


def pivot_kernel(dims, top_ref, out_ref, own_sem, peer_sem, send_y, send_z, send_leaf, send_x):
    n_z, n_y, n_x = dims
    leaf = lax.axis_index("leaf")
    me = lax.axis_index("front")
    x = me % n_x
    y = (me // n_x) % n_y
    z = me // (n_x * n_y)
    mine = out_ref.at[x]

    def remote(dst_leaf, dst_front, sem):
        return pltpu.make_async_remote_copy(
            mine, mine, sem, own_sem, device_id=(dst_leaf, dst_front), device_id_type=MESH
        )

    source = (leaf == 0) & (y == 0) & (z == 0)

    @pl.when(source)
    def _():
        pltpu.make_async_copy(top_ref, mine, own_sem).start()
        pltpu.make_async_copy(top_ref, mine, own_sem).wait()
        for dy in range(1, n_y):
            remote(0, dy * n_x + x, send_y.at[dy]).start()

    @pl.when(jnp.logical_not(source))
    def _():
        remote(0, me, send_y.at[0]).wait_recv()

    @pl.when((leaf == 0) & (z == 0))
    def _():
        for dz in range(1, n_z):
            remote(0, dz * n_x * n_y + y * n_x + x, send_z.at[dz]).start()

    @pl.when(leaf == 0)
    def _():
        remote(1, me, send_leaf).start()

    for dx in range(1, n_x):
        dst = me - x + (x + dx) % n_x
        pltpu.make_async_remote_copy(
            mine, mine, send_x.at[dx], peer_sem.at[x], device_id=(leaf, dst), device_id_type=MESH
        ).start()

    for dx in range(1, n_x):
        src = (x + dx) % n_x
        pltpu.make_async_remote_copy(
            out_ref.at[src], out_ref.at[src], send_x.at[dx], peer_sem.at[src],
            device_id=(leaf, me - x + src), device_id_type=MESH
        ).wait_recv()

    for dx in range(1, n_x):
        dst = me - x + (x + dx) % n_x
        pltpu.make_async_remote_copy(
            mine, mine, send_x.at[dx], peer_sem.at[x], device_id=(leaf, dst), device_id_type=MESH
        ).wait_send()

    @pl.when(leaf == 0)
    def _():
        remote(1, me, send_leaf).wait_send()

    @pl.when((leaf == 0) & (z == 0))
    def _():
        for dz in range(1, n_z):
            remote(0, dz * n_x * n_y + y * n_x + x, send_z.at[dz]).wait_send()

    @pl.when(source)
    def _():
        for dy in range(1, n_y):
            remote(0, dy * n_x + x, send_y.at[dy]).wait_send()


def broadcast_pivot(top, dims):
    rows, cols = top.shape
    n_src = S // cols
    return pl.pallas_call(
        functools.partial(pivot_kernel, dims),
        out_shape=jax.ShapeDtypeStruct((n_src, rows, cols), jnp.float32),
        in_specs=[pl.BlockSpec(memory_space=pltpu.VMEM)],
        out_specs=pl.BlockSpec(memory_space=pltpu.VMEM),
        scratch_shapes=[
            pltpu.SemaphoreType.DMA,
            pltpu.SemaphoreType.DMA((n_src,)),
            pltpu.SemaphoreType.DMA((dims[1],)),
            pltpu.SemaphoreType.DMA((dims[0],)),
            pltpu.SemaphoreType.DMA,
            pltpu.SemaphoreType.DMA((n_src,)),
        ],
        compiler_params=pltpu.CompilerParams(has_side_effects=True),
    )(top)


PANEL = 8


def _mm(a, b):
    return jnp.dot(a, b, precision=HIGHEST, preferred_element_type=jnp.float32)


def _mm_t(a, b):
    return lax.dot_general(a, b, (((1,), (1,)), ((), ())), precision=HIGHEST,
                           preferred_element_type=jnp.float32)


def chol_inv_kernel(a_ref, l_ref, linv_ref, w_ref, d_ref, e_ref, ut_ref, x_ref):
    n = w_ref.shape[0]
    b = d_ref.shape[0]
    nb = n // b
    lane = lax.broadcasted_iota(jnp.int32, (PANEL, b), 1)
    sub = lax.broadcasted_iota(jnp.int32, (PANEL, 1), 0)
    eye = (lax.broadcasted_iota(jnp.int32, (b, b), 0) == lax.broadcasted_iota(jnp.int32, (b, b), 1)).astype(jnp.float32)
    n_cb, _, cols = a_ref.shape
    for c in range(n_cb):
        w_ref[:, c * cols:(c + 1) * cols] = a_ref[c]
    l_ref[...] = jnp.zeros_like(l_ref)
    linv_ref[...] = jnp.zeros_like(linv_ref)

    def panel(p, carry):
        k = pl.multiple_of(p * PANEL, PANEL)
        r = d_ref[pl.ds(k, PANEL), :]
        e = e_ref[pl.ds(k, PANEL), :]
        for t in range(PANEL):
            c = k + t
            at_c = lane == c
            colv = jnp.sum(jnp.where(at_c, r, 0.0), axis=1, keepdims=True)
            piv = jnp.sum(jnp.where(at_c[t:t + 1], r[t:t + 1], 0.0), axis=1, keepdims=True)
            scale = 1.0 / jnp.sqrt(piv)
            urow = jnp.where(lane[t:t + 1] >= c, r[t:t + 1] * scale, 0.0)
            f = jnp.where(sub > t, colv * scale, 0.0)
            r = jnp.where(sub == t, urow, r - f * urow)
            xrow = e[t:t + 1] * scale
            e = jnp.where(sub == t, xrow, e - f * xrow)
        ut_ref[pl.ds(k, PANEL), :] = r
        x_ref[pl.ds(k, PANEL), :] = e
        rt = jnp.transpose(r)
        dd = d_ref[...]
        ee = e_ref[...]
        for t in range(PANEL):
            lcol = rt[:, t:t + 1]
            dd = dd - lcol * r[t:t + 1]
            ee = ee - lcol * e[t:t + 1]
        d_ref[...] = dd
        e_ref[...] = ee
        return carry

    for j in range(nb):
        jb = j * b
        d_ref[...] = w_ref[jb:jb + b, jb:jb + b]
        e_ref[...] = eye
        lax.fori_loop(0, b // PANEL, panel, 0)
        l_ref[jb:jb + b, jb:jb + b] = jnp.transpose(ut_ref[...])
        linv_ref[jb:jb + b, jb:jb + b] = x_ref[...]
        if j < nb - 1:
            lp = _mm_t(w_ref[jb + b:, jb:jb + b], x_ref[...])
            l_ref[jb + b:, jb:jb + b] = lp
            w_ref[jb + b:, jb + b:] = w_ref[jb + b:, jb + b:] - _mm_t(lp, lp)
    for j in range(nb):
        for i in range(j + 1, nb):
            acc = jnp.zeros((b, b), jnp.float32)
            for k in range(j, i):
                acc = acc + _mm(l_ref[i * b:(i + 1) * b, k * b:(k + 1) * b], linv_ref[k * b:(k + 1) * b, j * b:(j + 1) * b])
            linv_ref[i * b:(i + 1) * b, j * b:(j + 1) * b] = -_mm(linv_ref[i * b:(i + 1) * b, i * b:(i + 1) * b], acc)


def chol_inv(a, n, b=128):
    return pl.pallas_call(
        chol_inv_kernel,
        out_shape=(jax.ShapeDtypeStruct((n, n), jnp.float32), jax.ShapeDtypeStruct((n, n), jnp.float32)),
        in_specs=[pl.BlockSpec(memory_space=pltpu.VMEM)],
        out_specs=(pl.BlockSpec(memory_space=pltpu.VMEM), pl.BlockSpec(memory_space=pltpu.VMEM)),
        scratch_shapes=[
            pltpu.VMEM((n, n), jnp.float32),
            pltpu.VMEM((b, b), jnp.float32),
            pltpu.VMEM((b, b), jnp.float32),
            pltpu.VMEM((b, b), jnp.float32),
            pltpu.VMEM((b, b), jnp.float32),
        ],
    )(a)


def per_device(front_block, child_update, child_map):
    rows, cols = front_block.shape
    n_leaf = lax.axis_size("leaf")
    n_front = lax.axis_size("front")
    leaf = lax.axis_index("leaf")
    front = lax.axis_index("front")
    half_blocks = rows // BLK

    blocks = child_update[0].reshape(-1, BLK, cols)
    cmap = child_map[0]
    own = gather_half(blocks, cmap, leaf, half_blocks)
    send = gather_half(blocks, cmap, 1 - leaf, half_blocks)
    recv = lax.ppermute(send, "leaf", [(0, 1), (1, 0)])
    first = jnp.where(leaf == 0, own, recv)
    second = jnp.where(leaf == 0, recv, own)
    assembled = front_block + first + second

    top = assembled[:S]
    panel_rows = top.T

    piece = rows // n_front
    per_block = BLK // piece
    pieces = []
    for part in range(per_block):
        pairs = []
        for lf in range(n_leaf):
            for k in range(n_front // per_block):
                src = lf * half_blocks + k
                dst = lf * n_front + per_block * k + part
                pairs.append((src, dst))
        pieces.append(lax.ppermute(panel_rows[part * piece:(part + 1) * piece], ("leaf", "front"), pairs))
    my_piece = pieces[0]
    for part in range(1, per_block):
        my_piece = jnp.where(front % per_block == part, pieces[part], my_piece)
    partner_rows = lax.ppermute(panel_rows, "leaf", [(0, 1)])
    col_rows = jnp.where(leaf == 0, panel_rows, partner_rows)
    pivot = broadcast_pivot(top, (4, 4, 4))
    panel = lax.all_gather(my_piece, "front", tiled=True)
    factor, inverse = chol_inv(pivot, S)

    col_solved = lax.dot_general(col_rows, inverse, (((1,), (1,)), ((), ())), precision=HIGHEST)

    piv_cols = S // cols
    col_at = jnp.minimum(front, piv_cols - 1) * cols

    def pivot_columns():
        inv_rows = lax.dynamic_slice_in_dim(inverse, col_at, cols, 0)
        out = lax.dot_general(panel, inv_rows, (((1,), (1,)), ((), ())), precision=HIGHEST)
        top_rows = jnp.where(leaf == 0, lax.dynamic_slice_in_dim(factor, col_at, cols, 1), out[:S])
        return lax.dynamic_update_slice_in_dim(out, top_rows, 0, 0)

    def other_columns():
        weights = jnp.dot(col_solved, inverse, precision=HIGHEST).T
        out = assembled - jnp.dot(panel, weights, precision=HIGHEST)
        top_rows = jnp.where(leaf == 0, col_solved.T, out[:S])
        return lax.dynamic_update_slice_in_dim(out, top_rows, 0, 0)

    return lax.cond(front < piv_cols, pivot_columns, other_columns)


def solution(mesh):
    return jax.shard_map(
        per_device,
        mesh=mesh,
        in_specs=(P("leaf", "front"), P("leaf", None, "front"), P("leaf", None)),
        out_specs=P("leaf", "front"),
        check_vma=False,
    )
```

```python
import functools

import jax
import jax.numpy as jnp
from jax import lax
from jax.experimental import pallas as pl
from jax.experimental.pallas import tpu as pltpu
from jax.sharding import PartitionSpec as P

BLK = 128
S = 512
HIGHEST = lax.Precision.HIGHEST
MESH = pl.DeviceIdType.MESH


def gather_half(blocks, child_map, half, half_blocks):
    parent = half * half_blocks + jnp.arange(half_blocks, dtype=jnp.int32)
    hit = child_map[None, :] == parent[:, None]
    found = jnp.any(hit, axis=1)
    index = jnp.argmax(hit, axis=1)
    picked = jnp.take(blocks, index, axis=0)
    picked = jnp.where(found[:, None, None], picked, jnp.zeros_like(picked))
    return picked.reshape(half_blocks * BLK, blocks.shape[2])


def pivot_kernel(dims, top_ref, out_ref, own_sem, peer_sem, send_y, send_z, send_leaf, send_x):
    n_z, n_y, n_x = dims
    leaf = lax.axis_index("leaf")
    me = lax.axis_index("front")
    x = me % n_x
    y = (me // n_x) % n_y
    z = me // (n_x * n_y)
    mine = out_ref.at[x]

    def remote(dst_leaf, dst_front, sem):
        return pltpu.make_async_remote_copy(
            mine, mine, sem, own_sem, device_id=(dst_leaf, dst_front), device_id_type=MESH
        )

    source = (leaf == 0) & (y == 0) & (z == 0)

    @pl.when(source)
    def _():
        pltpu.make_async_copy(top_ref, mine, own_sem).start()
        pltpu.make_async_copy(top_ref, mine, own_sem).wait()
        for dy in range(1, n_y):
            remote(0, dy * n_x + x, send_y.at[dy]).start()

    @pl.when(jnp.logical_not(source))
    def _():
        remote(0, me, send_y.at[0]).wait_recv()

    @pl.when((leaf == 0) & (z == 0))
    def _():
        for dz in range(1, n_z):
            remote(0, dz * n_x * n_y + y * n_x + x, send_z.at[dz]).start()

    @pl.when(leaf == 0)
    def _():
        remote(1, me, send_leaf).start()

    for dx in range(1, n_x):
        dst = me - x + (x + dx) % n_x
        pltpu.make_async_remote_copy(
            mine, mine, send_x.at[dx], peer_sem.at[x], device_id=(leaf, dst), device_id_type=MESH
        ).start()

    for dx in range(1, n_x):
        src = (x + dx) % n_x
        pltpu.make_async_remote_copy(
            out_ref.at[src], out_ref.at[src], send_x.at[dx], peer_sem.at[src],
            device_id=(leaf, me - x + src), device_id_type=MESH
        ).wait_recv()

    for dx in range(1, n_x):
        dst = me - x + (x + dx) % n_x
        pltpu.make_async_remote_copy(
            mine, mine, send_x.at[dx], peer_sem.at[x], device_id=(leaf, dst), device_id_type=MESH
        ).wait_send()

    @pl.when(leaf == 0)
    def _():
        remote(1, me, send_leaf).wait_send()

    @pl.when((leaf == 0) & (z == 0))
    def _():
        for dz in range(1, n_z):
            remote(0, dz * n_x * n_y + y * n_x + x, send_z.at[dz]).wait_send()

    @pl.when(source)
    def _():
        for dy in range(1, n_y):
            remote(0, dy * n_x + x, send_y.at[dy]).wait_send()


def broadcast_pivot(top, dims):
    rows, cols = top.shape
    n_src = S // cols
    return pl.pallas_call(
        functools.partial(pivot_kernel, dims),
        out_shape=jax.ShapeDtypeStruct((n_src, rows, cols), jnp.float32),
        in_specs=[pl.BlockSpec(memory_space=pltpu.VMEM)],
        out_specs=pl.BlockSpec(memory_space=pltpu.VMEM),
        scratch_shapes=[
            pltpu.SemaphoreType.DMA,
            pltpu.SemaphoreType.DMA((n_src,)),
            pltpu.SemaphoreType.DMA((dims[1],)),
            pltpu.SemaphoreType.DMA((dims[0],)),
            pltpu.SemaphoreType.DMA,
            pltpu.SemaphoreType.DMA((n_src,)),
        ],
        compiler_params=pltpu.CompilerParams(has_side_effects=True),
    )(top)


PANEL = 8


def _mm(a, b):
    return jnp.dot(a, b, precision=HIGHEST, preferred_element_type=jnp.float32)


def _mm_t(a, b):
    return lax.dot_general(a, b, (((1,), (1,)), ((), ())), precision=HIGHEST,
                           preferred_element_type=jnp.float32)


def chol_inv_kernel(a_ref, l_ref, linv_ref, w_ref, d_ref, e_ref, ut_ref, x_ref):
    n = w_ref.shape[0]
    b = d_ref.shape[0]
    nb = n // b
    lane = lax.broadcasted_iota(jnp.int32, (PANEL, b), 1)
    sub = lax.broadcasted_iota(jnp.int32, (PANEL, 1), 0)
    eye = (lax.broadcasted_iota(jnp.int32, (b, b), 0) == lax.broadcasted_iota(jnp.int32, (b, b), 1)).astype(jnp.float32)
    n_cb, _, cols = a_ref.shape
    for c in range(n_cb):
        w_ref[:, c * cols:(c + 1) * cols] = a_ref[c]
    l_ref[...] = jnp.zeros_like(l_ref)
    linv_ref[...] = jnp.zeros_like(linv_ref)

    def panel(p, carry):
        k = pl.multiple_of(p * PANEL, PANEL)
        r = d_ref[pl.ds(k, PANEL), :]
        e = e_ref[pl.ds(k, PANEL), :]
        for t in range(PANEL):
            c = k + t
            at_c = lane == c
            colv = jnp.sum(jnp.where(at_c, r, 0.0), axis=1, keepdims=True)
            piv = jnp.sum(jnp.where(at_c[t:t + 1], r[t:t + 1], 0.0), axis=1, keepdims=True)
            scale = 1.0 / jnp.sqrt(piv)
            urow = jnp.where(lane[t:t + 1] >= c, r[t:t + 1] * scale, 0.0)
            f = jnp.where(sub > t, colv * scale, 0.0)
            r = jnp.where(sub == t, urow, r - f * urow)
            xrow = e[t:t + 1] * scale
            e = jnp.where(sub == t, xrow, e - f * xrow)
        ut_ref[pl.ds(k, PANEL), :] = r
        x_ref[pl.ds(k, PANEL), :] = e
        rt = jnp.transpose(r)
        dd = d_ref[...]
        ee = e_ref[...]
        for t in range(PANEL):
            lcol = rt[:, t:t + 1]
            dd = dd - lcol * r[t:t + 1]
            ee = ee - lcol * e[t:t + 1]
        d_ref[...] = dd
        e_ref[...] = ee
        return carry

    for j in range(nb):
        jb = j * b
        d_ref[...] = w_ref[jb:jb + b, jb:jb + b]
        e_ref[...] = eye
        lax.fori_loop(0, b // PANEL, panel, 0)
        l_ref[jb:jb + b, jb:jb + b] = jnp.transpose(ut_ref[...])
        linv_ref[jb:jb + b, jb:jb + b] = x_ref[...]
        if j < nb - 1:
            lp = _mm_t(w_ref[jb + b:, jb:jb + b], x_ref[...])
            l_ref[jb + b:, jb:jb + b] = lp
            w_ref[jb + b:, jb + b:] = w_ref[jb + b:, jb + b:] - _mm_t(lp, lp)
    for j in range(nb):
        for i in range(j + 1, nb):
            acc = jnp.zeros((b, b), jnp.float32)
            for k in range(j, i):
                acc = acc + _mm(l_ref[i * b:(i + 1) * b, k * b:(k + 1) * b], linv_ref[k * b:(k + 1) * b, j * b:(j + 1) * b])
            linv_ref[i * b:(i + 1) * b, j * b:(j + 1) * b] = -_mm(linv_ref[i * b:(i + 1) * b, i * b:(i + 1) * b], acc)


def chol_inv(a, n, b=128):
    return pl.pallas_call(
        chol_inv_kernel,
        out_shape=(jax.ShapeDtypeStruct((n, n), jnp.float32), jax.ShapeDtypeStruct((n, n), jnp.float32)),
        in_specs=[pl.BlockSpec(memory_space=pltpu.VMEM)],
        out_specs=(pl.BlockSpec(memory_space=pltpu.VMEM), pl.BlockSpec(memory_space=pltpu.VMEM)),
        scratch_shapes=[
            pltpu.VMEM((n, n), jnp.float32),
            pltpu.VMEM((b, b), jnp.float32),
            pltpu.VMEM((b, b), jnp.float32),
            pltpu.VMEM((b, b), jnp.float32),
            pltpu.VMEM((b, b), jnp.float32),
        ],
    )(a)


def per_device(front_block, child_update, child_map):
    rows, cols = front_block.shape
    n_leaf = lax.axis_size("leaf")
    n_front = lax.axis_size("front")
    leaf = lax.axis_index("leaf")
    front = lax.axis_index("front")
    half_blocks = rows // BLK

    blocks = child_update[0].reshape(-1, BLK, cols)
    cmap = child_map[0]
    own = gather_half(blocks, cmap, leaf, half_blocks)
    send = gather_half(blocks, cmap, 1 - leaf, half_blocks)
    recv = lax.ppermute(send, "leaf", [(0, 1), (1, 0)])
    first = jnp.where(leaf == 0, own, recv)
    second = jnp.where(leaf == 0, recv, own)
    assembled = front_block + first + second

    top = assembled[:S]
    panel_rows = top.T

    n_parts = 2
    piece = rows // (n_parts * n_front)
    per_block = BLK // piece
    blocks_per_part = half_blocks // n_parts

    def part_piece(h):
        received = []
        for q in range(per_block):
            pairs = []
            for lf in range(n_leaf):
                for k in range(blocks_per_part):
                    pairs.append((lf * half_blocks + h * blocks_per_part + k, lf * n_front + per_block * k + q))
            received.append(lax.ppermute(panel_rows[q * piece:(q + 1) * piece], ("leaf", "front"), pairs))
        mine = received[0]
        for q in range(1, per_block):
            mine = jnp.where(front % per_block == q, received[q], mine)
        return mine

    first_part = lax.all_gather(part_piece(0), "front", tiled=True)
    pivot = broadcast_pivot(top, (4, 4, 4))
    second_piece, pivot = lax.optimization_barrier((part_piece(1), pivot))
    second_part = lax.all_gather(second_piece, "front", tiled=True)
    parts = (first_part, second_part)
    partner_rows = lax.ppermute(panel_rows, "leaf", [(0, 1)])
    col_rows = jnp.where(leaf == 0, panel_rows, partner_rows)

    factor, inverse = chol_inv(pivot, S)

    col_solved = lax.dot_general(col_rows, inverse, (((1,), (1,)), ((), ())), precision=HIGHEST)

    piv_cols = S // cols
    col_at = jnp.minimum(front, piv_cols - 1) * cols

    def pivot_columns():
        inv_rows = lax.dynamic_slice_in_dim(inverse, col_at, cols, 0)
        out = jnp.concatenate(
            [lax.dot_general(part, inv_rows, (((1,), (1,)), ((), ())), precision=HIGHEST) for part in parts], axis=0
        )
        top_rows = jnp.where(leaf == 0, lax.dynamic_slice_in_dim(factor, col_at, cols, 1), out[:S])
        return lax.dynamic_update_slice_in_dim(out, top_rows, 0, 0)

    def other_columns():
        weights = jnp.dot(col_solved, inverse, precision=HIGHEST).T
        out = assembled - jnp.concatenate([jnp.dot(part, weights, precision=HIGHEST) for part in parts], axis=0)
        top_rows = jnp.where(leaf == 0, col_solved.T, out[:S])
        return lax.dynamic_update_slice_in_dim(out, top_rows, 0, 0)

    return lax.cond(front < piv_cols, pivot_columns, other_columns)


def solution(mesh):
    return jax.shard_map(
        per_device,
        mesh=mesh,
        in_specs=(P("leaf", "front"), P("leaf", None, "front"), P("leaf", None)),
        out_specs=P("leaf", "front"),
        check_vma=False,
    )
```

```python
import functools

import jax
import jax.numpy as jnp
from jax import lax
from jax.experimental import pallas as pl
from jax.experimental.pallas import tpu as pltpu
from jax.sharding import PartitionSpec as P

BLK = 128
S = 512
HIGHEST = lax.Precision.HIGHEST
MESH = pl.DeviceIdType.MESH


def gather_half(blocks, child_map, half, half_blocks):
    parent = half * half_blocks + jnp.arange(half_blocks, dtype=jnp.int32)
    hit = child_map[None, :] == parent[:, None]
    found = jnp.any(hit, axis=1)
    index = jnp.argmax(hit, axis=1)
    picked = jnp.take(blocks, index, axis=0)
    picked = jnp.where(found[:, None, None], picked, jnp.zeros_like(picked))
    return picked.reshape(half_blocks * BLK, blocks.shape[2])


def pivot_kernel(n_front, n_src, top_ref, out_ref, chunk, sem_a, sem_b, send_a, send_b, recv_g, send_g):
    leaf = lax.axis_index("leaf")
    me = lax.axis_index("front")
    per_src = n_front // n_src
    rows = chunk.shape[0]

    @pl.when((leaf == 0) & (me < n_src))
    def _():
        for k in range(per_src):
            src = top_ref.at[pl.ds(k * rows, rows)]
            dst = me * per_src + k
            if k == 0:
                @pl.when(me == 0)
                def _():
                    pltpu.make_async_copy(src, chunk, sem_a).start()

                @pl.when(me != 0)
                def _():
                    pltpu.make_async_remote_copy(
                        src, chunk, send_a.at[k], sem_a, device_id=(0, dst), device_id_type=MESH
                    ).start()
            else:
                pltpu.make_async_remote_copy(
                    src, chunk, send_a.at[k], sem_a, device_id=(0, dst), device_id_type=MESH
                ).start()

    @pl.when((leaf == 0) & (me == 0))
    def _():
        pltpu.make_async_copy(top_ref.at[pl.ds(0, rows)], chunk, sem_a).wait()

    @pl.when((leaf == 0) & (me != 0))
    def _():
        pltpu.make_async_remote_copy(
            top_ref.at[pl.ds(0, rows)], chunk, send_a.at[0], sem_a, device_id=(0, me), device_id_type=MESH
        ).wait_recv()

    @pl.when(leaf == 0)
    def _():
        pltpu.make_async_remote_copy(
            chunk, chunk, send_b, sem_b, device_id=(1, me), device_id_type=MESH
        ).start()

    @pl.when(leaf == 1)
    def _():
        pltpu.make_async_remote_copy(
            chunk, chunk, send_b, sem_b, device_id=(0, me), device_id_type=MESH
        ).wait_recv()

    pltpu.make_async_copy(chunk, out_ref.at[me], recv_g.at[me]).start()

    def send(j, carry):
        dst = lax.rem(me + j, n_front)
        pltpu.make_async_remote_copy(
            chunk, out_ref.at[me], send_g.at[j], recv_g.at[me], device_id=(leaf, dst), device_id_type=MESH
        ).start()
        return carry

    lax.fori_loop(1, n_front, send, 0)

    pltpu.make_async_copy(chunk, out_ref.at[me], recv_g.at[me]).wait()

    def receive(j, carry):
        src = lax.rem(me + j, n_front)
        pltpu.make_async_remote_copy(
            chunk, out_ref.at[src], send_g.at[j], recv_g.at[src], device_id=(leaf, src), device_id_type=MESH
        ).wait_recv()
        return carry

    lax.fori_loop(1, n_front, receive, 0)

    def sent(j, carry):
        dst = lax.rem(me + j, n_front)
        pltpu.make_async_remote_copy(
            chunk, out_ref.at[me], send_g.at[j], recv_g.at[me], device_id=(leaf, dst), device_id_type=MESH
        ).wait_send()
        return carry

    lax.fori_loop(1, n_front, sent, 0)

    @pl.when(leaf == 0)
    def _():
        pltpu.make_async_remote_copy(
            chunk, chunk, send_b, sem_b, device_id=(1, me), device_id_type=MESH
        ).wait_send()

    @pl.when((leaf == 0) & (me < n_src))
    def _():
        for k in range(per_src):
            src = top_ref.at[pl.ds(k * rows, rows)]
            dst = me * per_src + k
            if k == 0:
                @pl.when(me != 0)
                def _():
                    pltpu.make_async_remote_copy(
                        src, chunk, send_a.at[k], sem_a, device_id=(0, dst), device_id_type=MESH
                    ).wait_send()
            else:
                pltpu.make_async_remote_copy(
                    src, chunk, send_a.at[k], sem_a, device_id=(0, dst), device_id_type=MESH
                ).wait_send()


def broadcast_pivot(top, n_front):
    cols = top.shape[1]
    n_src = S // cols
    per_src = n_front // n_src
    rows = S // per_src
    gathered = pl.pallas_call(
        functools.partial(pivot_kernel, n_front, n_src),
        out_shape=jax.ShapeDtypeStruct((n_front, rows, cols), jnp.float32),
        in_specs=[pl.BlockSpec(memory_space=pltpu.VMEM)],
        out_specs=pl.BlockSpec(memory_space=pltpu.VMEM),
        scratch_shapes=[
            pltpu.VMEM((rows, cols), jnp.float32),
            pltpu.SemaphoreType.DMA,
            pltpu.SemaphoreType.DMA,
            pltpu.SemaphoreType.DMA((per_src,)),
            pltpu.SemaphoreType.DMA,
            pltpu.SemaphoreType.DMA((n_front,)),
            pltpu.SemaphoreType.DMA((n_front,)),
        ],
        compiler_params=pltpu.CompilerParams(has_side_effects=True),
    )(top)
    return gathered.reshape(n_src, per_src, rows, cols).transpose(1, 2, 0, 3).reshape(S, S)


PANEL = 8


def _mm(a, b):
    return jnp.dot(a, b, precision=HIGHEST, preferred_element_type=jnp.float32)


def _mm_t(a, b):
    return lax.dot_general(a, b, (((1,), (1,)), ((), ())), precision=HIGHEST,
                           preferred_element_type=jnp.float32)


def chol_inv_kernel(a_ref, l_ref, linvt_ref, w_ref, d_ref, e_ref, ut_ref, x_ref, linv_ref):
    n = a_ref.shape[0]
    b = d_ref.shape[0]
    nb = n // b
    lane = lax.broadcasted_iota(jnp.int32, (PANEL, b), 1)
    sub = lax.broadcasted_iota(jnp.int32, (PANEL, 1), 0)
    eye = (lax.broadcasted_iota(jnp.int32, (b, b), 0) == lax.broadcasted_iota(jnp.int32, (b, b), 1)).astype(jnp.float32)
    w_ref[...] = a_ref[...]
    l_ref[...] = jnp.zeros_like(l_ref)
    linv_ref[...] = jnp.zeros_like(linv_ref)

    def panel(p, carry):
        k = pl.multiple_of(p * PANEL, PANEL)
        r = d_ref[pl.ds(k, PANEL), :]
        e = e_ref[pl.ds(k, PANEL), :]
        for t in range(PANEL):
            c = k + t
            at_c = lane == c
            colv = jnp.sum(jnp.where(at_c, r, 0.0), axis=1, keepdims=True)
            piv = jnp.sum(jnp.where(at_c[t:t + 1], r[t:t + 1], 0.0), axis=1, keepdims=True)
            scale = 1.0 / jnp.sqrt(piv)
            urow = jnp.where(lane[t:t + 1] >= c, r[t:t + 1] * scale, 0.0)
            f = jnp.where(sub > t, colv * scale, 0.0)
            r = jnp.where(sub == t, urow, r - f * urow)
            xrow = e[t:t + 1] * scale
            e = jnp.where(sub == t, xrow, e - f * xrow)
        ut_ref[pl.ds(k, PANEL), :] = r
        x_ref[pl.ds(k, PANEL), :] = e
        rt = jnp.transpose(r)
        dd = d_ref[...]
        ee = e_ref[...]
        for t in range(PANEL):
            lcol = rt[:, t:t + 1]
            dd = dd - lcol * r[t:t + 1]
            ee = ee - lcol * e[t:t + 1]
        d_ref[...] = dd
        e_ref[...] = ee
        return carry

    for j in range(nb):
        jb = j * b
        d_ref[...] = w_ref[jb:jb + b, jb:jb + b]
        e_ref[...] = eye
        lax.fori_loop(0, b // PANEL, panel, 0)
        l_ref[jb:jb + b, jb:jb + b] = jnp.transpose(ut_ref[...])
        linv_ref[jb:jb + b, jb:jb + b] = x_ref[...]
        if j < nb - 1:
            lp = _mm_t(w_ref[jb + b:, jb:jb + b], x_ref[...])
            l_ref[jb + b:, jb:jb + b] = lp
            w_ref[jb + b:, jb + b:] = w_ref[jb + b:, jb + b:] - _mm_t(lp, lp)
    for j in range(nb):
        for i in range(j + 1, nb):
            acc = jnp.zeros((b, b), jnp.float32)
            for k in range(j, i):
                acc = acc + _mm(l_ref[i * b:(i + 1) * b, k * b:(k + 1) * b], linv_ref[k * b:(k + 1) * b, j * b:(j + 1) * b])
            linv_ref[i * b:(i + 1) * b, j * b:(j + 1) * b] = -_mm(linv_ref[i * b:(i + 1) * b, i * b:(i + 1) * b], acc)
    for j in range(nb):
        for i in range(nb):
            linvt_ref[j * b:(j + 1) * b, i * b:(i + 1) * b] = jnp.transpose(linv_ref[i * b:(i + 1) * b, j * b:(j + 1) * b])


def chol_inv(a, b=128):
    n = a.shape[0]
    return pl.pallas_call(
        chol_inv_kernel,
        out_shape=(jax.ShapeDtypeStruct((n, n), jnp.float32), jax.ShapeDtypeStruct((n, n), jnp.float32)),
        in_specs=[pl.BlockSpec(memory_space=pltpu.VMEM)],
        out_specs=(pl.BlockSpec(memory_space=pltpu.VMEM), pl.BlockSpec(memory_space=pltpu.VMEM)),
        scratch_shapes=[
            pltpu.VMEM((n, n), jnp.float32),
            pltpu.VMEM((b, b), jnp.float32),
            pltpu.VMEM((b, b), jnp.float32),
            pltpu.VMEM((b, b), jnp.float32),
            pltpu.VMEM((b, b), jnp.float32),
            pltpu.VMEM((n, n), jnp.float32),
        ],
    )(a)


def per_device(front_block, child_update, child_map):
    rows, cols = front_block.shape
    n_leaf = lax.axis_size("leaf")
    n_front = lax.axis_size("front")
    leaf = lax.axis_index("leaf")
    front = lax.axis_index("front")
    half_blocks = rows // BLK

    blocks = child_update[0].reshape(-1, BLK, cols)
    cmap = child_map[0]
    own = gather_half(blocks, cmap, leaf, half_blocks)
    send = gather_half(blocks, cmap, 1 - leaf, half_blocks)
    recv = lax.ppermute(send, "leaf", [(0, 1), (1, 0)])
    first = jnp.where(leaf == 0, own, recv)
    second = jnp.where(leaf == 0, recv, own)
    assembled = front_block + first + second

    top = assembled[:S]
    panel_rows = top.T

    piece = rows // n_front
    per_block = BLK // piece
    pieces = []
    for part in range(per_block):
        pairs = []
        for lf in range(n_leaf):
            for k in range(n_front // per_block):
                src = lf * half_blocks + k
                dst = lf * n_front + per_block * k + part
                pairs.append((src, dst))
        pieces.append(lax.ppermute(panel_rows[part * piece:(part + 1) * piece], ("leaf", "front"), pairs))
    my_piece = pieces[0]
    for part in range(1, per_block):
        my_piece = jnp.where(front % per_block == part, pieces[part], my_piece)
    pivot = broadcast_pivot(top, n_front)
    partner_rows = lax.ppermute(panel_rows, "leaf", [(0, 1)])
    col_rows = jnp.where(leaf == 0, panel_rows, partner_rows)
    my_piece, pivot = lax.optimization_barrier((my_piece, pivot))
    panel = lax.all_gather(my_piece, "front", tiled=True)
    factor, inverse_t = chol_inv(pivot)

    col_solved = jnp.dot(col_rows, inverse_t, precision=HIGHEST)

    piv_cols = S // cols
    col_at = jnp.minimum(front, piv_cols - 1) * cols

    def pivot_columns():
        inv_cols = lax.dynamic_slice_in_dim(inverse_t, col_at, cols, 1)
        out = jnp.dot(panel, inv_cols, precision=HIGHEST)
        top_rows = jnp.where(leaf == 0, lax.dynamic_slice_in_dim(factor, col_at, cols, 1), out[:S])
        return lax.dynamic_update_slice_in_dim(out, top_rows, 0, 0)

    def other_columns():
        weights = lax.dot_general(inverse_t, col_solved, (((1,), (1,)), ((), ())), precision=HIGHEST)
        out = assembled - jnp.dot(panel, weights, precision=HIGHEST)
        top_rows = jnp.where(leaf == 0, col_solved.T, out[:S])
        return lax.dynamic_update_slice_in_dim(out, top_rows, 0, 0)

    return lax.cond(front < piv_cols, pivot_columns, other_columns)


def solution(mesh):
    return jax.shard_map(
        per_device,
        mesh=mesh,
        in_specs=(P("leaf", "front"), P("leaf", None, "front"), P("leaf", None)),
        out_specs=P("leaf", "front"),
        check_vma=False,
    )
```

```python
import functools

import jax
import jax.numpy as jnp
from jax import lax
from jax.experimental import pallas as pl
from jax.experimental.pallas import tpu as pltpu
from jax.sharding import PartitionSpec as P

BLK = 128
S = 512
HIGHEST = lax.Precision.HIGHEST
MESH = pl.DeviceIdType.MESH


def gather_half(blocks, child_map, half, half_blocks):
    parent = half * half_blocks + jnp.arange(half_blocks, dtype=jnp.int32)
    hit = child_map[None, :] == parent[:, None]
    found = jnp.any(hit, axis=1)
    index = jnp.argmax(hit, axis=1)
    picked = jnp.take(blocks, index, axis=0)
    picked = jnp.where(found[:, None, None], picked, jnp.zeros_like(picked))
    return picked.reshape(half_blocks * BLK, blocks.shape[2])


def pivot_kernel(n_front, n_src, top_ref, out_ref, chunk, sem_a, sem_b, send_a, send_b, recv_g, send_g):
    leaf = lax.axis_index("leaf")
    me = lax.axis_index("front")
    per_src = n_front // n_src
    rows = chunk.shape[0]

    @pl.when((leaf == 0) & (me < n_src))
    def _():
        for k in range(per_src):
            src = top_ref.at[pl.ds(k * rows, rows)]
            dst = me * per_src + k
            if k == 0:
                @pl.when(me == 0)
                def _():
                    pltpu.make_async_copy(src, chunk, sem_a).start()

                @pl.when(me != 0)
                def _():
                    pltpu.make_async_remote_copy(
                        src, chunk, send_a.at[k], sem_a, device_id=(0, dst), device_id_type=MESH
                    ).start()
            else:
                pltpu.make_async_remote_copy(
                    src, chunk, send_a.at[k], sem_a, device_id=(0, dst), device_id_type=MESH
                ).start()

    @pl.when((leaf == 0) & (me == 0))
    def _():
        pltpu.make_async_copy(top_ref.at[pl.ds(0, rows)], chunk, sem_a).wait()

    @pl.when((leaf == 0) & (me != 0))
    def _():
        pltpu.make_async_remote_copy(
            top_ref.at[pl.ds(0, rows)], chunk, send_a.at[0], sem_a, device_id=(0, me), device_id_type=MESH
        ).wait_recv()

    @pl.when(leaf == 0)
    def _():
        pltpu.make_async_remote_copy(
            chunk, chunk, send_b, sem_b, device_id=(1, me), device_id_type=MESH
        ).start()

    @pl.when(leaf == 1)
    def _():
        pltpu.make_async_remote_copy(
            chunk, chunk, send_b, sem_b, device_id=(0, me), device_id_type=MESH
        ).wait_recv()

    pltpu.make_async_copy(chunk, out_ref.at[me], recv_g.at[me]).start()

    def send(j, carry):
        dst = lax.rem(me + j, n_front)
        pltpu.make_async_remote_copy(
            chunk, out_ref.at[me], send_g.at[j], recv_g.at[me], device_id=(leaf, dst), device_id_type=MESH
        ).start()
        return carry

    lax.fori_loop(1, n_front, send, 0)

    pltpu.make_async_copy(chunk, out_ref.at[me], recv_g.at[me]).wait()

    def receive(j, carry):
        src = lax.rem(me + j, n_front)
        pltpu.make_async_remote_copy(
            chunk, out_ref.at[src], send_g.at[j], recv_g.at[src], device_id=(leaf, src), device_id_type=MESH
        ).wait_recv()
        return carry

    lax.fori_loop(1, n_front, receive, 0)

    def sent(j, carry):
        dst = lax.rem(me + j, n_front)
        pltpu.make_async_remote_copy(
            chunk, out_ref.at[me], send_g.at[j], recv_g.at[me], device_id=(leaf, dst), device_id_type=MESH
        ).wait_send()
        return carry

    lax.fori_loop(1, n_front, sent, 0)

    @pl.when(leaf == 0)
    def _():
        pltpu.make_async_remote_copy(
            chunk, chunk, send_b, sem_b, device_id=(1, me), device_id_type=MESH
        ).wait_send()

    @pl.when((leaf == 0) & (me < n_src))
    def _():
        for k in range(per_src):
            src = top_ref.at[pl.ds(k * rows, rows)]
            dst = me * per_src + k
            if k == 0:
                @pl.when(me != 0)
                def _():
                    pltpu.make_async_remote_copy(
                        src, chunk, send_a.at[k], sem_a, device_id=(0, dst), device_id_type=MESH
                    ).wait_send()
            else:
                pltpu.make_async_remote_copy(
                    src, chunk, send_a.at[k], sem_a, device_id=(0, dst), device_id_type=MESH
                ).wait_send()


def broadcast_pivot(top, n_front):
    cols = top.shape[1]
    n_src = S // cols
    per_src = n_front // n_src
    rows = S // per_src
    gathered = pl.pallas_call(
        functools.partial(pivot_kernel, n_front, n_src),
        out_shape=jax.ShapeDtypeStruct((n_front, rows, cols), jnp.float32),
        in_specs=[pl.BlockSpec(memory_space=pltpu.VMEM)],
        out_specs=pl.BlockSpec(memory_space=pltpu.VMEM),
        scratch_shapes=[
            pltpu.VMEM((rows, cols), jnp.float32),
            pltpu.SemaphoreType.DMA,
            pltpu.SemaphoreType.DMA,
            pltpu.SemaphoreType.DMA((per_src,)),
            pltpu.SemaphoreType.DMA,
            pltpu.SemaphoreType.DMA((n_front,)),
            pltpu.SemaphoreType.DMA((n_front,)),
        ],
        compiler_params=pltpu.CompilerParams(has_side_effects=True),
    )(top)
    return gathered.reshape(n_src, per_src, rows, cols).transpose(1, 2, 0, 3).reshape(S, S)


PANEL = 8


def _mm(a, b):
    return jnp.dot(a, b, precision=HIGHEST, preferred_element_type=jnp.float32)


def _mm_t(a, b):
    return lax.dot_general(a, b, (((1,), (1,)), ((), ())), precision=HIGHEST,
                           preferred_element_type=jnp.float32)


def chol_inv_kernel(a_ref, l_ref, linv_ref, w_ref, d_ref, e_ref, ut_ref, x_ref):
    n = a_ref.shape[0]
    b = d_ref.shape[0]
    nb = n // b
    lane = lax.broadcasted_iota(jnp.int32, (PANEL, b), 1)
    sub = lax.broadcasted_iota(jnp.int32, (PANEL, 1), 0)
    eye = (lax.broadcasted_iota(jnp.int32, (b, b), 0) == lax.broadcasted_iota(jnp.int32, (b, b), 1)).astype(jnp.float32)
    w_ref[...] = a_ref[...]
    l_ref[...] = jnp.zeros_like(l_ref)
    linv_ref[...] = jnp.zeros_like(linv_ref)

    def panel(p, carry):
        k = pl.multiple_of(p * PANEL, PANEL)
        r = d_ref[pl.ds(k, PANEL), :]
        e = e_ref[pl.ds(k, PANEL), :]
        for t in range(PANEL):
            c = k + t
            at_c = lane == c
            colv = jnp.sum(jnp.where(at_c, r, 0.0), axis=1, keepdims=True)
            piv = jnp.sum(jnp.where(at_c[t:t + 1], r[t:t + 1], 0.0), axis=1, keepdims=True)
            scale = 1.0 / jnp.sqrt(piv)
            urow = jnp.where(lane[t:t + 1] >= c, r[t:t + 1] * scale, 0.0)
            f = jnp.where(sub > t, colv * scale, 0.0)
            r = jnp.where(sub == t, urow, r - f * urow)
            xrow = e[t:t + 1] * scale
            e = jnp.where(sub == t, xrow, e - f * xrow)
        ut_ref[pl.ds(k, PANEL), :] = r
        x_ref[pl.ds(k, PANEL), :] = e
        rt = jnp.transpose(r)
        dd = d_ref[...]
        ee = e_ref[...]
        for t in range(PANEL):
            lcol = rt[:, t:t + 1]
            dd = dd - lcol * r[t:t + 1]
            ee = ee - lcol * e[t:t + 1]
        d_ref[...] = dd
        e_ref[...] = ee
        return carry

    for j in range(nb):
        jb = j * b
        d_ref[...] = w_ref[jb:jb + b, jb:jb + b]
        e_ref[...] = eye
        lax.fori_loop(0, b // PANEL, panel, 0)
        l_ref[jb:jb + b, jb:jb + b] = jnp.transpose(ut_ref[...])
        linv_ref[jb:jb + b, jb:jb + b] = x_ref[...]
        if j < nb - 1:
            lp = _mm_t(w_ref[jb + b:, jb:jb + b], x_ref[...])
            l_ref[jb + b:, jb:jb + b] = lp
            w_ref[jb + b:, jb + b:] = w_ref[jb + b:, jb + b:] - _mm_t(lp, lp)
    for j in range(nb):
        for i in range(j + 1, nb):
            acc = jnp.zeros((b, b), jnp.float32)
            for k in range(j, i):
                acc = acc + _mm(l_ref[i * b:(i + 1) * b, k * b:(k + 1) * b], linv_ref[k * b:(k + 1) * b, j * b:(j + 1) * b])
            linv_ref[i * b:(i + 1) * b, j * b:(j + 1) * b] = -_mm(linv_ref[i * b:(i + 1) * b, i * b:(i + 1) * b], acc)


def chol_inv(a, b=128):
    n = a.shape[0]
    return pl.pallas_call(
        chol_inv_kernel,
        out_shape=(jax.ShapeDtypeStruct((n, n), jnp.float32), jax.ShapeDtypeStruct((n, n), jnp.float32)),
        in_specs=[pl.BlockSpec(memory_space=pltpu.VMEM)],
        out_specs=(pl.BlockSpec(memory_space=pltpu.VMEM), pl.BlockSpec(memory_space=pltpu.VMEM)),
        scratch_shapes=[
            pltpu.VMEM((n, n), jnp.float32),
            pltpu.VMEM((b, b), jnp.float32),
            pltpu.VMEM((b, b), jnp.float32),
            pltpu.VMEM((b, b), jnp.float32),
            pltpu.VMEM((b, b), jnp.float32),
        ],
    )(a)


def panel_product_kernel(subtract, use_top_ref, panel_ref, w_ref, base_ref, top_ref, out_ref):
    prod = jnp.dot(panel_ref[...], w_ref[...], precision=HIGHEST, preferred_element_type=jnp.float32)
    result = base_ref[...] - prod if subtract else prod
    replace = (pl.program_id(0) == 0) & (use_top_ref[0] == 1)
    out_ref[...] = jnp.where(replace, top_ref[...], result)


def panel_product(use_top, panel, weights, base, top_rows, subtract):
    rows, depth = panel.shape
    cols = weights.shape[1]
    return pl.pallas_call(
        functools.partial(panel_product_kernel, subtract),
        out_shape=jax.ShapeDtypeStruct((rows, cols), jnp.float32),
        grid_spec=pltpu.PrefetchScalarGridSpec(
            num_scalar_prefetch=1,
            grid=(rows // S,),
            in_specs=[
                pl.BlockSpec((S, depth), lambda i, flag: (i, 0)),
                pl.BlockSpec((depth, cols), lambda i, flag: (0, 0)),
                pl.BlockSpec((S, cols), lambda i, flag: (i, 0)),
                pl.BlockSpec((S, cols), lambda i, flag: (0, 0)),
            ],
            out_specs=pl.BlockSpec((S, cols), lambda i, flag: (i, 0)),
        ),
    )(use_top, panel, weights, base, top_rows)


def per_device(front_block, child_update, child_map):
    rows, cols = front_block.shape
    n_leaf = lax.axis_size("leaf")
    n_front = lax.axis_size("front")
    leaf = lax.axis_index("leaf")
    front = lax.axis_index("front")
    half_blocks = rows // BLK

    blocks = child_update[0].reshape(-1, BLK, cols)
    cmap = child_map[0]
    own = gather_half(blocks, cmap, leaf, half_blocks)
    send = gather_half(blocks, cmap, 1 - leaf, half_blocks)
    recv = lax.ppermute(send, "leaf", [(0, 1), (1, 0)])
    first = jnp.where(leaf == 0, own, recv)
    second = jnp.where(leaf == 0, recv, own)
    assembled = front_block + first + second

    top = assembled[:S]
    panel_rows = top.T

    piece = rows // n_front
    per_block = BLK // piece
    pieces = []
    for part in range(per_block):
        pairs = []
        for lf in range(n_leaf):
            for k in range(n_front // per_block):
                src = lf * half_blocks + k
                dst = lf * n_front + per_block * k + part
                pairs.append((src, dst))
        pieces.append(lax.ppermute(panel_rows[part * piece:(part + 1) * piece], ("leaf", "front"), pairs))
    my_piece = pieces[0]
    for part in range(1, per_block):
        my_piece = jnp.where(front % per_block == part, pieces[part], my_piece)
    pivot = broadcast_pivot(top, n_front)
    partner_rows = lax.ppermute(panel_rows, "leaf", [(0, 1)])
    col_rows = jnp.where(leaf == 0, panel_rows, partner_rows)
    my_piece, pivot = lax.optimization_barrier((my_piece, pivot))
    panel = lax.all_gather(my_piece, "front", tiled=True)
    factor, inverse = chol_inv(pivot)

    col_solved = lax.dot_general(col_rows, inverse, (((1,), (1,)), ((), ())), precision=HIGHEST)

    piv_cols = S // cols
    col_at = jnp.minimum(front, piv_cols - 1) * cols

    use_top = (leaf == 0).astype(jnp.int32).reshape(1)

    def pivot_columns():
        inv_rows = lax.dynamic_slice_in_dim(inverse, col_at, cols, 0)
        top_rows = lax.dynamic_slice_in_dim(factor, col_at, cols, 1)
        return panel_product(use_top, panel, inv_rows.T, assembled, top_rows, False)

    def other_columns():
        weights = jnp.dot(col_solved, inverse, precision=HIGHEST).T
        return panel_product(use_top, panel, weights, assembled, col_solved.T, True)

    return lax.cond(front < piv_cols, pivot_columns, other_columns)


def solution(mesh):
    return jax.shard_map(
        per_device,
        mesh=mesh,
        in_specs=(P("leaf", "front"), P("leaf", None, "front"), P("leaf", None)),
        out_specs=P("leaf", "front"),
        check_vma=False,
    )
```

```python
import functools

import jax
import jax.numpy as jnp
from jax import lax
from jax.experimental import pallas as pl
from jax.experimental.pallas import tpu as pltpu
from jax.sharding import PartitionSpec as P

BLK = 128
S = 512
HIGHEST = lax.Precision.HIGHEST
MESH = pl.DeviceIdType.MESH


def gather_half(blocks, child_map, half, half_blocks):
    parent = half * half_blocks + jnp.arange(half_blocks, dtype=jnp.int32)
    hit = child_map[None, :] == parent[:, None]
    found = jnp.any(hit, axis=1)
    index = jnp.argmax(hit, axis=1)
    picked = jnp.take(blocks, index, axis=0)
    picked = jnp.where(found[:, None, None], picked, jnp.zeros_like(picked))
    return picked.reshape(half_blocks * BLK, blocks.shape[2])


def pivot_kernel(n_front, n_src, top_ref, out_ref, chunk, sem_a, sem_b, send_a, send_b, recv_g, send_g):
    leaf = lax.axis_index("leaf")
    me = lax.axis_index("front")
    per_src = n_front // n_src
    rows = chunk.shape[0]

    @pl.when((leaf == 0) & (me < n_src))
    def _():
        for k in range(per_src):
            src = top_ref.at[pl.ds(k * rows, rows)]
            dst = me * per_src + k
            if k == 0:
                @pl.when(me == 0)
                def _():
                    pltpu.make_async_copy(src, chunk, sem_a).start()

                @pl.when(me != 0)
                def _():
                    pltpu.make_async_remote_copy(
                        src, chunk, send_a.at[k], sem_a, device_id=(0, dst), device_id_type=MESH
                    ).start()
            else:
                pltpu.make_async_remote_copy(
                    src, chunk, send_a.at[k], sem_a, device_id=(0, dst), device_id_type=MESH
                ).start()

    @pl.when((leaf == 0) & (me == 0))
    def _():
        pltpu.make_async_copy(top_ref.at[pl.ds(0, rows)], chunk, sem_a).wait()

    @pl.when((leaf == 0) & (me != 0))
    def _():
        pltpu.make_async_remote_copy(
            top_ref.at[pl.ds(0, rows)], chunk, send_a.at[0], sem_a, device_id=(0, me), device_id_type=MESH
        ).wait_recv()

    @pl.when(leaf == 0)
    def _():
        pltpu.make_async_remote_copy(
            chunk, chunk, send_b, sem_b, device_id=(1, me), device_id_type=MESH
        ).start()

    @pl.when(leaf == 1)
    def _():
        pltpu.make_async_remote_copy(
            chunk, chunk, send_b, sem_b, device_id=(0, me), device_id_type=MESH
        ).wait_recv()

    pltpu.make_async_copy(chunk, out_ref.at[me], recv_g.at[me]).start()

    def send(j, carry):
        dst = lax.rem(me + j, n_front)
        pltpu.make_async_remote_copy(
            chunk, out_ref.at[me], send_g.at[j], recv_g.at[me], device_id=(leaf, dst), device_id_type=MESH
        ).start()
        return carry

    lax.fori_loop(1, n_front, send, 0)

    pltpu.make_async_copy(chunk, out_ref.at[me], recv_g.at[me]).wait()

    def receive(j, carry):
        src = lax.rem(me + j, n_front)
        pltpu.make_async_remote_copy(
            chunk, out_ref.at[src], send_g.at[j], recv_g.at[src], device_id=(leaf, src), device_id_type=MESH
        ).wait_recv()
        return carry

    lax.fori_loop(1, n_front, receive, 0)

    def sent(j, carry):
        dst = lax.rem(me + j, n_front)
        pltpu.make_async_remote_copy(
            chunk, out_ref.at[me], send_g.at[j], recv_g.at[me], device_id=(leaf, dst), device_id_type=MESH
        ).wait_send()
        return carry

    lax.fori_loop(1, n_front, sent, 0)

    @pl.when(leaf == 0)
    def _():
        pltpu.make_async_remote_copy(
            chunk, chunk, send_b, sem_b, device_id=(1, me), device_id_type=MESH
        ).wait_send()

    @pl.when((leaf == 0) & (me < n_src))
    def _():
        for k in range(per_src):
            src = top_ref.at[pl.ds(k * rows, rows)]
            dst = me * per_src + k
            if k == 0:
                @pl.when(me != 0)
                def _():
                    pltpu.make_async_remote_copy(
                        src, chunk, send_a.at[k], sem_a, device_id=(0, dst), device_id_type=MESH
                    ).wait_send()
            else:
                pltpu.make_async_remote_copy(
                    src, chunk, send_a.at[k], sem_a, device_id=(0, dst), device_id_type=MESH
                ).wait_send()


def broadcast_pivot(top, n_front):
    cols = top.shape[1]
    n_src = S // cols
    per_src = n_front // n_src
    rows = S // per_src
    gathered = pl.pallas_call(
        functools.partial(pivot_kernel, n_front, n_src),
        out_shape=jax.ShapeDtypeStruct((n_front, rows, cols), jnp.float32),
        in_specs=[pl.BlockSpec(memory_space=pltpu.VMEM)],
        out_specs=pl.BlockSpec(memory_space=pltpu.VMEM),
        scratch_shapes=[
            pltpu.VMEM((rows, cols), jnp.float32),
            pltpu.SemaphoreType.DMA,
            pltpu.SemaphoreType.DMA,
            pltpu.SemaphoreType.DMA((per_src,)),
            pltpu.SemaphoreType.DMA,
            pltpu.SemaphoreType.DMA((n_front,)),
            pltpu.SemaphoreType.DMA((n_front,)),
        ],
        compiler_params=pltpu.CompilerParams(has_side_effects=True),
    )(top)
    return gathered.reshape(n_src, per_src, rows, cols).transpose(1, 2, 0, 3).reshape(S, S)


PANEL = 8


def _mm(a, b):
    return jnp.dot(a, b, precision=HIGHEST, preferred_element_type=jnp.float32)


def _mm_t(a, b):
    return lax.dot_general(a, b, (((1,), (1,)), ((), ())), precision=HIGHEST,
                           preferred_element_type=jnp.float32)


def chol_inv_kernel(a_ref, c_ref, l_ref, linv_ref, cs_ref, wt_ref, w_ref, d_ref, e_ref, ut_ref, x_ref):
    n = a_ref.shape[0]
    b = d_ref.shape[0]
    nb = n // b
    lane = lax.broadcasted_iota(jnp.int32, (PANEL, b), 1)
    sub = lax.broadcasted_iota(jnp.int32, (PANEL, 1), 0)
    eye = (lax.broadcasted_iota(jnp.int32, (b, b), 0) == lax.broadcasted_iota(jnp.int32, (b, b), 1)).astype(jnp.float32)
    w_ref[...] = a_ref[...]
    l_ref[...] = jnp.zeros_like(l_ref)
    linv_ref[...] = jnp.zeros_like(linv_ref)

    def panel(p, carry):
        k = pl.multiple_of(p * PANEL, PANEL)
        r = d_ref[pl.ds(k, PANEL), :]
        e = e_ref[pl.ds(k, PANEL), :]
        for t in range(PANEL):
            c = k + t
            at_c = lane == c
            colv = jnp.sum(jnp.where(at_c, r, 0.0), axis=1, keepdims=True)
            piv = jnp.sum(jnp.where(at_c[t:t + 1], r[t:t + 1], 0.0), axis=1, keepdims=True)
            scale = 1.0 / jnp.sqrt(piv)
            urow = jnp.where(lane[t:t + 1] >= c, r[t:t + 1] * scale, 0.0)
            f = jnp.where(sub > t, colv * scale, 0.0)
            r = jnp.where(sub == t, urow, r - f * urow)
            xrow = e[t:t + 1] * scale
            e = jnp.where(sub == t, xrow, e - f * xrow)
        ut_ref[pl.ds(k, PANEL), :] = r
        x_ref[pl.ds(k, PANEL), :] = e
        rt = jnp.transpose(r)
        dd = d_ref[...]
        ee = e_ref[...]
        for t in range(PANEL):
            lcol = rt[:, t:t + 1]
            dd = dd - lcol * r[t:t + 1]
            ee = ee - lcol * e[t:t + 1]
        d_ref[...] = dd
        e_ref[...] = ee
        return carry

    for j in range(nb):
        jb = j * b
        d_ref[...] = w_ref[jb:jb + b, jb:jb + b]
        e_ref[...] = eye
        lax.fori_loop(0, b // PANEL, panel, 0)
        l_ref[jb:jb + b, jb:jb + b] = jnp.transpose(ut_ref[...])
        linv_ref[jb:jb + b, jb:jb + b] = x_ref[...]
        if j < nb - 1:
            lp = _mm_t(w_ref[jb + b:, jb:jb + b], x_ref[...])
            l_ref[jb + b:, jb:jb + b] = lp
            w_ref[jb + b:, jb + b:] = w_ref[jb + b:, jb + b:] - _mm_t(lp, lp)
    for j in range(nb):
        for i in range(j + 1, nb):
            acc = jnp.zeros((b, b), jnp.float32)
            for k in range(j, i):
                acc = acc + _mm(l_ref[i * b:(i + 1) * b, k * b:(k + 1) * b], linv_ref[k * b:(k + 1) * b, j * b:(j + 1) * b])
            linv_ref[i * b:(i + 1) * b, j * b:(j + 1) * b] = -_mm(linv_ref[i * b:(i + 1) * b, i * b:(i + 1) * b], acc)
    solved = _mm_t(c_ref[...], linv_ref[...])
    cs_ref[...] = solved
    wt_ref[...] = jnp.transpose(_mm(solved, linv_ref[...]))


def chol_inv(a, c, b=128):
    n = a.shape[0]
    m = c.shape[0]
    return pl.pallas_call(
        chol_inv_kernel,
        out_shape=(
            jax.ShapeDtypeStruct((n, n), jnp.float32),
            jax.ShapeDtypeStruct((n, n), jnp.float32),
            jax.ShapeDtypeStruct((m, n), jnp.float32),
            jax.ShapeDtypeStruct((n, m), jnp.float32),
        ),
        in_specs=[pl.BlockSpec(memory_space=pltpu.VMEM)] * 2,
        out_specs=tuple(pl.BlockSpec(memory_space=pltpu.VMEM) for _ in range(4)),
        scratch_shapes=[
            pltpu.VMEM((n, n), jnp.float32),
            pltpu.VMEM((b, b), jnp.float32),
            pltpu.VMEM((b, b), jnp.float32),
            pltpu.VMEM((b, b), jnp.float32),
            pltpu.VMEM((b, b), jnp.float32),
        ],
    )(a, c)


def panel_product_kernel(subtract, use_top_ref, panel_ref, w_ref, base_ref, top_ref, out_ref):
    prod = jnp.dot(panel_ref[...], w_ref[...], precision=HIGHEST, preferred_element_type=jnp.float32)
    result = base_ref[...] - prod if subtract else prod
    replace = (pl.program_id(0) == 0) & (use_top_ref[0] == 1)
    out_ref[...] = jnp.where(replace, top_ref[...], result)


def panel_product(use_top, panel, weights, base, top_rows, subtract):
    rows, depth = panel.shape
    cols = weights.shape[1]
    return pl.pallas_call(
        functools.partial(panel_product_kernel, subtract),
        out_shape=jax.ShapeDtypeStruct((rows, cols), jnp.float32),
        grid_spec=pltpu.PrefetchScalarGridSpec(
            num_scalar_prefetch=1,
            grid=(rows // S,),
            in_specs=[
                pl.BlockSpec((S, depth), lambda i, flag: (i, 0)),
                pl.BlockSpec((depth, cols), lambda i, flag: (0, 0)),
                pl.BlockSpec((S, cols), lambda i, flag: (i, 0)),
                pl.BlockSpec((S, cols), lambda i, flag: (0, 0)),
            ],
            out_specs=pl.BlockSpec((S, cols), lambda i, flag: (i, 0)),
        ),
    )(use_top, panel, weights, base, top_rows)


def per_device(front_block, child_update, child_map):
    rows, cols = front_block.shape
    n_leaf = lax.axis_size("leaf")
    n_front = lax.axis_size("front")
    leaf = lax.axis_index("leaf")
    front = lax.axis_index("front")
    half_blocks = rows // BLK

    blocks = child_update[0].reshape(-1, BLK, cols)
    cmap = child_map[0]
    own = gather_half(blocks, cmap, leaf, half_blocks)
    send = gather_half(blocks, cmap, 1 - leaf, half_blocks)
    recv = lax.ppermute(send, "leaf", [(0, 1), (1, 0)])
    first = jnp.where(leaf == 0, own, recv)
    second = jnp.where(leaf == 0, recv, own)
    assembled = front_block + first + second

    top = assembled[:S]
    panel_rows = top.T

    piece = rows // n_front
    per_block = BLK // piece
    pieces = []
    for part in range(per_block):
        pairs = []
        for lf in range(n_leaf):
            for k in range(n_front // per_block):
                src = lf * half_blocks + k
                dst = lf * n_front + per_block * k + part
                pairs.append((src, dst))
        pieces.append(lax.ppermute(panel_rows[part * piece:(part + 1) * piece], ("leaf", "front"), pairs))
    my_piece = pieces[0]
    for part in range(1, per_block):
        my_piece = jnp.where(front % per_block == part, pieces[part], my_piece)
    pivot = broadcast_pivot(top, n_front)
    partner_rows = lax.ppermute(panel_rows, "leaf", [(0, 1)])
    col_rows = jnp.where(leaf == 0, panel_rows, partner_rows)
    my_piece, pivot = lax.optimization_barrier((my_piece, pivot))
    panel = lax.all_gather(my_piece, "front", tiled=True)
    factor, inverse, col_solved, weights = chol_inv(pivot, col_rows)


    piv_cols = S // cols
    col_at = jnp.minimum(front, piv_cols - 1) * cols

    use_top = (leaf == 0).astype(jnp.int32).reshape(1)

    def pivot_columns():
        inv_rows = lax.dynamic_slice_in_dim(inverse, col_at, cols, 0)
        top_rows = lax.dynamic_slice_in_dim(factor, col_at, cols, 1)
        return panel_product(use_top, panel, inv_rows.T, assembled, top_rows, False)

    def other_columns():
        return panel_product(use_top, panel, weights, assembled, col_solved.T, True)

    return lax.cond(front < piv_cols, pivot_columns, other_columns)


def solution(mesh):
    return jax.shard_map(
        per_device,
        mesh=mesh,
        in_specs=(P("leaf", "front"), P("leaf", None, "front"), P("leaf", None)),
        out_specs=P("leaf", "front"),
        check_vma=False,
    )
```

```python
import functools

import jax
import jax.numpy as jnp
from jax import lax
from jax.experimental import pallas as pl
from jax.experimental.pallas import tpu as pltpu
from jax.sharding import PartitionSpec as P

BLK = 128
S = 512
HIGHEST = lax.Precision.HIGHEST
MESH = pl.DeviceIdType.MESH


def gather_half(blocks, child_map, half, half_blocks):
    parent = half * half_blocks + jnp.arange(half_blocks, dtype=jnp.int32)
    hit = child_map[None, :] == parent[:, None]
    found = jnp.any(hit, axis=1)
    index = jnp.argmax(hit, axis=1)
    picked = jnp.take(blocks, index, axis=0)
    picked = jnp.where(found[:, None, None], picked, jnp.zeros_like(picked))
    return picked.reshape(half_blocks * BLK, blocks.shape[2])


def pivot_kernel(n_front, n_src, top_ref, out_ref, chunk, sem_a, sem_b, send_a, send_b, recv_g, send_g):
    leaf = lax.axis_index("leaf")
    me = lax.axis_index("front")
    per_src = n_front // n_src
    rows = chunk.shape[0]

    @pl.when((leaf == 0) & (me < n_src))
    def _():
        for k in range(per_src):
            src = top_ref.at[pl.ds(k * rows, rows)]
            dst = me * per_src + k
            if k == 0:
                @pl.when(me == 0)
                def _():
                    pltpu.make_async_copy(src, chunk, sem_a).start()

                @pl.when(me != 0)
                def _():
                    pltpu.make_async_remote_copy(
                        src, chunk, send_a.at[k], sem_a, device_id=(0, dst), device_id_type=MESH
                    ).start()
            else:
                pltpu.make_async_remote_copy(
                    src, chunk, send_a.at[k], sem_a, device_id=(0, dst), device_id_type=MESH
                ).start()

    @pl.when((leaf == 0) & (me == 0))
    def _():
        pltpu.make_async_copy(top_ref.at[pl.ds(0, rows)], chunk, sem_a).wait()

    @pl.when((leaf == 0) & (me != 0))
    def _():
        pltpu.make_async_remote_copy(
            top_ref.at[pl.ds(0, rows)], chunk, send_a.at[0], sem_a, device_id=(0, me), device_id_type=MESH
        ).wait_recv()

    @pl.when(leaf == 0)
    def _():
        pltpu.make_async_remote_copy(
            chunk, chunk, send_b, sem_b, device_id=(1, me), device_id_type=MESH
        ).start()

    @pl.when(leaf == 1)
    def _():
        pltpu.make_async_remote_copy(
            chunk, chunk, send_b, sem_b, device_id=(0, me), device_id_type=MESH
        ).wait_recv()

    pltpu.make_async_copy(chunk, out_ref.at[me], recv_g.at[me]).start()

    def send(j, carry):
        dst = lax.rem(me + j, n_front)
        pltpu.make_async_remote_copy(
            chunk, out_ref.at[me], send_g.at[j], recv_g.at[me], device_id=(leaf, dst), device_id_type=MESH
        ).start()
        return carry

    lax.fori_loop(1, n_front, send, 0)

    pltpu.make_async_copy(chunk, out_ref.at[me], recv_g.at[me]).wait()

    def receive(j, carry):
        src = lax.rem(me + j, n_front)
        pltpu.make_async_remote_copy(
            chunk, out_ref.at[src], send_g.at[j], recv_g.at[src], device_id=(leaf, src), device_id_type=MESH
        ).wait_recv()
        return carry

    lax.fori_loop(1, n_front, receive, 0)

    def sent(j, carry):
        dst = lax.rem(me + j, n_front)
        pltpu.make_async_remote_copy(
            chunk, out_ref.at[me], send_g.at[j], recv_g.at[me], device_id=(leaf, dst), device_id_type=MESH
        ).wait_send()
        return carry

    lax.fori_loop(1, n_front, sent, 0)

    @pl.when(leaf == 0)
    def _():
        pltpu.make_async_remote_copy(
            chunk, chunk, send_b, sem_b, device_id=(1, me), device_id_type=MESH
        ).wait_send()

    @pl.when((leaf == 0) & (me < n_src))
    def _():
        for k in range(per_src):
            src = top_ref.at[pl.ds(k * rows, rows)]
            dst = me * per_src + k
            if k == 0:
                @pl.when(me != 0)
                def _():
                    pltpu.make_async_remote_copy(
                        src, chunk, send_a.at[k], sem_a, device_id=(0, dst), device_id_type=MESH
                    ).wait_send()
            else:
                pltpu.make_async_remote_copy(
                    src, chunk, send_a.at[k], sem_a, device_id=(0, dst), device_id_type=MESH
                ).wait_send()


def broadcast_pivot(top, n_front):
    cols = top.shape[1]
    n_src = S // cols
    per_src = n_front // n_src
    rows = S // per_src
    gathered = pl.pallas_call(
        functools.partial(pivot_kernel, n_front, n_src),
        out_shape=jax.ShapeDtypeStruct((n_front, rows, cols), jnp.float32),
        in_specs=[pl.BlockSpec(memory_space=pltpu.VMEM)],
        out_specs=pl.BlockSpec(memory_space=pltpu.VMEM),
        scratch_shapes=[
            pltpu.VMEM((rows, cols), jnp.float32),
            pltpu.SemaphoreType.DMA,
            pltpu.SemaphoreType.DMA,
            pltpu.SemaphoreType.DMA((per_src,)),
            pltpu.SemaphoreType.DMA,
            pltpu.SemaphoreType.DMA((n_front,)),
            pltpu.SemaphoreType.DMA((n_front,)),
        ],
        compiler_params=pltpu.CompilerParams(has_side_effects=True),
    )(top)
    return gathered.reshape(n_src, per_src, rows, cols).transpose(1, 2, 0, 3).reshape(S, S)


PANEL = 8


def _mm(a, b):
    return jnp.dot(a, b, precision=HIGHEST, preferred_element_type=jnp.float32)


def _mm_t(a, b):
    return lax.dot_general(a, b, (((1,), (1,)), ((), ())), precision=HIGHEST,
                           preferred_element_type=jnp.float32)


def chol_inv_kernel(a_ref, l_ref, linv_ref, w_ref, d_ref, e_ref, ut_ref, x_ref):
    n = a_ref.shape[0]
    b = d_ref.shape[0]
    nb = n // b
    lane = lax.broadcasted_iota(jnp.int32, (PANEL, b), 1)
    sub = lax.broadcasted_iota(jnp.int32, (PANEL, 1), 0)
    eye = (lax.broadcasted_iota(jnp.int32, (b, b), 0) == lax.broadcasted_iota(jnp.int32, (b, b), 1)).astype(jnp.float32)
    w_ref[...] = a_ref[...]
    l_ref[...] = jnp.zeros_like(l_ref)
    linv_ref[...] = jnp.zeros_like(linv_ref)

    def panel(p, carry):
        k = pl.multiple_of(p * PANEL, PANEL)
        r = d_ref[pl.ds(k, PANEL), :]
        e = e_ref[pl.ds(k, PANEL), :]
        for t in range(PANEL):
            c = k + t
            at_c = lane == c
            colv = jnp.sum(jnp.where(at_c, r, 0.0), axis=1, keepdims=True)
            piv = jnp.sum(jnp.where(at_c[t:t + 1], r[t:t + 1], 0.0), axis=1, keepdims=True)
            scale = 1.0 / jnp.sqrt(piv)
            urow = jnp.where(lane[t:t + 1] >= c, r[t:t + 1] * scale, 0.0)
            f = jnp.where(sub > t, colv * scale, 0.0)
            r = jnp.where(sub == t, urow, r - f * urow)
            xrow = e[t:t + 1] * scale
            e = jnp.where(sub == t, xrow, e - f * xrow)
        ut_ref[pl.ds(k, PANEL), :] = r
        x_ref[pl.ds(k, PANEL), :] = e
        rt = jnp.transpose(r)
        dd = d_ref[...]
        ee = e_ref[...]
        for t in range(PANEL):
            lcol = rt[:, t:t + 1]
            dd = dd - lcol * r[t:t + 1]
            ee = ee - lcol * e[t:t + 1]
        d_ref[...] = dd
        e_ref[...] = ee
        return carry

    for j in range(nb):
        jb = j * b
        d_ref[...] = w_ref[jb:jb + b, jb:jb + b]
        e_ref[...] = eye
        lax.fori_loop(0, b // PANEL, panel, 0)
        l_ref[jb:jb + b, jb:jb + b] = jnp.transpose(ut_ref[...])
        linv_ref[jb:jb + b, jb:jb + b] = x_ref[...]
        if j < nb - 1:
            lp = _mm_t(w_ref[jb + b:, jb:jb + b], x_ref[...])
            l_ref[jb + b:, jb:jb + b] = lp
            w_ref[jb + b:, jb + b:] = w_ref[jb + b:, jb + b:] - _mm_t(lp, lp)
    for j in range(nb):
        for i in range(j + 1, nb):
            acc = jnp.zeros((b, b), jnp.float32)
            for k in range(j, i):
                acc = acc + _mm(l_ref[i * b:(i + 1) * b, k * b:(k + 1) * b], linv_ref[k * b:(k + 1) * b, j * b:(j + 1) * b])
            linv_ref[i * b:(i + 1) * b, j * b:(j + 1) * b] = -_mm(linv_ref[i * b:(i + 1) * b, i * b:(i + 1) * b], acc)


def chol_inv(a, b=128):
    n = a.shape[0]
    return pl.pallas_call(
        chol_inv_kernel,
        out_shape=(jax.ShapeDtypeStruct((n, n), jnp.float32), jax.ShapeDtypeStruct((n, n), jnp.float32)),
        in_specs=[pl.BlockSpec(memory_space=pltpu.VMEM)],
        out_specs=(pl.BlockSpec(memory_space=pltpu.VMEM), pl.BlockSpec(memory_space=pltpu.VMEM)),
        scratch_shapes=[
            pltpu.VMEM((n, n), jnp.float32),
            pltpu.VMEM((b, b), jnp.float32),
            pltpu.VMEM((b, b), jnp.float32),
            pltpu.VMEM((b, b), jnp.float32),
            pltpu.VMEM((b, b), jnp.float32),
        ],
    )(a)


def panel_product_kernel(subtract, use_top_ref, panel_ref, w_ref, base_ref, top_ref, out_ref):
    prod = jnp.transpose(lax.dot_general(w_ref[...], panel_ref[...], (((1,), (1,)), ((), ())),
                                         precision=HIGHEST, preferred_element_type=jnp.float32))
    result = base_ref[...] - prod if subtract else prod
    replace = (pl.program_id(0) == 0) & (use_top_ref[0] == 1)
    out_ref[...] = jnp.where(replace, top_ref[...], result)


def panel_product(use_top, panel, weights, base, top_rows, subtract):
    rows, depth = panel.shape
    cols = weights.shape[0]
    return pl.pallas_call(
        functools.partial(panel_product_kernel, subtract),
        out_shape=jax.ShapeDtypeStruct((rows, cols), jnp.float32),
        grid_spec=pltpu.PrefetchScalarGridSpec(
            num_scalar_prefetch=1,
            grid=(rows // S,),
            in_specs=[
                pl.BlockSpec((S, depth), lambda i, flag: (i, 0)),
                pl.BlockSpec((cols, depth), lambda i, flag: (0, 0)),
                pl.BlockSpec((S, cols), lambda i, flag: (i, 0)),
                pl.BlockSpec((S, cols), lambda i, flag: (0, 0)),
            ],
            out_specs=pl.BlockSpec((S, cols), lambda i, flag: (i, 0)),
        ),
    )(use_top, panel, weights, base, top_rows)


def per_device(front_block, child_update, child_map):
    rows, cols = front_block.shape
    n_leaf = lax.axis_size("leaf")
    n_front = lax.axis_size("front")
    leaf = lax.axis_index("leaf")
    front = lax.axis_index("front")
    half_blocks = rows // BLK

    blocks = child_update[0].reshape(-1, BLK, cols)
    cmap = child_map[0]
    own = gather_half(blocks, cmap, leaf, half_blocks)
    send = gather_half(blocks, cmap, 1 - leaf, half_blocks)
    recv = lax.ppermute(send, "leaf", [(0, 1), (1, 0)])
    first = jnp.where(leaf == 0, own, recv)
    second = jnp.where(leaf == 0, recv, own)
    assembled = front_block + first + second

    top = assembled[:S]
    panel_rows = top.T

    piece = rows // n_front
    per_block = BLK // piece
    pieces = []
    for part in range(per_block):
        pairs = []
        for lf in range(n_leaf):
            for k in range(n_front // per_block):
                src = lf * half_blocks + k
                dst = lf * n_front + per_block * k + part
                pairs.append((src, dst))
        pieces.append(lax.ppermute(panel_rows[part * piece:(part + 1) * piece], ("leaf", "front"), pairs))
    my_piece = pieces[0]
    for part in range(1, per_block):
        my_piece = jnp.where(front % per_block == part, pieces[part], my_piece)
    pivot = broadcast_pivot(top, n_front)
    partner_rows = lax.ppermute(panel_rows, "leaf", [(0, 1)])
    col_rows = jnp.where(leaf == 0, panel_rows, partner_rows)
    my_piece, pivot = lax.optimization_barrier((my_piece, pivot))
    panel = lax.all_gather(my_piece, "front", tiled=True)
    factor, inverse = chol_inv(pivot)

    col_solved = lax.dot_general(col_rows, inverse, (((1,), (1,)), ((), ())), precision=HIGHEST)

    piv_cols = S // cols
    col_at = jnp.minimum(front, piv_cols - 1) * cols

    use_top = (leaf == 0).astype(jnp.int32).reshape(1)

    def pivot_columns():
        inv_rows = lax.dynamic_slice_in_dim(inverse, col_at, cols, 0)
        top_rows = lax.dynamic_slice_in_dim(factor, col_at, cols, 1)
        return panel_product(use_top, panel, inv_rows, assembled, top_rows, False)

    def other_columns():
        weights = jnp.dot(col_solved, inverse, precision=HIGHEST)
        return panel_product(use_top, panel, weights, assembled, col_solved.T, True)

    return lax.cond(front < piv_cols, pivot_columns, other_columns)


def solution(mesh):
    return jax.shard_map(
        per_device,
        mesh=mesh,
        in_specs=(P("leaf", "front"), P("leaf", None, "front"), P("leaf", None)),
        out_specs=P("leaf", "front"),
        check_vma=False,
    )
```

```python
import functools

import jax
import jax.numpy as jnp
from jax import lax
from jax.experimental import pallas as pl
from jax.experimental.pallas import tpu as pltpu
from jax.sharding import PartitionSpec as P

BLK = 128
S = 512
HIGHEST = lax.Precision.HIGHEST
MESH = pl.DeviceIdType.MESH


def gather_half(blocks, child_map, half, half_blocks):
    parent = half * half_blocks + jnp.arange(half_blocks, dtype=jnp.int32)
    hit = child_map[None, :] == parent[:, None]
    found = jnp.any(hit, axis=1)
    index = jnp.argmax(hit, axis=1)
    picked = jnp.take(blocks, index, axis=0)
    picked = jnp.where(found[:, None, None], picked, jnp.zeros_like(picked))
    return picked.reshape(half_blocks * BLK, blocks.shape[2])


def pivot_kernel(n_front, n_src, top_ref, out_ref, chunk, sem_a, sem_b, send_a, send_b, recv_g, send_g):
    leaf = lax.axis_index("leaf")
    me = lax.axis_index("front")
    per_src = n_front // n_src
    rows = chunk.shape[0]

    @pl.when((leaf == 0) & (me < n_src))
    def _():
        for k in range(per_src):
            src = top_ref.at[pl.ds(k * rows, rows)]
            dst = me * per_src + k
            if k == 0:
                @pl.when(me == 0)
                def _():
                    pltpu.make_async_copy(src, chunk, sem_a).start()

                @pl.when(me != 0)
                def _():
                    pltpu.make_async_remote_copy(
                        src, chunk, send_a.at[k], sem_a, device_id=(0, dst), device_id_type=MESH
                    ).start()
            else:
                pltpu.make_async_remote_copy(
                    src, chunk, send_a.at[k], sem_a, device_id=(0, dst), device_id_type=MESH
                ).start()

    @pl.when((leaf == 0) & (me == 0))
    def _():
        pltpu.make_async_copy(top_ref.at[pl.ds(0, rows)], chunk, sem_a).wait()

    @pl.when((leaf == 0) & (me != 0))
    def _():
        pltpu.make_async_remote_copy(
            top_ref.at[pl.ds(0, rows)], chunk, send_a.at[0], sem_a, device_id=(0, me), device_id_type=MESH
        ).wait_recv()

    @pl.when(leaf == 0)
    def _():
        pltpu.make_async_remote_copy(
            chunk, chunk, send_b, sem_b, device_id=(1, me), device_id_type=MESH
        ).start()

    @pl.when(leaf == 1)
    def _():
        pltpu.make_async_remote_copy(
            chunk, chunk, send_b, sem_b, device_id=(0, me), device_id_type=MESH
        ).wait_recv()

    pltpu.make_async_copy(chunk, out_ref.at[me], recv_g.at[me]).start()

    def send(j, carry):
        dst = lax.rem(me + j, n_front)
        pltpu.make_async_remote_copy(
            chunk, out_ref.at[me], send_g.at[j], recv_g.at[me], device_id=(leaf, dst), device_id_type=MESH
        ).start()
        return carry

    lax.fori_loop(1, n_front, send, 0)

    pltpu.make_async_copy(chunk, out_ref.at[me], recv_g.at[me]).wait()

    def receive(j, carry):
        src = lax.rem(me + j, n_front)
        pltpu.make_async_remote_copy(
            chunk, out_ref.at[src], send_g.at[j], recv_g.at[src], device_id=(leaf, src), device_id_type=MESH
        ).wait_recv()
        return carry

    lax.fori_loop(1, n_front, receive, 0)

    def sent(j, carry):
        dst = lax.rem(me + j, n_front)
        pltpu.make_async_remote_copy(
            chunk, out_ref.at[me], send_g.at[j], recv_g.at[me], device_id=(leaf, dst), device_id_type=MESH
        ).wait_send()
        return carry

    lax.fori_loop(1, n_front, sent, 0)

    @pl.when(leaf == 0)
    def _():
        pltpu.make_async_remote_copy(
            chunk, chunk, send_b, sem_b, device_id=(1, me), device_id_type=MESH
        ).wait_send()

    @pl.when((leaf == 0) & (me < n_src))
    def _():
        for k in range(per_src):
            src = top_ref.at[pl.ds(k * rows, rows)]
            dst = me * per_src + k
            if k == 0:
                @pl.when(me != 0)
                def _():
                    pltpu.make_async_remote_copy(
                        src, chunk, send_a.at[k], sem_a, device_id=(0, dst), device_id_type=MESH
                    ).wait_send()
            else:
                pltpu.make_async_remote_copy(
                    src, chunk, send_a.at[k], sem_a, device_id=(0, dst), device_id_type=MESH
                ).wait_send()


def broadcast_pivot(top, n_front):
    cols = top.shape[1]
    n_src = S // cols
    per_src = n_front // n_src
    rows = S // per_src
    gathered = pl.pallas_call(
        functools.partial(pivot_kernel, n_front, n_src),
        out_shape=jax.ShapeDtypeStruct((n_front, rows, cols), jnp.float32),
        in_specs=[pl.BlockSpec(memory_space=pltpu.VMEM)],
        out_specs=pl.BlockSpec(memory_space=pltpu.VMEM),
        scratch_shapes=[
            pltpu.VMEM((rows, cols), jnp.float32),
            pltpu.SemaphoreType.DMA,
            pltpu.SemaphoreType.DMA,
            pltpu.SemaphoreType.DMA((per_src,)),
            pltpu.SemaphoreType.DMA,
            pltpu.SemaphoreType.DMA((n_front,)),
            pltpu.SemaphoreType.DMA((n_front,)),
        ],
        compiler_params=pltpu.CompilerParams(has_side_effects=True),
    )(top)
    return gathered


PANEL = 8


def _mm(a, b):
    return jnp.dot(a, b, precision=HIGHEST, preferred_element_type=jnp.float32)


def _mm_t(a, b):
    return lax.dot_general(a, b, (((1,), (1,)), ((), ())), precision=HIGHEST,
                           preferred_element_type=jnp.float32)


def chol_inv_kernel(a_ref, l_ref, linv_ref, w_ref, d_ref, e_ref, ut_ref, x_ref):
    n = w_ref.shape[0]
    b = d_ref.shape[0]
    nb = n // b
    lane = lax.broadcasted_iota(jnp.int32, (PANEL, b), 1)
    sub = lax.broadcasted_iota(jnp.int32, (PANEL, 1), 0)
    eye = (lax.broadcasted_iota(jnp.int32, (b, b), 0) == lax.broadcasted_iota(jnp.int32, (b, b), 1)).astype(jnp.float32)
    n_slots, rows, cols = a_ref.shape
    per_src = n_slots // (n // cols)
    for slot in range(n_slots):
        c, k = divmod(slot, per_src)
        w_ref[k * rows:(k + 1) * rows, c * cols:(c + 1) * cols] = a_ref[slot]
    l_ref[...] = jnp.zeros_like(l_ref)
    linv_ref[...] = jnp.zeros_like(linv_ref)

    def panel(p, carry):
        k = pl.multiple_of(p * PANEL, PANEL)
        r = d_ref[pl.ds(k, PANEL), :]
        e = e_ref[pl.ds(k, PANEL), :]
        for t in range(PANEL):
            c = k + t
            at_c = lane == c
            colv = jnp.sum(jnp.where(at_c, r, 0.0), axis=1, keepdims=True)
            piv = jnp.sum(jnp.where(at_c[t:t + 1], r[t:t + 1], 0.0), axis=1, keepdims=True)
            scale = 1.0 / jnp.sqrt(piv)
            urow = jnp.where(lane[t:t + 1] >= c, r[t:t + 1] * scale, 0.0)
            f = jnp.where(sub > t, colv * scale, 0.0)
            r = jnp.where(sub == t, urow, r - f * urow)
            xrow = e[t:t + 1] * scale
            e = jnp.where(sub == t, xrow, e - f * xrow)
        ut_ref[pl.ds(k, PANEL), :] = r
        x_ref[pl.ds(k, PANEL), :] = e
        rt = jnp.transpose(r)
        dd = d_ref[...]
        ee = e_ref[...]
        for t in range(PANEL):
            lcol = rt[:, t:t + 1]
            dd = dd - lcol * r[t:t + 1]
            ee = ee - lcol * e[t:t + 1]
        d_ref[...] = dd
        e_ref[...] = ee
        return carry

    for j in range(nb):
        jb = j * b
        d_ref[...] = w_ref[jb:jb + b, jb:jb + b]
        e_ref[...] = eye
        lax.fori_loop(0, b // PANEL, panel, 0)
        l_ref[jb:jb + b, jb:jb + b] = jnp.transpose(ut_ref[...])
        linv_ref[jb:jb + b, jb:jb + b] = x_ref[...]
        if j < nb - 1:
            lp = _mm_t(w_ref[jb + b:, jb:jb + b], x_ref[...])
            l_ref[jb + b:, jb:jb + b] = lp
            w_ref[jb + b:, jb + b:] = w_ref[jb + b:, jb + b:] - _mm_t(lp, lp)
    for j in range(nb):
        for i in range(j + 1, nb):
            acc = jnp.zeros((b, b), jnp.float32)
            for k in range(j, i):
                acc = acc + _mm(l_ref[i * b:(i + 1) * b, k * b:(k + 1) * b], linv_ref[k * b:(k + 1) * b, j * b:(j + 1) * b])
            linv_ref[i * b:(i + 1) * b, j * b:(j + 1) * b] = -_mm(linv_ref[i * b:(i + 1) * b, i * b:(i + 1) * b], acc)


def chol_inv(a, n, b=128):
    return pl.pallas_call(
        chol_inv_kernel,
        out_shape=(jax.ShapeDtypeStruct((n, n), jnp.float32), jax.ShapeDtypeStruct((n, n), jnp.float32)),
        in_specs=[pl.BlockSpec(memory_space=pltpu.VMEM)],
        out_specs=(pl.BlockSpec(memory_space=pltpu.VMEM), pl.BlockSpec(memory_space=pltpu.VMEM)),
        scratch_shapes=[
            pltpu.VMEM((n, n), jnp.float32),
            pltpu.VMEM((b, b), jnp.float32),
            pltpu.VMEM((b, b), jnp.float32),
            pltpu.VMEM((b, b), jnp.float32),
            pltpu.VMEM((b, b), jnp.float32),
        ],
    )(a)


def panel_product_kernel(subtract, use_top_ref, panel_ref, w_ref, base_ref, top_ref, out_ref):
    prod = jnp.transpose(lax.dot_general(w_ref[...], panel_ref[...], (((1,), (1,)), ((), ())),
                                         precision=HIGHEST, preferred_element_type=jnp.float32))
    result = base_ref[...] - prod if subtract else prod
    replace = (pl.program_id(0) == 0) & (use_top_ref[0] == 1)
    out_ref[...] = jnp.where(replace, top_ref[...], result)


def panel_product(use_top, panel, weights, base, top_rows, subtract):
    rows, depth = panel.shape
    cols = weights.shape[0]
    return pl.pallas_call(
        functools.partial(panel_product_kernel, subtract),
        out_shape=jax.ShapeDtypeStruct((rows, cols), jnp.float32),
        grid_spec=pltpu.PrefetchScalarGridSpec(
            num_scalar_prefetch=1,
            grid=(rows // S,),
            in_specs=[
                pl.BlockSpec((S, depth), lambda i, flag: (i, 0)),
                pl.BlockSpec((cols, depth), lambda i, flag: (0, 0)),
                pl.BlockSpec((S, cols), lambda i, flag: (i, 0)),
                pl.BlockSpec((S, cols), lambda i, flag: (0, 0)),
            ],
            out_specs=pl.BlockSpec((S, cols), lambda i, flag: (i, 0)),
        ),
    )(use_top, panel, weights, base, top_rows)


def per_device(front_block, child_update, child_map):
    rows, cols = front_block.shape
    n_leaf = lax.axis_size("leaf")
    n_front = lax.axis_size("front")
    leaf = lax.axis_index("leaf")
    front = lax.axis_index("front")
    half_blocks = rows // BLK

    blocks = child_update[0].reshape(-1, BLK, cols)
    cmap = child_map[0]
    own = gather_half(blocks, cmap, leaf, half_blocks)
    send = gather_half(blocks, cmap, 1 - leaf, half_blocks)
    recv = lax.ppermute(send, "leaf", [(0, 1), (1, 0)])
    first = jnp.where(leaf == 0, own, recv)
    second = jnp.where(leaf == 0, recv, own)
    assembled = front_block + first + second

    top = assembled[:S]
    panel_rows = top.T

    piece = rows // n_front
    per_block = BLK // piece
    pieces = []
    for part in range(per_block):
        pairs = []
        for lf in range(n_leaf):
            for k in range(n_front // per_block):
                src = lf * half_blocks + k
                dst = lf * n_front + per_block * k + part
                pairs.append((src, dst))
        pieces.append(lax.ppermute(panel_rows[part * piece:(part + 1) * piece], ("leaf", "front"), pairs))
    my_piece = pieces[0]
    for part in range(1, per_block):
        my_piece = jnp.where(front % per_block == part, pieces[part], my_piece)
    pivot = broadcast_pivot(top, n_front)
    partner_rows = lax.ppermute(panel_rows, "leaf", [(0, 1)])
    col_rows = jnp.where(leaf == 0, panel_rows, partner_rows)
    my_piece, pivot = lax.optimization_barrier((my_piece, pivot))
    panel = lax.all_gather(my_piece, "front", tiled=True)
    factor, inverse = chol_inv(pivot, S)

    col_solved = lax.dot_general(col_rows, inverse, (((1,), (1,)), ((), ())), precision=HIGHEST)

    piv_cols = S // cols
    col_at = jnp.minimum(front, piv_cols - 1) * cols

    use_top = (leaf == 0).astype(jnp.int32).reshape(1)

    def pivot_columns():
        inv_rows = lax.dynamic_slice_in_dim(inverse, col_at, cols, 0)
        top_rows = lax.dynamic_slice_in_dim(factor, col_at, cols, 1)
        return panel_product(use_top, panel, inv_rows, assembled, top_rows, False)

    def other_columns():
        weights = jnp.dot(col_solved, inverse, precision=HIGHEST)
        return panel_product(use_top, panel, weights, assembled, col_solved.T, True)

    return lax.cond(front < piv_cols, pivot_columns, other_columns)


def solution(mesh):
    return jax.shard_map(
        per_device,
        mesh=mesh,
        in_specs=(P("leaf", "front"), P("leaf", None, "front"), P("leaf", None)),
        out_specs=P("leaf", "front"),
        check_vma=False,
    )
```

```python
import functools

import jax
import jax.numpy as jnp
from jax import lax
from jax.experimental import pallas as pl
from jax.experimental.pallas import tpu as pltpu
from jax.sharding import PartitionSpec as P

BLK = 128
S = 512
HIGHEST = lax.Precision.HIGHEST
MESH = pl.DeviceIdType.MESH


def gather_half(blocks, child_map, half, half_blocks):
    parent = half * half_blocks + jnp.arange(half_blocks, dtype=jnp.int32)
    hit = child_map[None, :] == parent[:, None]
    found = jnp.any(hit, axis=1)
    index = jnp.argmax(hit, axis=1)
    picked = jnp.take(blocks, index, axis=0)
    picked = jnp.where(found[:, None, None], picked, jnp.zeros_like(picked))
    return picked.reshape(half_blocks * BLK, blocks.shape[2])


def pivot_kernel(n_front, n_src, top_ref, out_ref, chunk, sem_a, sem_b, send_a, send_b, recv_g, send_g):
    leaf = lax.axis_index("leaf")
    me = lax.axis_index("front")
    per_src = n_front // n_src
    rows = chunk.shape[0]

    @pl.when((leaf == 0) & (me < n_src))
    def _():
        for k in range(per_src):
            src = top_ref.at[pl.ds(k * rows, rows)]
            dst = me * per_src + k
            if k == 0:
                @pl.when(me == 0)
                def _():
                    pltpu.make_async_copy(src, chunk, sem_a).start()

                @pl.when(me != 0)
                def _():
                    pltpu.make_async_remote_copy(
                        src, chunk, send_a.at[k], sem_a, device_id=(0, dst), device_id_type=MESH
                    ).start()
            else:
                pltpu.make_async_remote_copy(
                    src, chunk, send_a.at[k], sem_a, device_id=(0, dst), device_id_type=MESH
                ).start()

    @pl.when((leaf == 0) & (me == 0))
    def _():
        pltpu.make_async_copy(top_ref.at[pl.ds(0, rows)], chunk, sem_a).wait()

    @pl.when((leaf == 0) & (me != 0))
    def _():
        pltpu.make_async_remote_copy(
            top_ref.at[pl.ds(0, rows)], chunk, send_a.at[0], sem_a, device_id=(0, me), device_id_type=MESH
        ).wait_recv()

    @pl.when(leaf == 0)
    def _():
        pltpu.make_async_remote_copy(
            chunk, chunk, send_b, sem_b, device_id=(1, me), device_id_type=MESH
        ).start()

    @pl.when(leaf == 1)
    def _():
        pltpu.make_async_remote_copy(
            chunk, chunk, send_b, sem_b, device_id=(0, me), device_id_type=MESH
        ).wait_recv()

    pltpu.make_async_copy(chunk, out_ref.at[me], recv_g.at[me]).start()

    def send(j, carry):
        dst = lax.rem(me + j, n_front)
        pltpu.make_async_remote_copy(
            chunk, out_ref.at[me], send_g.at[j], recv_g.at[me], device_id=(leaf, dst), device_id_type=MESH
        ).start()
        return carry

    lax.fori_loop(1, n_front, send, 0)

    pltpu.make_async_copy(chunk, out_ref.at[me], recv_g.at[me]).wait()

    def receive(j, carry):
        src = lax.rem(me + j, n_front)
        pltpu.make_async_remote_copy(
            chunk, out_ref.at[src], send_g.at[j], recv_g.at[src], device_id=(leaf, src), device_id_type=MESH
        ).wait_recv()
        return carry

    lax.fori_loop(1, n_front, receive, 0)

    def sent(j, carry):
        dst = lax.rem(me + j, n_front)
        pltpu.make_async_remote_copy(
            chunk, out_ref.at[me], send_g.at[j], recv_g.at[me], device_id=(leaf, dst), device_id_type=MESH
        ).wait_send()
        return carry

    lax.fori_loop(1, n_front, sent, 0)

    @pl.when(leaf == 0)
    def _():
        pltpu.make_async_remote_copy(
            chunk, chunk, send_b, sem_b, device_id=(1, me), device_id_type=MESH
        ).wait_send()

    @pl.when((leaf == 0) & (me < n_src))
    def _():
        for k in range(per_src):
            src = top_ref.at[pl.ds(k * rows, rows)]
            dst = me * per_src + k
            if k == 0:
                @pl.when(me != 0)
                def _():
                    pltpu.make_async_remote_copy(
                        src, chunk, send_a.at[k], sem_a, device_id=(0, dst), device_id_type=MESH
                    ).wait_send()
            else:
                pltpu.make_async_remote_copy(
                    src, chunk, send_a.at[k], sem_a, device_id=(0, dst), device_id_type=MESH
                ).wait_send()


def broadcast_pivot(top, n_front):
    cols = top.shape[1]
    n_src = S // cols
    per_src = n_front // n_src
    rows = S // per_src
    gathered = pl.pallas_call(
        functools.partial(pivot_kernel, n_front, n_src),
        out_shape=jax.ShapeDtypeStruct((n_front, rows, cols), jnp.float32),
        in_specs=[pl.BlockSpec(memory_space=pltpu.VMEM)],
        out_specs=pl.BlockSpec(memory_space=pltpu.VMEM),
        scratch_shapes=[
            pltpu.VMEM((rows, cols), jnp.float32),
            pltpu.SemaphoreType.DMA,
            pltpu.SemaphoreType.DMA,
            pltpu.SemaphoreType.DMA((per_src,)),
            pltpu.SemaphoreType.DMA,
            pltpu.SemaphoreType.DMA((n_front,)),
            pltpu.SemaphoreType.DMA((n_front,)),
        ],
        compiler_params=pltpu.CompilerParams(has_side_effects=True),
    )(top)
    return gathered


PANEL = 8


def _mm(a, b):
    return jnp.dot(a, b, precision=HIGHEST, preferred_element_type=jnp.float32)


def _mm_t(a, b):
    return lax.dot_general(a, b, (((1,), (1,)), ((), ())), precision=HIGHEST,
                           preferred_element_type=jnp.float32)


def chol_inv_kernel(a_ref, l_ref, linv_ref, w_ref, d_ref, e_ref, ut_ref, x_ref):
    n = w_ref.shape[0]
    b = d_ref.shape[0]
    nb = n // b
    lane = lax.broadcasted_iota(jnp.int32, (PANEL, b), 1)
    sub = lax.broadcasted_iota(jnp.int32, (PANEL, 1), 0)
    eye = (lax.broadcasted_iota(jnp.int32, (b, b), 0) == lax.broadcasted_iota(jnp.int32, (b, b), 1)).astype(jnp.float32)
    n_slots, rows, cols = a_ref.shape
    per_src = n_slots // (n // cols)
    for slot in range(n_slots):
        c, k = divmod(slot, per_src)
        w_ref[k * rows:(k + 1) * rows, c * cols:(c + 1) * cols] = a_ref[slot]
    l_ref[...] = jnp.zeros_like(l_ref)
    linv_ref[...] = jnp.zeros_like(linv_ref)

    def panel(p, carry):
        k = pl.multiple_of(p * PANEL, PANEL)
        r = d_ref[pl.ds(k, PANEL), :]
        e = e_ref[pl.ds(k, PANEL), :]
        for t in range(PANEL):
            c = k + t
            at_c = lane == c
            colv = jnp.sum(jnp.where(at_c, r, 0.0), axis=1, keepdims=True)
            piv = jnp.sum(jnp.where(at_c[t:t + 1], r[t:t + 1], 0.0), axis=1, keepdims=True)
            scale = 1.0 / jnp.sqrt(piv)
            urow = jnp.where(lane[t:t + 1] >= c, r[t:t + 1] * scale, 0.0)
            f = jnp.where(sub > t, colv * scale, 0.0)
            r = jnp.where(sub == t, urow, r - f * urow)
            xrow = e[t:t + 1] * scale
            e = jnp.where(sub == t, xrow, e - f * xrow)
        ut_ref[pl.ds(k, PANEL), :] = r
        x_ref[pl.ds(k, PANEL), :] = e
        rt = jnp.transpose(r)
        dd = d_ref[...]
        ee = e_ref[...]
        for t in range(PANEL):
            lcol = rt[:, t:t + 1]
            dd = dd - lcol * r[t:t + 1]
            ee = ee - lcol * e[t:t + 1]
        d_ref[...] = dd
        e_ref[...] = ee
        return carry

    for j in range(nb):
        jb = j * b
        d_ref[...] = w_ref[jb:jb + b, jb:jb + b]
        e_ref[...] = eye
        lax.fori_loop(0, b // PANEL, panel, 0)
        l_ref[jb:jb + b, jb:jb + b] = jnp.transpose(ut_ref[...])
        linv_ref[jb:jb + b, jb:jb + b] = x_ref[...]
        if j < nb - 1:
            lp = _mm_t(w_ref[jb + b:, jb:jb + b], x_ref[...])
            l_ref[jb + b:, jb:jb + b] = lp
            w_ref[jb + b:, jb + b:] = w_ref[jb + b:, jb + b:] - _mm_t(lp, lp)
    for j in range(nb):
        for i in range(j + 1, nb):
            acc = jnp.zeros((b, b), jnp.float32)
            for k in range(j, i):
                acc = acc + _mm(l_ref[i * b:(i + 1) * b, k * b:(k + 1) * b], linv_ref[k * b:(k + 1) * b, j * b:(j + 1) * b])
            linv_ref[i * b:(i + 1) * b, j * b:(j + 1) * b] = -_mm(linv_ref[i * b:(i + 1) * b, i * b:(i + 1) * b], acc)


def chol_inv(a, n, b=128):
    return pl.pallas_call(
        chol_inv_kernel,
        out_shape=(jax.ShapeDtypeStruct((n, n), jnp.float32), jax.ShapeDtypeStruct((n, n), jnp.float32)),
        in_specs=[pl.BlockSpec(memory_space=pltpu.VMEM)],
        out_specs=(pl.BlockSpec(memory_space=pltpu.VMEM), pl.BlockSpec(memory_space=pltpu.VMEM)),
        scratch_shapes=[
            pltpu.VMEM((n, n), jnp.float32),
            pltpu.VMEM((b, b), jnp.float32),
            pltpu.VMEM((b, b), jnp.float32),
            pltpu.VMEM((b, b), jnp.float32),
            pltpu.VMEM((b, b), jnp.float32),
        ],
    )(a)


def panel_product_kernel(subtract, use_top_ref, panel_ref, w_ref, base_ref, top_ref, out_ref):
    prod = jnp.transpose(lax.dot_general(w_ref[...], panel_ref[...], (((1,), (1,)), ((), ())),
                                         precision=HIGHEST, preferred_element_type=jnp.float32))
    result = base_ref[...] - prod if subtract else prod
    replace = (pl.program_id(0) == 0) & (use_top_ref[0] == 1)
    out_ref[...] = jnp.where(replace, top_ref[...], result)


def panel_product(use_top, panel, weights, base, top_rows, subtract):
    rows, depth = panel.shape
    cols = weights.shape[0]
    return pl.pallas_call(
        functools.partial(panel_product_kernel, subtract),
        out_shape=jax.ShapeDtypeStruct((rows, cols), jnp.float32),
        grid_spec=pltpu.PrefetchScalarGridSpec(
            num_scalar_prefetch=1,
            grid=(rows // S,),
            in_specs=[
                pl.BlockSpec((S, depth), lambda i, flag: (i, 0)),
                pl.BlockSpec((cols, depth), lambda i, flag: (0, 0)),
                pl.BlockSpec((S, cols), lambda i, flag: (i, 0)),
                pl.BlockSpec((S, cols), lambda i, flag: (0, 0)),
            ],
            out_specs=pl.BlockSpec((S, cols), lambda i, flag: (i, 0)),
        ),
    )(use_top, panel, weights, base, top_rows)


def per_device(front_block, child_update, child_map):
    rows, cols = front_block.shape
    n_leaf = lax.axis_size("leaf")
    n_front = lax.axis_size("front")
    leaf = lax.axis_index("leaf")
    front = lax.axis_index("front")
    half_blocks = rows // BLK

    blocks = child_update[0].reshape(-1, BLK, cols)
    cmap = child_map[0]
    own = gather_half(blocks, cmap, leaf, half_blocks)
    send = gather_half(blocks, cmap, 1 - leaf, half_blocks)
    recv = lax.ppermute(send, "leaf", [(0, 1), (1, 0)])
    first = jnp.where(leaf == 0, own, recv)
    second = jnp.where(leaf == 0, recv, own)
    assembled = front_block + first + second

    top = assembled[:S]
    panel_rows = top.T

    pivot = broadcast_pivot(top, n_front)
    piece_rows, pivot = lax.optimization_barrier((panel_rows, pivot))

    piece = rows // n_front
    per_block = BLK // piece
    pieces = []
    for part in range(per_block):
        pairs = []
        for lf in range(n_leaf):
            for k in range(n_front // per_block):
                src = lf * half_blocks + k
                dst = lf * n_front + per_block * k + part
                pairs.append((src, dst))
        pieces.append(lax.ppermute(piece_rows[part * piece:(part + 1) * piece], ("leaf", "front"), pairs))
    my_piece = pieces[0]
    for part in range(1, per_block):
        my_piece = jnp.where(front % per_block == part, pieces[part], my_piece)
    partner_rows = lax.ppermute(panel_rows, "leaf", [(0, 1)])
    col_rows = jnp.where(leaf == 0, panel_rows, partner_rows)
    panel = lax.all_gather(my_piece, "front", tiled=True)
    factor, inverse = chol_inv(pivot, S)

    col_solved = lax.dot_general(col_rows, inverse, (((1,), (1,)), ((), ())), precision=HIGHEST)

    piv_cols = S // cols
    col_at = jnp.minimum(front, piv_cols - 1) * cols

    use_top = (leaf == 0).astype(jnp.int32).reshape(1)

    def pivot_columns():
        inv_rows = lax.dynamic_slice_in_dim(inverse, col_at, cols, 0)
        top_rows = lax.dynamic_slice_in_dim(factor, col_at, cols, 1)
        return panel_product(use_top, panel, inv_rows, assembled, top_rows, False)

    def other_columns():
        weights = jnp.dot(col_solved, inverse, precision=HIGHEST)
        return panel_product(use_top, panel, weights, assembled, col_solved.T, True)

    return lax.cond(front < piv_cols, pivot_columns, other_columns)


def solution(mesh):
    return jax.shard_map(
        per_device,
        mesh=mesh,
        in_specs=(P("leaf", "front"), P("leaf", None, "front"), P("leaf", None)),
        out_specs=P("leaf", "front"),
        check_vma=False,
    )
```

```python
import functools

import jax
import jax.numpy as jnp
from jax import lax
from jax.experimental import pallas as pl
from jax.experimental.pallas import tpu as pltpu
from jax.sharding import PartitionSpec as P

BLK = 128
S = 512
HIGHEST = lax.Precision.HIGHEST
MESH = pl.DeviceIdType.MESH


def gather_half(blocks, child_map, half, half_blocks):
    parent = half * half_blocks + jnp.arange(half_blocks, dtype=jnp.int32)
    hit = child_map[None, :] == parent[:, None]
    found = jnp.any(hit, axis=1)
    index = jnp.argmax(hit, axis=1)
    picked = jnp.take(blocks, index, axis=0)
    picked = jnp.where(found[:, None, None], picked, jnp.zeros_like(picked))
    return picked.reshape(half_blocks * BLK, blocks.shape[2])


def pivot_kernel(n_front, n_src, top_ref, out_ref, chunk, sem_a, sem_b, send_a, send_b, recv_g, send_g):
    leaf = lax.axis_index("leaf")
    me = lax.axis_index("front")
    per_src = n_front // n_src
    rows = chunk.shape[0]

    @pl.when((leaf == 0) & (me < n_src))
    def _():
        for k in range(per_src):
            src = top_ref.at[pl.ds(k * rows, rows)]
            dst = me * per_src + k
            if k == 0:
                @pl.when(me == 0)
                def _():
                    pltpu.make_async_copy(src, chunk, sem_a).start()

                @pl.when(me != 0)
                def _():
                    pltpu.make_async_remote_copy(
                        src, chunk, send_a.at[k], sem_a, device_id=(0, dst), device_id_type=MESH
                    ).start()
            else:
                pltpu.make_async_remote_copy(
                    src, chunk, send_a.at[k], sem_a, device_id=(0, dst), device_id_type=MESH
                ).start()

    @pl.when((leaf == 0) & (me == 0))
    def _():
        pltpu.make_async_copy(top_ref.at[pl.ds(0, rows)], chunk, sem_a).wait()

    @pl.when((leaf == 0) & (me != 0))
    def _():
        pltpu.make_async_remote_copy(
            top_ref.at[pl.ds(0, rows)], chunk, send_a.at[0], sem_a, device_id=(0, me), device_id_type=MESH
        ).wait_recv()

    @pl.when(leaf == 0)
    def _():
        pltpu.make_async_remote_copy(
            chunk, chunk, send_b, sem_b, device_id=(1, me), device_id_type=MESH
        ).start()

    @pl.when(leaf == 1)
    def _():
        pltpu.make_async_remote_copy(
            chunk, chunk, send_b, sem_b, device_id=(0, me), device_id_type=MESH
        ).wait_recv()

    pltpu.make_async_copy(chunk, out_ref.at[me], recv_g.at[me]).start()

    def send(j, carry):
        dst = lax.rem(me + j, n_front)
        pltpu.make_async_remote_copy(
            chunk, out_ref.at[me], send_g.at[j], recv_g.at[me], device_id=(leaf, dst), device_id_type=MESH
        ).start()
        return carry

    lax.fori_loop(1, n_front, send, 0)

    pltpu.make_async_copy(chunk, out_ref.at[me], recv_g.at[me]).wait()

    def receive(j, carry):
        src = lax.rem(me + j, n_front)
        pltpu.make_async_remote_copy(
            chunk, out_ref.at[src], send_g.at[j], recv_g.at[src], device_id=(leaf, src), device_id_type=MESH
        ).wait_recv()
        return carry

    lax.fori_loop(1, n_front, receive, 0)

    def sent(j, carry):
        dst = lax.rem(me + j, n_front)
        pltpu.make_async_remote_copy(
            chunk, out_ref.at[me], send_g.at[j], recv_g.at[me], device_id=(leaf, dst), device_id_type=MESH
        ).wait_send()
        return carry

    lax.fori_loop(1, n_front, sent, 0)

    @pl.when(leaf == 0)
    def _():
        pltpu.make_async_remote_copy(
            chunk, chunk, send_b, sem_b, device_id=(1, me), device_id_type=MESH
        ).wait_send()

    @pl.when((leaf == 0) & (me < n_src))
    def _():
        for k in range(per_src):
            src = top_ref.at[pl.ds(k * rows, rows)]
            dst = me * per_src + k
            if k == 0:
                @pl.when(me != 0)
                def _():
                    pltpu.make_async_remote_copy(
                        src, chunk, send_a.at[k], sem_a, device_id=(0, dst), device_id_type=MESH
                    ).wait_send()
            else:
                pltpu.make_async_remote_copy(
                    src, chunk, send_a.at[k], sem_a, device_id=(0, dst), device_id_type=MESH
                ).wait_send()


def broadcast_pivot(top, n_front):
    cols = top.shape[1]
    n_src = S // cols
    per_src = n_front // n_src
    rows = S // per_src
    gathered = pl.pallas_call(
        functools.partial(pivot_kernel, n_front, n_src),
        out_shape=jax.ShapeDtypeStruct((n_front, rows, cols), jnp.float32),
        in_specs=[pl.BlockSpec(memory_space=pltpu.VMEM)],
        out_specs=pl.BlockSpec(memory_space=pltpu.VMEM),
        scratch_shapes=[
            pltpu.VMEM((rows, cols), jnp.float32),
            pltpu.SemaphoreType.DMA,
            pltpu.SemaphoreType.DMA,
            pltpu.SemaphoreType.DMA((per_src,)),
            pltpu.SemaphoreType.DMA,
            pltpu.SemaphoreType.DMA((n_front,)),
            pltpu.SemaphoreType.DMA((n_front,)),
        ],
        compiler_params=pltpu.CompilerParams(has_side_effects=True),
    )(top)
    return gathered


PANEL = 8


def _mm(a, b):
    return jnp.dot(a, b, precision=HIGHEST, preferred_element_type=jnp.float32)


def _mm_t(a, b):
    return lax.dot_general(a, b, (((1,), (1,)), ((), ())), precision=HIGHEST,
                           preferred_element_type=jnp.float32)


def chol_inv_kernel(a_ref, l_ref, linv_ref, w_ref, d_ref, e_ref, ut_ref, x_ref):
    n = w_ref.shape[0]
    b = d_ref.shape[0]
    nb = n // b
    lane = lax.broadcasted_iota(jnp.int32, (PANEL, b), 1)
    sub = lax.broadcasted_iota(jnp.int32, (PANEL, 1), 0)
    eye = (lax.broadcasted_iota(jnp.int32, (b, b), 0) == lax.broadcasted_iota(jnp.int32, (b, b), 1)).astype(jnp.float32)
    n_slots, rows, cols = a_ref.shape
    per_src = n_slots // (n // cols)
    for slot in range(n_slots):
        c, k = divmod(slot, per_src)
        w_ref[k * rows:(k + 1) * rows, c * cols:(c + 1) * cols] = a_ref[slot]
    l_ref[...] = jnp.zeros_like(l_ref)
    linv_ref[...] = jnp.zeros_like(linv_ref)

    def panel(p, carry):
        k = pl.multiple_of(p * PANEL, PANEL)
        r = d_ref[pl.ds(k, PANEL), :]
        e = e_ref[pl.ds(k, PANEL), :]
        for t in range(PANEL):
            c = k + t
            at_c = lane == c
            colv = jnp.sum(jnp.where(at_c, r, 0.0), axis=1, keepdims=True)
            piv = jnp.sum(jnp.where(at_c[t:t + 1], r[t:t + 1], 0.0), axis=1, keepdims=True)
            scale = 1.0 / jnp.sqrt(piv)
            urow = jnp.where(lane[t:t + 1] >= c, r[t:t + 1] * scale, 0.0)
            f = jnp.where(sub > t, colv * scale, 0.0)
            r = jnp.where(sub == t, urow, r - f * urow)
            xrow = e[t:t + 1] * scale
            e = jnp.where(sub == t, xrow, e - f * xrow)
        ut_ref[pl.ds(k, PANEL), :] = r
        x_ref[pl.ds(k, PANEL), :] = e
        rt = jnp.transpose(r)
        dd = d_ref[...]
        ee = e_ref[...]
        for t in range(PANEL):
            lcol = rt[:, t:t + 1]
            dd = dd - lcol * r[t:t + 1]
            ee = ee - lcol * e[t:t + 1]
        d_ref[...] = dd
        e_ref[...] = ee
        return carry

    for j in range(nb):
        jb = j * b
        d_ref[...] = w_ref[jb:jb + b, jb:jb + b]
        e_ref[...] = eye
        lax.fori_loop(0, b // PANEL, panel, 0)
        l_ref[jb:jb + b, jb:jb + b] = jnp.transpose(ut_ref[...])
        linv_ref[jb:jb + b, jb:jb + b] = x_ref[...]
        if j < nb - 1:
            lp = _mm_t(w_ref[jb + b:, jb:jb + b], x_ref[...])
            l_ref[jb + b:, jb:jb + b] = lp
            w_ref[jb + b:, jb + b:] = w_ref[jb + b:, jb + b:] - _mm_t(lp, lp)
    for j in range(nb):
        for i in range(j + 1, nb):
            acc = jnp.zeros((b, b), jnp.float32)
            for k in range(j, i):
                acc = acc + _mm(l_ref[i * b:(i + 1) * b, k * b:(k + 1) * b], linv_ref[k * b:(k + 1) * b, j * b:(j + 1) * b])
            linv_ref[i * b:(i + 1) * b, j * b:(j + 1) * b] = -_mm(linv_ref[i * b:(i + 1) * b, i * b:(i + 1) * b], acc)


def chol_inv(a, n, b=128):
    return pl.pallas_call(
        chol_inv_kernel,
        out_shape=(jax.ShapeDtypeStruct((n, n), jnp.float32), jax.ShapeDtypeStruct((n, n), jnp.float32)),
        in_specs=[pl.BlockSpec(memory_space=pltpu.VMEM)],
        out_specs=(pl.BlockSpec(memory_space=pltpu.VMEM), pl.BlockSpec(memory_space=pltpu.VMEM)),
        scratch_shapes=[
            pltpu.VMEM((n, n), jnp.float32),
            pltpu.VMEM((b, b), jnp.float32),
            pltpu.VMEM((b, b), jnp.float32),
            pltpu.VMEM((b, b), jnp.float32),
            pltpu.VMEM((b, b), jnp.float32),
        ],
    )(a)


def panel_product_kernel(subtract, use_top_ref, panel_ref, w_ref, base_ref, top_ref, out_ref):
    prod = jnp.transpose(lax.dot_general(w_ref[...], panel_ref[...], (((1,), (1,)), ((), ())),
                                         precision=HIGHEST, preferred_element_type=jnp.float32))
    result = base_ref[...] - prod if subtract else prod
    replace = (pl.program_id(0) == 0) & (use_top_ref[0] == 1)
    out_ref[...] = jnp.where(replace, top_ref[...], result)


def panel_product(use_top, panel, weights, base, top_rows, subtract):
    rows, depth = panel.shape
    cols = weights.shape[0]
    return pl.pallas_call(
        functools.partial(panel_product_kernel, subtract),
        out_shape=jax.ShapeDtypeStruct((rows, cols), jnp.float32),
        grid_spec=pltpu.PrefetchScalarGridSpec(
            num_scalar_prefetch=1,
            grid=(rows // S,),
            in_specs=[
                pl.BlockSpec((S, depth), lambda i, flag: (i, 0)),
                pl.BlockSpec((cols, depth), lambda i, flag: (0, 0)),
                pl.BlockSpec((S, cols), lambda i, flag: (i, 0)),
                pl.BlockSpec((S, cols), lambda i, flag: (0, 0)),
            ],
            out_specs=pl.BlockSpec((S, cols), lambda i, flag: (i, 0)),
        ),
    )(use_top, panel, weights, base, top_rows)


def schur_kernel(use_top_ref, rows_ref, inv_ref, panel_ref, base_ref, out_ref, w_ref, top_ref):
    @pl.when(pl.program_id(0) == 0)
    def _():
        solved = _mm_t(rows_ref[...], inv_ref[...])
        w_ref[...] = _mm(solved, inv_ref[...])
        top_ref[...] = jnp.transpose(solved)

    prod = jnp.transpose(lax.dot_general(w_ref[...], panel_ref[...], (((1,), (1,)), ((), ())),
                                         precision=HIGHEST, preferred_element_type=jnp.float32))
    replace = (pl.program_id(0) == 0) & (use_top_ref[0] == 1)
    out_ref[...] = jnp.where(replace, top_ref[...], base_ref[...] - prod)


def schur_update(use_top, col_rows, inverse, panel, base):
    rows, depth = panel.shape
    cols = col_rows.shape[0]
    return pl.pallas_call(
        schur_kernel,
        out_shape=jax.ShapeDtypeStruct((rows, cols), jnp.float32),
        grid_spec=pltpu.PrefetchScalarGridSpec(
            num_scalar_prefetch=1,
            grid=(rows // S,),
            in_specs=[
                pl.BlockSpec((cols, depth), lambda i, flag: (0, 0)),
                pl.BlockSpec((depth, depth), lambda i, flag: (0, 0)),
                pl.BlockSpec((S, depth), lambda i, flag: (i, 0)),
                pl.BlockSpec((S, cols), lambda i, flag: (i, 0)),
            ],
            out_specs=pl.BlockSpec((S, cols), lambda i, flag: (i, 0)),
            scratch_shapes=[pltpu.VMEM((cols, depth), jnp.float32), pltpu.VMEM((S, cols), jnp.float32)],
        ),
    )(use_top, col_rows, inverse, panel, base)


def per_device(front_block, child_update, child_map):
    rows, cols = front_block.shape
    n_leaf = lax.axis_size("leaf")
    n_front = lax.axis_size("front")
    leaf = lax.axis_index("leaf")
    front = lax.axis_index("front")
    half_blocks = rows // BLK

    blocks = child_update[0].reshape(-1, BLK, cols)
    cmap = child_map[0]
    own = gather_half(blocks, cmap, leaf, half_blocks)
    send = gather_half(blocks, cmap, 1 - leaf, half_blocks)
    recv = lax.ppermute(send, "leaf", [(0, 1), (1, 0)])
    first = jnp.where(leaf == 0, own, recv)
    second = jnp.where(leaf == 0, recv, own)
    assembled = front_block + first + second

    top = assembled[:S]
    panel_rows = top.T

    piece = rows // n_front
    per_block = BLK // piece
    pieces = []
    for part in range(per_block):
        pairs = []
        for lf in range(n_leaf):
            for k in range(n_front // per_block):
                src = lf * half_blocks + k
                dst = lf * n_front + per_block * k + part
                pairs.append((src, dst))
        pieces.append(lax.ppermute(panel_rows[part * piece:(part + 1) * piece], ("leaf", "front"), pairs))
    my_piece = pieces[0]
    for part in range(1, per_block):
        my_piece = jnp.where(front % per_block == part, pieces[part], my_piece)
    pivot = broadcast_pivot(top, n_front)
    partner_rows = lax.ppermute(panel_rows, "leaf", [(0, 1)])
    col_rows = jnp.where(leaf == 0, panel_rows, partner_rows)
    my_piece, pivot = lax.optimization_barrier((my_piece, pivot))
    panel = lax.all_gather(my_piece, "front", tiled=True)
    factor, inverse = chol_inv(pivot, S)


    piv_cols = S // cols
    col_at = jnp.minimum(front, piv_cols - 1) * cols

    use_top = (leaf == 0).astype(jnp.int32).reshape(1)

    def pivot_columns():
        inv_rows = lax.dynamic_slice_in_dim(inverse, col_at, cols, 0)
        top_rows = lax.dynamic_slice_in_dim(factor, col_at, cols, 1)
        return panel_product(use_top, panel, inv_rows, assembled, top_rows, False)

    def other_columns():
        return schur_update(use_top, col_rows, inverse, panel, assembled)

    return lax.cond(front < piv_cols, pivot_columns, other_columns)


def solution(mesh):
    return jax.shard_map(
        per_device,
        mesh=mesh,
        in_specs=(P("leaf", "front"), P("leaf", None, "front"), P("leaf", None)),
        out_specs=P("leaf", "front"),
        check_vma=False,
    )
```

```python
import functools

import jax
import jax.numpy as jnp
from jax import lax
from jax.experimental import pallas as pl
from jax.experimental.pallas import tpu as pltpu
from jax.sharding import PartitionSpec as P

BLK = 128
S = 512
HIGHEST = lax.Precision.HIGHEST
MESH = pl.DeviceIdType.MESH


def gather_half(blocks, child_map, half, half_blocks):
    parent = half * half_blocks + jnp.arange(half_blocks, dtype=jnp.int32)
    hit = child_map[None, :] == parent[:, None]
    found = jnp.any(hit, axis=1)
    index = jnp.argmax(hit, axis=1)
    picked = jnp.take(blocks, index, axis=0)
    picked = jnp.where(found[:, None, None], picked, jnp.zeros_like(picked))
    return picked.reshape(half_blocks * BLK, blocks.shape[2])


def pivot_kernel(n_front, n_src, top_ref, out_ref, cols_ref, chunk, sem_a, sem_b, send_a, send_b, recv_g, send_g, sem_t, send_t):
    leaf = lax.axis_index("leaf")
    me = lax.axis_index("front")
    per_src = n_front // n_src
    rows = chunk.shape[0]

    @pl.when((leaf == 0) & (me < n_src))
    def _():
        for k in range(per_src):
            src = top_ref.at[pl.ds(k * rows, rows)]
            dst = me * per_src + k
            if k == 0:
                @pl.when(me == 0)
                def _():
                    pltpu.make_async_copy(src, chunk, sem_a).start()

                @pl.when(me != 0)
                def _():
                    pltpu.make_async_remote_copy(
                        src, chunk, send_a.at[k], sem_a, device_id=(0, dst), device_id_type=MESH
                    ).start()
            else:
                pltpu.make_async_remote_copy(
                    src, chunk, send_a.at[k], sem_a, device_id=(0, dst), device_id_type=MESH
                ).start()

    @pl.when((leaf == 0) & (me == 0))
    def _():
        pltpu.make_async_copy(top_ref.at[pl.ds(0, rows)], chunk, sem_a).wait()

    @pl.when((leaf == 0) & (me != 0))
    def _():
        pltpu.make_async_remote_copy(
            top_ref.at[pl.ds(0, rows)], chunk, send_a.at[0], sem_a, device_id=(0, me), device_id_type=MESH
        ).wait_recv()

    @pl.when(leaf == 0)
    def _():
        pltpu.make_async_copy(top_ref, cols_ref, sem_t).start()
        pltpu.make_async_remote_copy(
            top_ref, cols_ref, send_t, sem_t, device_id=(1, me), device_id_type=MESH
        ).start()

    @pl.when(leaf == 0)
    def _():
        pltpu.make_async_remote_copy(
            chunk, chunk, send_b, sem_b, device_id=(1, me), device_id_type=MESH
        ).start()

    @pl.when(leaf == 1)
    def _():
        pltpu.make_async_remote_copy(
            chunk, chunk, send_b, sem_b, device_id=(0, me), device_id_type=MESH
        ).wait_recv()

    pltpu.make_async_copy(chunk, out_ref.at[me], recv_g.at[me]).start()

    def send(j, carry):
        dst = lax.rem(me + j, n_front)
        pltpu.make_async_remote_copy(
            chunk, out_ref.at[me], send_g.at[j], recv_g.at[me], device_id=(leaf, dst), device_id_type=MESH
        ).start()
        return carry

    lax.fori_loop(1, n_front, send, 0)

    pltpu.make_async_copy(chunk, out_ref.at[me], recv_g.at[me]).wait()

    def receive(j, carry):
        src = lax.rem(me + j, n_front)
        pltpu.make_async_remote_copy(
            chunk, out_ref.at[src], send_g.at[j], recv_g.at[src], device_id=(leaf, src), device_id_type=MESH
        ).wait_recv()
        return carry

    lax.fori_loop(1, n_front, receive, 0)

    def sent(j, carry):
        dst = lax.rem(me + j, n_front)
        pltpu.make_async_remote_copy(
            chunk, out_ref.at[me], send_g.at[j], recv_g.at[me], device_id=(leaf, dst), device_id_type=MESH
        ).wait_send()
        return carry

    lax.fori_loop(1, n_front, sent, 0)

    @pl.when(leaf == 0)
    def _():
        pltpu.make_async_remote_copy(
            chunk, chunk, send_b, sem_b, device_id=(1, me), device_id_type=MESH
        ).wait_send()

    @pl.when(leaf == 0)
    def _():
        pltpu.make_async_copy(top_ref, cols_ref, sem_t).wait()
        pltpu.make_async_remote_copy(
            top_ref, cols_ref, send_t, sem_t, device_id=(1, me), device_id_type=MESH
        ).wait_send()

    @pl.when(leaf == 1)
    def _():
        pltpu.make_async_remote_copy(
            top_ref, cols_ref, send_t, sem_t, device_id=(0, me), device_id_type=MESH
        ).wait_recv()

    @pl.when((leaf == 0) & (me < n_src))
    def _():
        for k in range(per_src):
            src = top_ref.at[pl.ds(k * rows, rows)]
            dst = me * per_src + k
            if k == 0:
                @pl.when(me != 0)
                def _():
                    pltpu.make_async_remote_copy(
                        src, chunk, send_a.at[k], sem_a, device_id=(0, dst), device_id_type=MESH
                    ).wait_send()
            else:
                pltpu.make_async_remote_copy(
                    src, chunk, send_a.at[k], sem_a, device_id=(0, dst), device_id_type=MESH
                ).wait_send()


def broadcast_pivot(top, n_front):
    cols = top.shape[1]
    n_src = S // cols
    per_src = n_front // n_src
    rows = S // per_src
    gathered, own_cols = pl.pallas_call(
        functools.partial(pivot_kernel, n_front, n_src),
        out_shape=(jax.ShapeDtypeStruct((n_front, rows, cols), jnp.float32), jax.ShapeDtypeStruct(top.shape, jnp.float32)),
        in_specs=[pl.BlockSpec(memory_space=pltpu.VMEM)],
        out_specs=(pl.BlockSpec(memory_space=pltpu.VMEM), pl.BlockSpec(memory_space=pltpu.VMEM)),
        scratch_shapes=[
            pltpu.VMEM((rows, cols), jnp.float32),
            pltpu.SemaphoreType.DMA,
            pltpu.SemaphoreType.DMA,
            pltpu.SemaphoreType.DMA((per_src,)),
            pltpu.SemaphoreType.DMA,
            pltpu.SemaphoreType.DMA((n_front,)),
            pltpu.SemaphoreType.DMA((n_front,)),
            pltpu.SemaphoreType.DMA,
            pltpu.SemaphoreType.DMA,
        ],
        compiler_params=pltpu.CompilerParams(has_side_effects=True),
    )(top)
    return gathered, own_cols


PANEL = 8


def _mm(a, b):
    return jnp.dot(a, b, precision=HIGHEST, preferred_element_type=jnp.float32)


def _mm_t(a, b):
    return lax.dot_general(a, b, (((1,), (1,)), ((), ())), precision=HIGHEST,
                           preferred_element_type=jnp.float32)


def chol_inv_kernel(a_ref, l_ref, linv_ref, w_ref, d_ref, e_ref, ut_ref, x_ref):
    n = w_ref.shape[0]
    b = d_ref.shape[0]
    nb = n // b
    lane = lax.broadcasted_iota(jnp.int32, (PANEL, b), 1)
    sub = lax.broadcasted_iota(jnp.int32, (PANEL, 1), 0)
    eye = (lax.broadcasted_iota(jnp.int32, (b, b), 0) == lax.broadcasted_iota(jnp.int32, (b, b), 1)).astype(jnp.float32)
    n_slots, rows, cols = a_ref.shape
    per_src = n_slots // (n // cols)
    for slot in range(n_slots):
        c, k = divmod(slot, per_src)
        w_ref[k * rows:(k + 1) * rows, c * cols:(c + 1) * cols] = a_ref[slot]
    l_ref[...] = jnp.zeros_like(l_ref)
    linv_ref[...] = jnp.zeros_like(linv_ref)

    def panel(p, carry):
        k = pl.multiple_of(p * PANEL, PANEL)
        r = d_ref[pl.ds(k, PANEL), :]
        e = e_ref[pl.ds(k, PANEL), :]
        for t in range(PANEL):
            c = k + t
            at_c = lane == c
            colv = jnp.sum(jnp.where(at_c, r, 0.0), axis=1, keepdims=True)
            piv = jnp.sum(jnp.where(at_c[t:t + 1], r[t:t + 1], 0.0), axis=1, keepdims=True)
            scale = 1.0 / jnp.sqrt(piv)
            urow = jnp.where(lane[t:t + 1] >= c, r[t:t + 1] * scale, 0.0)
            f = jnp.where(sub > t, colv * scale, 0.0)
            r = jnp.where(sub == t, urow, r - f * urow)
            xrow = e[t:t + 1] * scale
            e = jnp.where(sub == t, xrow, e - f * xrow)
        ut_ref[pl.ds(k, PANEL), :] = r
        x_ref[pl.ds(k, PANEL), :] = e
        rt = jnp.transpose(r)
        dd = d_ref[...]
        ee = e_ref[...]
        for t in range(PANEL):
            lcol = rt[:, t:t + 1]
            dd = dd - lcol * r[t:t + 1]
            ee = ee - lcol * e[t:t + 1]
        d_ref[...] = dd
        e_ref[...] = ee
        return carry

    for j in range(nb):
        jb = j * b
        d_ref[...] = w_ref[jb:jb + b, jb:jb + b]
        e_ref[...] = eye
        lax.fori_loop(0, b // PANEL, panel, 0)
        l_ref[jb:jb + b, jb:jb + b] = jnp.transpose(ut_ref[...])
        linv_ref[jb:jb + b, jb:jb + b] = x_ref[...]
        if j < nb - 1:
            lp = _mm_t(w_ref[jb + b:, jb:jb + b], x_ref[...])
            l_ref[jb + b:, jb:jb + b] = lp
            w_ref[jb + b:, jb + b:] = w_ref[jb + b:, jb + b:] - _mm_t(lp, lp)
    for j in range(nb):
        for i in range(j + 1, nb):
            acc = jnp.zeros((b, b), jnp.float32)
            for k in range(j, i):
                acc = acc + _mm(l_ref[i * b:(i + 1) * b, k * b:(k + 1) * b], linv_ref[k * b:(k + 1) * b, j * b:(j + 1) * b])
            linv_ref[i * b:(i + 1) * b, j * b:(j + 1) * b] = -_mm(linv_ref[i * b:(i + 1) * b, i * b:(i + 1) * b], acc)


def chol_inv(a, n, b=128):
    return pl.pallas_call(
        chol_inv_kernel,
        out_shape=(jax.ShapeDtypeStruct((n, n), jnp.float32), jax.ShapeDtypeStruct((n, n), jnp.float32)),
        in_specs=[pl.BlockSpec(memory_space=pltpu.VMEM)],
        out_specs=(pl.BlockSpec(memory_space=pltpu.VMEM), pl.BlockSpec(memory_space=pltpu.VMEM)),
        scratch_shapes=[
            pltpu.VMEM((n, n), jnp.float32),
            pltpu.VMEM((b, b), jnp.float32),
            pltpu.VMEM((b, b), jnp.float32),
            pltpu.VMEM((b, b), jnp.float32),
            pltpu.VMEM((b, b), jnp.float32),
        ],
    )(a)


def panel_product_kernel(subtract, use_top_ref, panel_ref, w_ref, base_ref, top_ref, out_ref):
    prod = jnp.transpose(lax.dot_general(w_ref[...], panel_ref[...], (((1,), (1,)), ((), ())),
                                         precision=HIGHEST, preferred_element_type=jnp.float32))
    result = base_ref[...] - prod if subtract else prod
    replace = (pl.program_id(0) == 0) & (use_top_ref[0] == 1)
    out_ref[...] = jnp.where(replace, top_ref[...], result)


def panel_product(use_top, panel, weights, base, top_rows, subtract):
    rows, depth = panel.shape
    cols = weights.shape[0]
    return pl.pallas_call(
        functools.partial(panel_product_kernel, subtract),
        out_shape=jax.ShapeDtypeStruct((rows, cols), jnp.float32),
        grid_spec=pltpu.PrefetchScalarGridSpec(
            num_scalar_prefetch=1,
            grid=(rows // S,),
            in_specs=[
                pl.BlockSpec((S, depth), lambda i, flag: (i, 0)),
                pl.BlockSpec((cols, depth), lambda i, flag: (0, 0)),
                pl.BlockSpec((S, cols), lambda i, flag: (i, 0)),
                pl.BlockSpec((S, cols), lambda i, flag: (0, 0)),
            ],
            out_specs=pl.BlockSpec((S, cols), lambda i, flag: (i, 0)),
        ),
    )(use_top, panel, weights, base, top_rows)


def per_device(front_block, child_update, child_map):
    rows, cols = front_block.shape
    n_leaf = lax.axis_size("leaf")
    n_front = lax.axis_size("front")
    leaf = lax.axis_index("leaf")
    front = lax.axis_index("front")
    half_blocks = rows // BLK

    blocks = child_update[0].reshape(-1, BLK, cols)
    cmap = child_map[0]
    own = gather_half(blocks, cmap, leaf, half_blocks)
    send = gather_half(blocks, cmap, 1 - leaf, half_blocks)
    recv = lax.ppermute(send, "leaf", [(0, 1), (1, 0)])
    first = jnp.where(leaf == 0, own, recv)
    second = jnp.where(leaf == 0, recv, own)
    assembled = front_block + first + second

    top = assembled[:S]
    panel_rows = top.T

    piece = rows // n_front
    per_block = BLK // piece
    pieces = []
    for part in range(per_block):
        pairs = []
        for lf in range(n_leaf):
            for k in range(n_front // per_block):
                src = lf * half_blocks + k
                dst = lf * n_front + per_block * k + part
                pairs.append((src, dst))
        pieces.append(lax.ppermute(panel_rows[part * piece:(part + 1) * piece], ("leaf", "front"), pairs))
    my_piece = pieces[0]
    for part in range(1, per_block):
        my_piece = jnp.where(front % per_block == part, pieces[part], my_piece)
    pivot, own_cols = broadcast_pivot(top, n_front)
    col_rows = own_cols.T
    my_piece, pivot = lax.optimization_barrier((my_piece, pivot))
    panel = lax.all_gather(my_piece, "front", tiled=True)
    factor, inverse = chol_inv(pivot, S)

    col_solved = lax.dot_general(col_rows, inverse, (((1,), (1,)), ((), ())), precision=HIGHEST)

    piv_cols = S // cols
    col_at = jnp.minimum(front, piv_cols - 1) * cols

    use_top = (leaf == 0).astype(jnp.int32).reshape(1)

    def pivot_columns():
        inv_rows = lax.dynamic_slice_in_dim(inverse, col_at, cols, 0)
        top_rows = lax.dynamic_slice_in_dim(factor, col_at, cols, 1)
        return panel_product(use_top, panel, inv_rows, assembled, top_rows, False)

    def other_columns():
        weights = jnp.dot(col_solved, inverse, precision=HIGHEST)
        return panel_product(use_top, panel, weights, assembled, col_solved.T, True)

    return lax.cond(front < piv_cols, pivot_columns, other_columns)


def solution(mesh):
    return jax.shard_map(
        per_device,
        mesh=mesh,
        in_specs=(P("leaf", "front"), P("leaf", None, "front"), P("leaf", None)),
        out_specs=P("leaf", "front"),
        check_vma=False,
    )
```

```python
import functools

import jax
import jax.numpy as jnp
from jax import lax
from jax.experimental import pallas as pl
from jax.experimental.pallas import tpu as pltpu
from jax.sharding import PartitionSpec as P

BLK = 128
S = 512
HIGHEST = lax.Precision.HIGHEST
MESH = pl.DeviceIdType.MESH


def gather_half(blocks, child_map, half, half_blocks):
    parent = half * half_blocks + jnp.arange(half_blocks, dtype=jnp.int32)
    hit = child_map[None, :] == parent[:, None]
    found = jnp.any(hit, axis=1)
    index = jnp.argmax(hit, axis=1)
    picked = jnp.take(blocks, index, axis=0)
    picked = jnp.where(found[:, None, None], picked, jnp.zeros_like(picked))
    return picked.reshape(half_blocks * BLK, blocks.shape[2])


def pivot_kernel(n_front, n_src, top_ref, out_ref, cols_ref, chunk, sem_a, sem_b, send_a, send_b, recv_g, send_g, sem_t, send_t):
    leaf = lax.axis_index("leaf")
    me = lax.axis_index("front")
    per_src = n_front // n_src
    rows = chunk.shape[0]

    @pl.when((leaf == 0) & (me < n_src))
    def _():
        for k in range(per_src):
            src = top_ref.at[pl.ds(k * rows, rows)]
            dst = me * per_src + k
            if k == 0:
                @pl.when(me == 0)
                def _():
                    pltpu.make_async_copy(src, chunk, sem_a).start()

                @pl.when(me != 0)
                def _():
                    pltpu.make_async_remote_copy(
                        src, chunk, send_a.at[k], sem_a, device_id=(0, dst), device_id_type=MESH
                    ).start()
            else:
                pltpu.make_async_remote_copy(
                    src, chunk, send_a.at[k], sem_a, device_id=(0, dst), device_id_type=MESH
                ).start()

    @pl.when((leaf == 0) & (me == 0))
    def _():
        pltpu.make_async_copy(top_ref.at[pl.ds(0, rows)], chunk, sem_a).wait()

    @pl.when((leaf == 0) & (me != 0))
    def _():
        pltpu.make_async_remote_copy(
            top_ref.at[pl.ds(0, rows)], chunk, send_a.at[0], sem_a, device_id=(0, me), device_id_type=MESH
        ).wait_recv()

    @pl.when(leaf == 0)
    def _():
        pltpu.make_async_copy(top_ref, cols_ref, sem_t).start()
        pltpu.make_async_remote_copy(
            top_ref, cols_ref, send_t, sem_t, device_id=(1, me), device_id_type=MESH
        ).start()

    @pl.when(leaf == 0)
    def _():
        pltpu.make_async_remote_copy(
            chunk, chunk, send_b, sem_b, device_id=(1, me), device_id_type=MESH
        ).start()

    @pl.when(leaf == 1)
    def _():
        pltpu.make_async_remote_copy(
            chunk, chunk, send_b, sem_b, device_id=(0, me), device_id_type=MESH
        ).wait_recv()

    pltpu.make_async_copy(chunk, out_ref.at[me], recv_g.at[me]).start()

    def send(j, carry):
        dst = lax.rem(me + j, n_front)
        pltpu.make_async_remote_copy(
            chunk, out_ref.at[me], send_g.at[j], recv_g.at[me], device_id=(leaf, dst), device_id_type=MESH
        ).start()
        return carry

    lax.fori_loop(1, n_front, send, 0)

    pltpu.make_async_copy(chunk, out_ref.at[me], recv_g.at[me]).wait()

    def receive(j, carry):
        src = lax.rem(me + j, n_front)
        pltpu.make_async_remote_copy(
            chunk, out_ref.at[src], send_g.at[j], recv_g.at[src], device_id=(leaf, src), device_id_type=MESH
        ).wait_recv()
        return carry

    lax.fori_loop(1, n_front, receive, 0)

    def sent(j, carry):
        dst = lax.rem(me + j, n_front)
        pltpu.make_async_remote_copy(
            chunk, out_ref.at[me], send_g.at[j], recv_g.at[me], device_id=(leaf, dst), device_id_type=MESH
        ).wait_send()
        return carry

    lax.fori_loop(1, n_front, sent, 0)

    @pl.when(leaf == 0)
    def _():
        pltpu.make_async_remote_copy(
            chunk, chunk, send_b, sem_b, device_id=(1, me), device_id_type=MESH
        ).wait_send()

    @pl.when(leaf == 0)
    def _():
        pltpu.make_async_copy(top_ref, cols_ref, sem_t).wait()
        pltpu.make_async_remote_copy(
            top_ref, cols_ref, send_t, sem_t, device_id=(1, me), device_id_type=MESH
        ).wait_send()

    @pl.when(leaf == 1)
    def _():
        pltpu.make_async_remote_copy(
            top_ref, cols_ref, send_t, sem_t, device_id=(0, me), device_id_type=MESH
        ).wait_recv()

    @pl.when((leaf == 0) & (me < n_src))
    def _():
        for k in range(per_src):
            src = top_ref.at[pl.ds(k * rows, rows)]
            dst = me * per_src + k
            if k == 0:
                @pl.when(me != 0)
                def _():
                    pltpu.make_async_remote_copy(
                        src, chunk, send_a.at[k], sem_a, device_id=(0, dst), device_id_type=MESH
                    ).wait_send()
            else:
                pltpu.make_async_remote_copy(
                    src, chunk, send_a.at[k], sem_a, device_id=(0, dst), device_id_type=MESH
                ).wait_send()


def broadcast_pivot(top, n_front):
    cols = top.shape[1]
    n_src = S // cols
    per_src = n_front // n_src
    rows = S // per_src
    gathered, own_cols = pl.pallas_call(
        functools.partial(pivot_kernel, n_front, n_src),
        out_shape=(jax.ShapeDtypeStruct((n_front, rows, cols), jnp.float32), jax.ShapeDtypeStruct(top.shape, jnp.float32)),
        in_specs=[pl.BlockSpec(memory_space=pltpu.VMEM)],
        out_specs=(pl.BlockSpec(memory_space=pltpu.VMEM), pl.BlockSpec(memory_space=pltpu.VMEM)),
        scratch_shapes=[
            pltpu.VMEM((rows, cols), jnp.float32),
            pltpu.SemaphoreType.DMA,
            pltpu.SemaphoreType.DMA,
            pltpu.SemaphoreType.DMA((per_src,)),
            pltpu.SemaphoreType.DMA,
            pltpu.SemaphoreType.DMA((n_front,)),
            pltpu.SemaphoreType.DMA((n_front,)),
            pltpu.SemaphoreType.DMA,
            pltpu.SemaphoreType.DMA,
        ],
        compiler_params=pltpu.CompilerParams(has_side_effects=True),
    )(top)
    return gathered, own_cols


PANEL = 8
TILE = 1024


def _mm(a, b):
    return jnp.dot(a, b, precision=HIGHEST, preferred_element_type=jnp.float32)


def _mm_t(a, b):
    return lax.dot_general(a, b, (((1,), (1,)), ((), ())), precision=HIGHEST,
                           preferred_element_type=jnp.float32)


def chol_inv_kernel(a_ref, l_ref, linv_ref, w_ref, d_ref, e_ref, ut_ref, x_ref):
    n = w_ref.shape[0]
    b = d_ref.shape[0]
    nb = n // b
    lane = lax.broadcasted_iota(jnp.int32, (PANEL, b), 1)
    sub = lax.broadcasted_iota(jnp.int32, (PANEL, 1), 0)
    eye = (lax.broadcasted_iota(jnp.int32, (b, b), 0) == lax.broadcasted_iota(jnp.int32, (b, b), 1)).astype(jnp.float32)
    n_slots, rows, cols = a_ref.shape
    per_src = n_slots // (n // cols)
    for slot in range(n_slots):
        c, k = divmod(slot, per_src)
        w_ref[k * rows:(k + 1) * rows, c * cols:(c + 1) * cols] = a_ref[slot]
    l_ref[...] = jnp.zeros_like(l_ref)
    linv_ref[...] = jnp.zeros_like(linv_ref)

    def panel(p, carry):
        k = pl.multiple_of(p * PANEL, PANEL)
        r = d_ref[pl.ds(k, PANEL), :]
        e = e_ref[pl.ds(k, PANEL), :]
        for t in range(PANEL):
            c = k + t
            at_c = lane == c
            colv = jnp.sum(jnp.where(at_c, r, 0.0), axis=1, keepdims=True)
            piv = jnp.sum(jnp.where(at_c[t:t + 1], r[t:t + 1], 0.0), axis=1, keepdims=True)
            scale = 1.0 / jnp.sqrt(piv)
            urow = jnp.where(lane[t:t + 1] >= c, r[t:t + 1] * scale, 0.0)
            f = jnp.where(sub > t, colv * scale, 0.0)
            r = jnp.where(sub == t, urow, r - f * urow)
            xrow = e[t:t + 1] * scale
            e = jnp.where(sub == t, xrow, e - f * xrow)
        ut_ref[pl.ds(k, PANEL), :] = r
        x_ref[pl.ds(k, PANEL), :] = e
        rt = jnp.transpose(r)
        dd = d_ref[...]
        ee = e_ref[...]
        for t in range(PANEL):
            lcol = rt[:, t:t + 1]
            dd = dd - lcol * r[t:t + 1]
            ee = ee - lcol * e[t:t + 1]
        d_ref[...] = dd
        e_ref[...] = ee
        return carry

    for j in range(nb):
        jb = j * b
        d_ref[...] = w_ref[jb:jb + b, jb:jb + b]
        e_ref[...] = eye
        lax.fori_loop(0, b // PANEL, panel, 0)
        l_ref[jb:jb + b, jb:jb + b] = jnp.transpose(ut_ref[...])
        linv_ref[jb:jb + b, jb:jb + b] = x_ref[...]
        if j < nb - 1:
            lp = _mm_t(w_ref[jb + b:, jb:jb + b], x_ref[...])
            l_ref[jb + b:, jb:jb + b] = lp
            w_ref[jb + b:, jb + b:] = w_ref[jb + b:, jb + b:] - _mm_t(lp, lp)
    for j in range(nb):
        for i in range(j + 1, nb):
            acc = jnp.zeros((b, b), jnp.float32)
            for k in range(j, i):
                acc = acc + _mm(l_ref[i * b:(i + 1) * b, k * b:(k + 1) * b], linv_ref[k * b:(k + 1) * b, j * b:(j + 1) * b])
            linv_ref[i * b:(i + 1) * b, j * b:(j + 1) * b] = -_mm(linv_ref[i * b:(i + 1) * b, i * b:(i + 1) * b], acc)


def chol_inv(a, n, b=128):
    return pl.pallas_call(
        chol_inv_kernel,
        out_shape=(jax.ShapeDtypeStruct((n, n), jnp.float32), jax.ShapeDtypeStruct((n, n), jnp.float32)),
        in_specs=[pl.BlockSpec(memory_space=pltpu.VMEM)],
        out_specs=(pl.BlockSpec(memory_space=pltpu.VMEM), pl.BlockSpec(memory_space=pltpu.VMEM)),
        scratch_shapes=[
            pltpu.VMEM((n, n), jnp.float32),
            pltpu.VMEM((b, b), jnp.float32),
            pltpu.VMEM((b, b), jnp.float32),
            pltpu.VMEM((b, b), jnp.float32),
            pltpu.VMEM((b, b), jnp.float32),
        ],
    )(a)


def panel_product_kernel(subtract, use_top_ref, panel_ref, w_ref, base_ref, top_ref, out_ref):
    prod = jnp.transpose(lax.dot_general(w_ref[...], panel_ref[...], (((1,), (1,)), ((), ())),
                                         precision=HIGHEST, preferred_element_type=jnp.float32))
    result = base_ref[...] - prod if subtract else prod
    out_ref[...] = result

    @pl.when((pl.program_id(0) == 0) & (use_top_ref[0] == 1))
    def _():
        out_ref[0:S, :] = top_ref[...]


def panel_product(use_top, panel, weights, base, top_rows, subtract):
    rows, depth = panel.shape
    cols = weights.shape[0]
    return pl.pallas_call(
        functools.partial(panel_product_kernel, subtract),
        out_shape=jax.ShapeDtypeStruct((rows, cols), jnp.float32),
        grid_spec=pltpu.PrefetchScalarGridSpec(
            num_scalar_prefetch=1,
            grid=(rows // TILE,),
            in_specs=[
                pl.BlockSpec((TILE, depth), lambda i, flag: (i, 0)),
                pl.BlockSpec((cols, depth), lambda i, flag: (0, 0)),
                pl.BlockSpec((TILE, cols), lambda i, flag: (i, 0)),
                pl.BlockSpec((S, cols), lambda i, flag: (0, 0)),
            ],
            out_specs=pl.BlockSpec((TILE, cols), lambda i, flag: (i, 0)),
        ),
    )(use_top, panel, weights, base, top_rows)


def per_device(front_block, child_update, child_map):
    rows, cols = front_block.shape
    n_leaf = lax.axis_size("leaf")
    n_front = lax.axis_size("front")
    leaf = lax.axis_index("leaf")
    front = lax.axis_index("front")
    half_blocks = rows // BLK

    blocks = child_update[0].reshape(-1, BLK, cols)
    cmap = child_map[0]
    own = gather_half(blocks, cmap, leaf, half_blocks)
    send = gather_half(blocks, cmap, 1 - leaf, half_blocks)
    recv = lax.ppermute(send, "leaf", [(0, 1), (1, 0)])
    first = jnp.where(leaf == 0, own, recv)
    second = jnp.where(leaf == 0, recv, own)
    assembled = front_block + first + second

    top = assembled[:S]
    panel_rows = top.T

    piece = rows // n_front
    per_block = BLK // piece
    pieces = []
    for part in range(per_block):
        pairs = []
        for lf in range(n_leaf):
            for k in range(n_front // per_block):
                src = lf * half_blocks + k
                dst = lf * n_front + per_block * k + part
                pairs.append((src, dst))
        pieces.append(lax.ppermute(panel_rows[part * piece:(part + 1) * piece], ("leaf", "front"), pairs))
    my_piece = pieces[0]
    for part in range(1, per_block):
        my_piece = jnp.where(front % per_block == part, pieces[part], my_piece)
    pivot, own_cols = broadcast_pivot(top, n_front)
    col_rows = own_cols.T
    my_piece, pivot = lax.optimization_barrier((my_piece, pivot))
    panel = lax.all_gather(my_piece, "front", tiled=True)
    factor, inverse = chol_inv(pivot, S)

    col_solved = lax.dot_general(col_rows, inverse, (((1,), (1,)), ((), ())), precision=HIGHEST)

    piv_cols = S // cols
    col_at = jnp.minimum(front, piv_cols - 1) * cols

    use_top = (leaf == 0).astype(jnp.int32).reshape(1)

    def pivot_columns():
        inv_rows = lax.dynamic_slice_in_dim(inverse, col_at, cols, 0)
        top_rows = lax.dynamic_slice_in_dim(factor, col_at, cols, 1)
        return panel_product(use_top, panel, inv_rows, assembled, top_rows, False)

    def other_columns():
        weights = jnp.dot(col_solved, inverse, precision=HIGHEST)
        return panel_product(use_top, panel, weights, assembled, col_solved.T, True)

    return lax.cond(front < piv_cols, pivot_columns, other_columns)


def solution(mesh):
    return jax.shard_map(
        per_device,
        mesh=mesh,
        in_specs=(P("leaf", "front"), P("leaf", None, "front"), P("leaf", None)),
        out_specs=P("leaf", "front"),
        check_vma=False,
    )
```

```python
import functools

import jax
import jax.numpy as jnp
from jax import lax
from jax.experimental import pallas as pl
from jax.experimental.pallas import tpu as pltpu
from jax.sharding import PartitionSpec as P

BLK = 128
S = 512
HIGHEST = lax.Precision.HIGHEST
MESH = pl.DeviceIdType.MESH


def gather_half(blocks, child_map, half, half_blocks):
    parent = half * half_blocks + jnp.arange(half_blocks, dtype=jnp.int32)
    hit = child_map[None, :] == parent[:, None]
    found = jnp.any(hit, axis=1)
    index = jnp.argmax(hit, axis=1)
    picked = jnp.take(blocks, index, axis=0)
    picked = jnp.where(found[:, None, None], picked, jnp.zeros_like(picked))
    return picked.reshape(half_blocks * BLK, blocks.shape[2])


def pivot_kernel(n_front, n_src, top_ref, out_ref, cols_ref, chunk, sem_a, sem_b, send_a, send_b, recv_g, send_g, sem_t, send_t):
    leaf = lax.axis_index("leaf")
    me = lax.axis_index("front")
    per_src = n_front // n_src
    rows = chunk.shape[0]

    @pl.when((leaf == 0) & (me < n_src))
    def _():
        for k in range(per_src):
            src = top_ref.at[pl.ds(k * rows, rows)]
            dst = me * per_src + k
            if k == 0:
                @pl.when(me == 0)
                def _():
                    pltpu.make_async_copy(src, chunk, sem_a).start()

                @pl.when(me != 0)
                def _():
                    pltpu.make_async_remote_copy(
                        src, chunk, send_a.at[k], sem_a, device_id=(0, dst), device_id_type=MESH
                    ).start()
            else:
                pltpu.make_async_remote_copy(
                    src, chunk, send_a.at[k], sem_a, device_id=(0, dst), device_id_type=MESH
                ).start()

    @pl.when((leaf == 0) & (me == 0))
    def _():
        pltpu.make_async_copy(top_ref.at[pl.ds(0, rows)], chunk, sem_a).wait()

    @pl.when((leaf == 0) & (me != 0))
    def _():
        pltpu.make_async_remote_copy(
            top_ref.at[pl.ds(0, rows)], chunk, send_a.at[0], sem_a, device_id=(0, me), device_id_type=MESH
        ).wait_recv()

    @pl.when(leaf == 0)
    def _():
        pltpu.make_async_copy(top_ref, cols_ref, sem_t).start()
        pltpu.make_async_remote_copy(
            top_ref, cols_ref, send_t, sem_t, device_id=(1, me), device_id_type=MESH
        ).start()

    @pl.when(leaf == 0)
    def _():
        pltpu.make_async_remote_copy(
            chunk, chunk, send_b, sem_b, device_id=(1, me), device_id_type=MESH
        ).start()

    @pl.when(leaf == 1)
    def _():
        pltpu.make_async_remote_copy(
            chunk, chunk, send_b, sem_b, device_id=(0, me), device_id_type=MESH
        ).wait_recv()

    pltpu.make_async_copy(chunk, out_ref.at[me], recv_g.at[me]).start()

    def send(j, carry):
        dst = lax.rem(me + j, n_front)
        pltpu.make_async_remote_copy(
            chunk, out_ref.at[me], send_g.at[j], recv_g.at[me], device_id=(leaf, dst), device_id_type=MESH
        ).start()
        return carry

    lax.fori_loop(1, n_front, send, 0)

    pltpu.make_async_copy(chunk, out_ref.at[me], recv_g.at[me]).wait()

    def receive(j, carry):
        src = lax.rem(me + j, n_front)
        pltpu.make_async_remote_copy(
            chunk, out_ref.at[src], send_g.at[j], recv_g.at[src], device_id=(leaf, src), device_id_type=MESH
        ).wait_recv()
        return carry

    lax.fori_loop(1, n_front, receive, 0)

    def sent(j, carry):
        dst = lax.rem(me + j, n_front)
        pltpu.make_async_remote_copy(
            chunk, out_ref.at[me], send_g.at[j], recv_g.at[me], device_id=(leaf, dst), device_id_type=MESH
        ).wait_send()
        return carry

    lax.fori_loop(1, n_front, sent, 0)

    @pl.when(leaf == 0)
    def _():
        pltpu.make_async_remote_copy(
            chunk, chunk, send_b, sem_b, device_id=(1, me), device_id_type=MESH
        ).wait_send()

    @pl.when(leaf == 0)
    def _():
        pltpu.make_async_copy(top_ref, cols_ref, sem_t).wait()
        pltpu.make_async_remote_copy(
            top_ref, cols_ref, send_t, sem_t, device_id=(1, me), device_id_type=MESH
        ).wait_send()

    @pl.when(leaf == 1)
    def _():
        pltpu.make_async_remote_copy(
            top_ref, cols_ref, send_t, sem_t, device_id=(0, me), device_id_type=MESH
        ).wait_recv()

    @pl.when((leaf == 0) & (me < n_src))
    def _():
        for k in range(per_src):
            src = top_ref.at[pl.ds(k * rows, rows)]
            dst = me * per_src + k
            if k == 0:
                @pl.when(me != 0)
                def _():
                    pltpu.make_async_remote_copy(
                        src, chunk, send_a.at[k], sem_a, device_id=(0, dst), device_id_type=MESH
                    ).wait_send()
            else:
                pltpu.make_async_remote_copy(
                    src, chunk, send_a.at[k], sem_a, device_id=(0, dst), device_id_type=MESH
                ).wait_send()


def broadcast_pivot(top, n_front):
    cols = top.shape[1]
    n_src = S // cols
    per_src = n_front // n_src
    rows = S // per_src
    gathered, own_cols = pl.pallas_call(
        functools.partial(pivot_kernel, n_front, n_src),
        out_shape=(jax.ShapeDtypeStruct((n_front, rows, cols), jnp.float32), jax.ShapeDtypeStruct(top.shape, jnp.float32)),
        in_specs=[pl.BlockSpec(memory_space=pltpu.VMEM)],
        out_specs=(pl.BlockSpec(memory_space=pltpu.VMEM), pl.BlockSpec(memory_space=pltpu.VMEM)),
        scratch_shapes=[
            pltpu.VMEM((rows, cols), jnp.float32),
            pltpu.SemaphoreType.DMA,
            pltpu.SemaphoreType.DMA,
            pltpu.SemaphoreType.DMA((per_src,)),
            pltpu.SemaphoreType.DMA,
            pltpu.SemaphoreType.DMA((n_front,)),
            pltpu.SemaphoreType.DMA((n_front,)),
            pltpu.SemaphoreType.DMA,
            pltpu.SemaphoreType.DMA,
        ],
        compiler_params=pltpu.CompilerParams(has_side_effects=True),
    )(top)
    return gathered, own_cols


PANEL = 8
TILE = 1024


def _mm(a, b):
    return jnp.dot(a, b, precision=HIGHEST, preferred_element_type=jnp.float32)


def _mm_t(a, b):
    return lax.dot_general(a, b, (((1,), (1,)), ((), ())), precision=HIGHEST,
                           preferred_element_type=jnp.float32)


def chol_inv_kernel(a_ref, c_ref, l_ref, linv_ref, st_ref, wt_ref, w_ref, d_ref, e_ref, ut_ref, x_ref):
    n = w_ref.shape[0]
    b = d_ref.shape[0]
    nb = n // b
    lane = lax.broadcasted_iota(jnp.int32, (PANEL, b), 1)
    sub = lax.broadcasted_iota(jnp.int32, (PANEL, 1), 0)
    eye = (lax.broadcasted_iota(jnp.int32, (b, b), 0) == lax.broadcasted_iota(jnp.int32, (b, b), 1)).astype(jnp.float32)
    n_slots, rows, cols = a_ref.shape
    per_src = n_slots // (n // cols)
    for slot in range(n_slots):
        c, k = divmod(slot, per_src)
        w_ref[k * rows:(k + 1) * rows, c * cols:(c + 1) * cols] = a_ref[slot]
    l_ref[...] = jnp.zeros_like(l_ref)
    linv_ref[...] = jnp.zeros_like(linv_ref)

    def panel(p, carry):
        k = pl.multiple_of(p * PANEL, PANEL)
        r = d_ref[pl.ds(k, PANEL), :]
        e = e_ref[pl.ds(k, PANEL), :]
        for t in range(PANEL):
            c = k + t
            at_c = lane == c
            colv = jnp.sum(jnp.where(at_c, r, 0.0), axis=1, keepdims=True)
            piv = jnp.sum(jnp.where(at_c[t:t + 1], r[t:t + 1], 0.0), axis=1, keepdims=True)
            scale = 1.0 / jnp.sqrt(piv)
            urow = jnp.where(lane[t:t + 1] >= c, r[t:t + 1] * scale, 0.0)
            f = jnp.where(sub > t, colv * scale, 0.0)
            r = jnp.where(sub == t, urow, r - f * urow)
            xrow = e[t:t + 1] * scale
            e = jnp.where(sub == t, xrow, e - f * xrow)
        ut_ref[pl.ds(k, PANEL), :] = r
        x_ref[pl.ds(k, PANEL), :] = e
        rt = jnp.transpose(r)
        dd = d_ref[...]
        ee = e_ref[...]
        for t in range(PANEL):
            lcol = rt[:, t:t + 1]
            dd = dd - lcol * r[t:t + 1]
            ee = ee - lcol * e[t:t + 1]
        d_ref[...] = dd
        e_ref[...] = ee
        return carry

    for j in range(nb):
        jb = j * b
        d_ref[...] = w_ref[jb:jb + b, jb:jb + b]
        e_ref[...] = eye
        lax.fori_loop(0, b // PANEL, panel, 0)
        l_ref[jb:jb + b, jb:jb + b] = jnp.transpose(ut_ref[...])
        linv_ref[jb:jb + b, jb:jb + b] = x_ref[...]
        if j < nb - 1:
            lp = _mm_t(w_ref[jb + b:, jb:jb + b], x_ref[...])
            l_ref[jb + b:, jb:jb + b] = lp
            w_ref[jb + b:, jb + b:] = w_ref[jb + b:, jb + b:] - _mm_t(lp, lp)
    for j in range(nb):
        for i in range(j + 1, nb):
            acc = jnp.zeros((b, b), jnp.float32)
            for k in range(j, i):
                acc = acc + _mm(l_ref[i * b:(i + 1) * b, k * b:(k + 1) * b], linv_ref[k * b:(k + 1) * b, j * b:(j + 1) * b])
            linv_ref[i * b:(i + 1) * b, j * b:(j + 1) * b] = -_mm(linv_ref[i * b:(i + 1) * b, i * b:(i + 1) * b], acc)
    solved_t = _mm(linv_ref[...], c_ref[...])
    st_ref[...] = solved_t
    wt_ref[...] = lax.dot_general(solved_t, linv_ref[...], (((0,), (0,)), ((), ())), precision=HIGHEST,
                                  preferred_element_type=jnp.float32)


def chol_inv(a, c, n, b=128):
    m = c.shape[1]
    return pl.pallas_call(
        chol_inv_kernel,
        out_shape=(jax.ShapeDtypeStruct((n, n), jnp.float32), jax.ShapeDtypeStruct((n, n), jnp.float32),
                   jax.ShapeDtypeStruct((n, m), jnp.float32), jax.ShapeDtypeStruct((m, n), jnp.float32)),
        in_specs=[pl.BlockSpec(memory_space=pltpu.VMEM)] * 2,
        out_specs=tuple(pl.BlockSpec(memory_space=pltpu.VMEM) for _ in range(4)),
        scratch_shapes=[
            pltpu.VMEM((n, n), jnp.float32),
            pltpu.VMEM((b, b), jnp.float32),
            pltpu.VMEM((b, b), jnp.float32),
            pltpu.VMEM((b, b), jnp.float32),
            pltpu.VMEM((b, b), jnp.float32),
        ],
    )(a, c)


def panel_product_kernel(subtract, use_top_ref, panel_ref, w_ref, base_ref, top_ref, out_ref):
    prod = jnp.transpose(lax.dot_general(w_ref[...], panel_ref[...], (((1,), (1,)), ((), ())),
                                         precision=HIGHEST, preferred_element_type=jnp.float32))
    result = base_ref[...] - prod if subtract else prod
    out_ref[...] = result

    @pl.when((pl.program_id(0) == 0) & (use_top_ref[0] == 1))
    def _():
        out_ref[0:S, :] = top_ref[...]


def panel_product(use_top, panel, weights, base, top_rows, subtract):
    rows, depth = panel.shape
    cols = weights.shape[0]
    return pl.pallas_call(
        functools.partial(panel_product_kernel, subtract),
        out_shape=jax.ShapeDtypeStruct((rows, cols), jnp.float32),
        grid_spec=pltpu.PrefetchScalarGridSpec(
            num_scalar_prefetch=1,
            grid=(rows // TILE,),
            in_specs=[
                pl.BlockSpec((TILE, depth), lambda i, flag: (i, 0)),
                pl.BlockSpec((cols, depth), lambda i, flag: (0, 0)),
                pl.BlockSpec((TILE, cols), lambda i, flag: (i, 0)),
                pl.BlockSpec((S, cols), lambda i, flag: (0, 0)),
            ],
            out_specs=pl.BlockSpec((TILE, cols), lambda i, flag: (i, 0)),
        ),
    )(use_top, panel, weights, base, top_rows)


def per_device(front_block, child_update, child_map):
    rows, cols = front_block.shape
    n_leaf = lax.axis_size("leaf")
    n_front = lax.axis_size("front")
    leaf = lax.axis_index("leaf")
    front = lax.axis_index("front")
    half_blocks = rows // BLK

    blocks = child_update[0].reshape(-1, BLK, cols)
    cmap = child_map[0]
    own = gather_half(blocks, cmap, leaf, half_blocks)
    send = gather_half(blocks, cmap, 1 - leaf, half_blocks)
    recv = lax.ppermute(send, "leaf", [(0, 1), (1, 0)])
    first = jnp.where(leaf == 0, own, recv)
    second = jnp.where(leaf == 0, recv, own)
    assembled = front_block + first + second

    top = assembled[:S]
    panel_rows = top.T

    piece = rows // n_front
    per_block = BLK // piece
    pieces = []
    for part in range(per_block):
        pairs = []
        for lf in range(n_leaf):
            for k in range(n_front // per_block):
                src = lf * half_blocks + k
                dst = lf * n_front + per_block * k + part
                pairs.append((src, dst))
        pieces.append(lax.ppermute(panel_rows[part * piece:(part + 1) * piece], ("leaf", "front"), pairs))
    my_piece = pieces[0]
    for part in range(1, per_block):
        my_piece = jnp.where(front % per_block == part, pieces[part], my_piece)
    pivot, own_cols = broadcast_pivot(top, n_front)
    my_piece, pivot = lax.optimization_barrier((my_piece, pivot))
    panel = lax.all_gather(my_piece, "front", tiled=True)
    factor, inverse, solved_t, weights = chol_inv(pivot, own_cols, S)


    piv_cols = S // cols
    col_at = jnp.minimum(front, piv_cols - 1) * cols

    use_top = (leaf == 0).astype(jnp.int32).reshape(1)

    def pivot_columns():
        inv_rows = lax.dynamic_slice_in_dim(inverse, col_at, cols, 0)
        top_rows = lax.dynamic_slice_in_dim(factor, col_at, cols, 1)
        return panel_product(use_top, panel, inv_rows, assembled, top_rows, False)

    def other_columns():
        return panel_product(use_top, panel, weights, assembled, solved_t, True)

    return lax.cond(front < piv_cols, pivot_columns, other_columns)


def solution(mesh):
    return jax.shard_map(
        per_device,
        mesh=mesh,
        in_specs=(P("leaf", "front"), P("leaf", None, "front"), P("leaf", None)),
        out_specs=P("leaf", "front"),
        check_vma=False,
    )
```

```python
import functools

import jax
import jax.numpy as jnp
from jax import lax
from jax.experimental import pallas as pl
from jax.experimental.pallas import tpu as pltpu
from jax.sharding import PartitionSpec as P

BLK = 128
S = 512
HIGHEST = lax.Precision.HIGHEST
MESH = pl.DeviceIdType.MESH


def gather_half(blocks, child_map, half, half_blocks):
    parent = half * half_blocks + jnp.arange(half_blocks, dtype=jnp.int32)
    hit = child_map[None, :] == parent[:, None]
    found = jnp.any(hit, axis=1)
    index = jnp.argmax(hit, axis=1)
    picked = jnp.take(blocks, index, axis=0)
    picked = jnp.where(found[:, None, None], picked, jnp.zeros_like(picked))
    return picked.reshape(half_blocks * BLK, blocks.shape[2])


def pivot_kernel(n_front, n_src, top_ref, out_ref, cols_ref, chunk, sem_a, sem_b, send_a, send_b, recv_g, send_g, sem_t, send_t):
    leaf = lax.axis_index("leaf")
    me = lax.axis_index("front")
    per_src = n_front // n_src
    rows = chunk.shape[0]

    @pl.when((leaf == 0) & (me < n_src))
    def _():
        for k in range(per_src):
            src = top_ref.at[pl.ds(k * rows, rows)]
            dst = me * per_src + k
            if k == 0:
                @pl.when(me == 0)
                def _():
                    pltpu.make_async_copy(src, chunk, sem_a).start()

                @pl.when(me != 0)
                def _():
                    pltpu.make_async_remote_copy(
                        src, chunk, send_a.at[k], sem_a, device_id=(0, dst), device_id_type=MESH
                    ).start()
            else:
                pltpu.make_async_remote_copy(
                    src, chunk, send_a.at[k], sem_a, device_id=(0, dst), device_id_type=MESH
                ).start()

    @pl.when((leaf == 0) & (me == 0))
    def _():
        pltpu.make_async_copy(top_ref.at[pl.ds(0, rows)], chunk, sem_a).wait()

    @pl.when((leaf == 0) & (me != 0))
    def _():
        pltpu.make_async_remote_copy(
            top_ref.at[pl.ds(0, rows)], chunk, send_a.at[0], sem_a, device_id=(0, me), device_id_type=MESH
        ).wait_recv()

    @pl.when(leaf == 0)
    def _():
        pltpu.make_async_copy(top_ref, cols_ref, sem_t).start()
        pltpu.make_async_remote_copy(
            top_ref, cols_ref, send_t, sem_t, device_id=(1, me), device_id_type=MESH
        ).start()

    @pl.when(leaf == 0)
    def _():
        pltpu.make_async_remote_copy(
            chunk, chunk, send_b, sem_b, device_id=(1, me), device_id_type=MESH
        ).start()

    @pl.when(leaf == 1)
    def _():
        pltpu.make_async_remote_copy(
            chunk, chunk, send_b, sem_b, device_id=(0, me), device_id_type=MESH
        ).wait_recv()

    pltpu.make_async_copy(chunk, out_ref.at[me], recv_g.at[me]).start()

    def send(j, carry):
        dst = lax.rem(me + j, n_front)
        pltpu.make_async_remote_copy(
            chunk, out_ref.at[me], send_g.at[j], recv_g.at[me], device_id=(leaf, dst), device_id_type=MESH
        ).start()
        return carry

    lax.fori_loop(1, n_front, send, 0)

    pltpu.make_async_copy(chunk, out_ref.at[me], recv_g.at[me]).wait()

    def receive(j, carry):
        src = lax.rem(me + j, n_front)
        pltpu.make_async_remote_copy(
            chunk, out_ref.at[src], send_g.at[j], recv_g.at[src], device_id=(leaf, src), device_id_type=MESH
        ).wait_recv()
        return carry

    lax.fori_loop(1, n_front, receive, 0)

    def sent(j, carry):
        dst = lax.rem(me + j, n_front)
        pltpu.make_async_remote_copy(
            chunk, out_ref.at[me], send_g.at[j], recv_g.at[me], device_id=(leaf, dst), device_id_type=MESH
        ).wait_send()
        return carry

    lax.fori_loop(1, n_front, sent, 0)

    @pl.when(leaf == 0)
    def _():
        pltpu.make_async_remote_copy(
            chunk, chunk, send_b, sem_b, device_id=(1, me), device_id_type=MESH
        ).wait_send()

    @pl.when(leaf == 0)
    def _():
        pltpu.make_async_copy(top_ref, cols_ref, sem_t).wait()
        pltpu.make_async_remote_copy(
            top_ref, cols_ref, send_t, sem_t, device_id=(1, me), device_id_type=MESH
        ).wait_send()

    @pl.when(leaf == 1)
    def _():
        pltpu.make_async_remote_copy(
            top_ref, cols_ref, send_t, sem_t, device_id=(0, me), device_id_type=MESH
        ).wait_recv()

    @pl.when((leaf == 0) & (me < n_src))
    def _():
        for k in range(per_src):
            src = top_ref.at[pl.ds(k * rows, rows)]
            dst = me * per_src + k
            if k == 0:
                @pl.when(me != 0)
                def _():
                    pltpu.make_async_remote_copy(
                        src, chunk, send_a.at[k], sem_a, device_id=(0, dst), device_id_type=MESH
                    ).wait_send()
            else:
                pltpu.make_async_remote_copy(
                    src, chunk, send_a.at[k], sem_a, device_id=(0, dst), device_id_type=MESH
                ).wait_send()


def broadcast_pivot(top, n_front):
    cols = top.shape[1]
    n_src = S // cols
    per_src = n_front // n_src
    rows = S // per_src
    gathered, own_cols = pl.pallas_call(
        functools.partial(pivot_kernel, n_front, n_src),
        out_shape=(jax.ShapeDtypeStruct((n_front, rows, cols), jnp.float32), jax.ShapeDtypeStruct(top.shape, jnp.float32)),
        in_specs=[pl.BlockSpec(memory_space=pltpu.VMEM)],
        out_specs=(pl.BlockSpec(memory_space=pltpu.VMEM), pl.BlockSpec(memory_space=pltpu.VMEM)),
        scratch_shapes=[
            pltpu.VMEM((rows, cols), jnp.float32),
            pltpu.SemaphoreType.DMA,
            pltpu.SemaphoreType.DMA,
            pltpu.SemaphoreType.DMA((per_src,)),
            pltpu.SemaphoreType.DMA,
            pltpu.SemaphoreType.DMA((n_front,)),
            pltpu.SemaphoreType.DMA((n_front,)),
            pltpu.SemaphoreType.DMA,
            pltpu.SemaphoreType.DMA,
        ],
        compiler_params=pltpu.CompilerParams(has_side_effects=True),
    )(top)
    return gathered, own_cols


PANEL = 8
TILE = 1024


def _mm(a, b):
    return jnp.dot(a, b, precision=HIGHEST, preferred_element_type=jnp.float32)


def _mm_t(a, b):
    return lax.dot_general(a, b, (((1,), (1,)), ((), ())), precision=HIGHEST,
                           preferred_element_type=jnp.float32)


def chol_inv_kernel(a_ref, l_ref, linv_ref, w_ref, d_ref, e_ref, ut_ref, x_ref):
    n = w_ref.shape[0]
    b = d_ref.shape[0]
    nb = n // b
    lane = lax.broadcasted_iota(jnp.int32, (PANEL, b), 1)
    sub = lax.broadcasted_iota(jnp.int32, (PANEL, 1), 0)
    eye = (lax.broadcasted_iota(jnp.int32, (b, b), 0) == lax.broadcasted_iota(jnp.int32, (b, b), 1)).astype(jnp.float32)
    n_slots, rows, cols = a_ref.shape
    per_src = n_slots // (n // cols)
    for slot in range(n_slots):
        c, k = divmod(slot, per_src)
        w_ref[k * rows:(k + 1) * rows, c * cols:(c + 1) * cols] = a_ref[slot]
    l_ref[...] = jnp.zeros_like(l_ref)
    linv_ref[...] = jnp.zeros_like(linv_ref)

    def panel(p, carry):
        k = pl.multiple_of(p * PANEL, PANEL)
        r = d_ref[pl.ds(k, PANEL), :]
        e = e_ref[pl.ds(k, PANEL), :]
        for t in range(PANEL):
            c = k + t
            at_c = lane == c
            colv = jnp.sum(jnp.where(at_c, r, 0.0), axis=1, keepdims=True)
            piv = jnp.sum(jnp.where(at_c[t:t + 1], r[t:t + 1], 0.0), axis=1, keepdims=True)
            scale = 1.0 / jnp.sqrt(piv)
            urow = jnp.where(lane[t:t + 1] >= c, r[t:t + 1] * scale, 0.0)
            f = jnp.where(sub > t, colv * scale, 0.0)
            r = jnp.where(sub == t, urow, r - f * urow)
            xrow = e[t:t + 1] * scale
            e = jnp.where(sub == t, xrow, e - f * xrow)
        ut_ref[pl.ds(k, PANEL), :] = r
        x_ref[pl.ds(k, PANEL), :] = e
        rt = jnp.transpose(r)
        dd = d_ref[...]
        ee = e_ref[...]
        for t in range(PANEL):
            lcol = rt[:, t:t + 1]
            dd = dd - lcol * r[t:t + 1]
            ee = ee - lcol * e[t:t + 1]
        d_ref[...] = dd
        e_ref[...] = ee
        return carry

    for j in range(nb):
        jb = j * b
        d_ref[...] = w_ref[jb:jb + b, jb:jb + b]
        e_ref[...] = eye
        lax.fori_loop(0, b // PANEL, panel, 0)
        l_ref[jb:jb + b, jb:jb + b] = jnp.transpose(ut_ref[...])
        linv_ref[jb:jb + b, jb:jb + b] = x_ref[...]
        if j < nb - 1:
            lp = _mm_t(w_ref[jb + b:, jb:jb + b], x_ref[...])
            l_ref[jb + b:, jb:jb + b] = lp
            w_ref[jb + b:, jb + b:] = w_ref[jb + b:, jb + b:] - _mm_t(lp, lp)
    for j in range(nb):
        for i in range(j + 1, nb):
            acc = jnp.zeros((b, b), jnp.float32)
            for k in range(j, i):
                acc = acc + _mm(l_ref[i * b:(i + 1) * b, k * b:(k + 1) * b], linv_ref[k * b:(k + 1) * b, j * b:(j + 1) * b])
            linv_ref[i * b:(i + 1) * b, j * b:(j + 1) * b] = -_mm(linv_ref[i * b:(i + 1) * b, i * b:(i + 1) * b], acc)


def chol_inv(a, n, b=128):
    return pl.pallas_call(
        chol_inv_kernel,
        out_shape=(jax.ShapeDtypeStruct((n, n), jnp.float32), jax.ShapeDtypeStruct((n, n), jnp.float32)),
        in_specs=[pl.BlockSpec(memory_space=pltpu.VMEM)],
        out_specs=(pl.BlockSpec(memory_space=pltpu.VMEM), pl.BlockSpec(memory_space=pltpu.VMEM)),
        scratch_shapes=[
            pltpu.VMEM((n, n), jnp.float32),
            pltpu.VMEM((b, b), jnp.float32),
            pltpu.VMEM((b, b), jnp.float32),
            pltpu.VMEM((b, b), jnp.float32),
            pltpu.VMEM((b, b), jnp.float32),
        ],
    )(a)


def panel_product_kernel(subtract, use_top_ref, panel_ref, w_ref, base_ref, top_ref, out_ref):
    prod = jnp.transpose(lax.dot_general(w_ref[...], panel_ref[...], (((1,), (1,)), ((), ())),
                                         precision=HIGHEST, preferred_element_type=jnp.float32))
    result = base_ref[...] - prod if subtract else prod
    out_ref[...] = result

    @pl.when((pl.program_id(0) == 0) & (use_top_ref[0] == 1))
    def _():
        out_ref[0:S, :] = top_ref[...]


def panel_product(use_top, panel, weights, base, top_rows, subtract):
    rows, depth = panel.shape
    cols = weights.shape[0]
    return pl.pallas_call(
        functools.partial(panel_product_kernel, subtract),
        out_shape=jax.ShapeDtypeStruct((rows, cols), jnp.float32),
        grid_spec=pltpu.PrefetchScalarGridSpec(
            num_scalar_prefetch=1,
            grid=(rows // TILE,),
            in_specs=[
                pl.BlockSpec((TILE, depth), lambda i, flag: (i, 0)),
                pl.BlockSpec((cols, depth), lambda i, flag: (0, 0)),
                pl.BlockSpec((TILE, cols), lambda i, flag: (i, 0)),
                pl.BlockSpec((S, cols), lambda i, flag: (0, 0)),
            ],
            out_specs=pl.BlockSpec((TILE, cols), lambda i, flag: (i, 0)),
        ),
    )(use_top, panel, weights, base, top_rows)


def per_device(front_block, child_update, child_map):
    rows, cols = front_block.shape
    n_leaf = lax.axis_size("leaf")
    n_front = lax.axis_size("front")
    leaf = lax.axis_index("leaf")
    front = lax.axis_index("front")
    half_blocks = rows // BLK

    blocks = child_update[0].reshape(-1, BLK, cols)
    cmap = child_map[0]
    own = gather_half(blocks, cmap, leaf, half_blocks)
    send = gather_half(blocks, cmap, 1 - leaf, half_blocks)
    recv = lax.ppermute(send, "leaf", [(0, 1), (1, 0)])
    first = jnp.where(leaf == 0, own, recv)
    second = jnp.where(leaf == 0, recv, own)
    assembled = front_block + first + second

    top = assembled[:S]
    panel_rows = top.T

    piece = rows // n_front
    per_block = BLK // piece
    pieces = []
    for part in range(per_block):
        pairs = []
        for lf in range(n_leaf):
            for k in range(n_front // per_block):
                src = lf * half_blocks + k
                dst = lf * n_front + per_block * k + part
                pairs.append((src, dst))
        pieces.append(lax.ppermute(panel_rows[part * piece:(part + 1) * piece], ("leaf", "front"), pairs))
    my_piece = pieces[0]
    for part in range(1, per_block):
        my_piece = jnp.where(front % per_block == part, pieces[part], my_piece)
    my_piece, top = lax.optimization_barrier((my_piece, top))
    pivot, own_cols = broadcast_pivot(top, n_front)
    col_rows = own_cols.T
    my_piece, pivot = lax.optimization_barrier((my_piece, pivot))
    panel = lax.all_gather(my_piece, "front", tiled=True)
    factor, inverse = chol_inv(pivot, S)

    col_solved = lax.dot_general(col_rows, inverse, (((1,), (1,)), ((), ())), precision=HIGHEST)

    piv_cols = S // cols
    col_at = jnp.minimum(front, piv_cols - 1) * cols

    use_top = (leaf == 0).astype(jnp.int32).reshape(1)

    def pivot_columns():
        inv_rows = lax.dynamic_slice_in_dim(inverse, col_at, cols, 0)
        top_rows = lax.dynamic_slice_in_dim(factor, col_at, cols, 1)
        return panel_product(use_top, panel, inv_rows, assembled, top_rows, False)

    def other_columns():
        weights = jnp.dot(col_solved, inverse, precision=HIGHEST)
        return panel_product(use_top, panel, weights, assembled, col_solved.T, True)

    return lax.cond(front < piv_cols, pivot_columns, other_columns)


def solution(mesh):
    return jax.shard_map(
        per_device,
        mesh=mesh,
        in_specs=(P("leaf", "front"), P("leaf", None, "front"), P("leaf", None)),
        out_specs=P("leaf", "front"),
        check_vma=False,
    )
```
